256 devices in a mesh: gx: 16 (over z_lo, x, core), gy: 4 (over y), tx: 4 (over z_hi).
Axes of the slice: x: 4, y: 4, z: 8 (z_hi: 4, z_lo: 2; z = z_hi * 2 + z_lo), core: 2. Of those that a mesh axis runs over, the one named last changes fastest.
Arguments:
- src_cell: int32 [8], P('tx'), may hold values from 0 to 524287
- basis: bfloat16 [16, 2, 3, 8, 128, 512], P('tx', None, None, None, 'gx', 'gy'), as said below
- images: bfloat16 [16, 2, 3, 8, 128, 512], P('tx', None, None, None, 'gx', 'gy'), as said below
- induction: bfloat16 [3, 8, 128, 512], P(None, 'tx', 'gx', 'gy'), may hold values from 0.25 to 4
Outputs:
- solution: float32 [8, 2, 3, 8, 128, 512], P('tx', None, None, None, 'gx', 'gy')
- residual: float32 [8, 2, 3, 8, 128, 512], P('tx', None, None, None, 'gx', 'gy')
The draws below stay inside these ranges and needn't reach their ends.
Inputs may be any that keep to these rules, and one draw needn't show every extreme that they name: `basis`: entries of order one. `images`: entries of order one.
All inputs are finite; a program needn't handle non-finite values.
Results may differ from the reference program's by a relative error of at most 0.0003.
Values may be sent and summed in bfloat16 or wider, within the bound.
No kernel may reach another device: no remote copies, remote signals or barrier semaphores. Data moves between devices by JAX's collectives and lax.ppermute only.
A program may use at most 64 MiB of HBM per device.

```python
import math
import jax
import jax.numpy as jnp
from jax import lax

NZ = 8
CYCLES = 2
ARNOLDI = 2
NX = 128
NY = 512
SOURCES = 8
VECS = 16


def shaped_modes():
    index = jnp.arange(VECS)
    p_wave = (index // 4).astype(jnp.float32)
    q_wave = (index % 4).astype(jnp.float32)
    x_pos = (jnp.arange(NX).astype(jnp.float32) + 0.5) / NX
    y_pos = (jnp.arange(NY).astype(jnp.float32) + 0.5) / NY
    z_pos = (jnp.arange(NZ).astype(jnp.float32) + 0.5) / NZ
    along_x = jnp.cos(math.pi * (p_wave[:, None] + 0.5) * x_pos[None, :])
    along_y = jnp.cos(math.pi * (q_wave[:, None] + 0.5) * y_pos[None, :])
    plane = along_x[:, :, None] * along_y[:, None, :]
    z_factor = 1.0 + 0.3 * jnp.cos(math.pi * z_pos)
    comp_factor = jnp.array([1.0, 0.7, 0.4], dtype=jnp.float32)
    part_factor = jnp.array([1.0, -0.5], dtype=jnp.float32)
    return plane[:, None, None, None, :, :] * part_factor[None, :, None, None, None, None] * comp_factor[None, None, :, None, None, None] * z_factor[None, None, None, :, None, None]


def rough_field(key):
    shape = (VECS, 2, 3, NZ, NX, NY)
    noise = jax.random.normal(key, shape, jnp.float32)
    return shaped_modes() * (1.0 + 0.5 * noise)


def draw_basis(key, part):
    return rough_field(jax.random.fold_in(key, 11)).astype(jnp.bfloat16)


def draw_images(key, part):
    return (2.0 * rough_field(jax.random.fold_in(key, 23))).astype(jnp.bfloat16)


def set_ends(entries, rng, least, high):
    extent = entries.shape
    index_at = [jax.random.randint(jax.random.fold_in(rng, axis), (), 0, extent[axis]) for axis in range(len(extent))]
    entries = entries.at[tuple(index_at)].set(least)
    longest = extent.index(max(extent))
    index_at[longest] = (index_at[longest] + 1) % extent[longest]
    return entries.at[tuple(index_at)].set(high)


def shard_levels(key, extent, pieces, least, largest):
    gain = 1.0
    for dim, blocks in pieces:
        heights = jax.random.uniform(jax.random.fold_in(jax.random.fold_in(key, 6), dim), (blocks,), jnp.float32, least / len(pieces), largest / len(pieces))
        gain = gain * jnp.repeat(jnp.exp(heights), extent[dim] // blocks).reshape((-1,) + (1,) * (len(extent) - 1 - dim))
    return gain


def setup_inputs(seed: int = 0) -> dict:
    splits = jax.random.split(jax.random.key(seed), 5)
    return {
        "src_cell": set_ends(jax.random.randint(splits[0], (SOURCES,), 0, NX * NY * NZ), jax.random.fold_in(splits[0], 1), 0, (NX * NY * NZ) - 1).astype(jnp.int32),
        "basis": draw_basis(jax.random.fold_in(splits[4], 71), 0),
        "images": draw_images(jax.random.fold_in(splits[4], 71), 0),
        "induction": jnp.clip(jnp.exp(math.log(4.0) - 2.7725887 * jax.random.uniform(splits[3], (3, NZ, NX, NY), jnp.float32) ** shard_levels(splits[3], (3, NZ, NX, NY), ((1, 4), (2, 16), (3, 4)), -0.2, 0.2)), 0.25, 4.0).astype(jnp.bfloat16),
    }


eps = 1e-06

def differ(field, axis, forward):
    axis = field.ndim + axis
    count = field.shape[axis]
    delta = lax.slice_in_dim(field, 1, count, axis=axis) - lax.slice_in_dim(field, 0, count - 1, axis=axis)
    zero = jnp.zeros_like(lax.slice_in_dim(field, 0, 1, axis=axis))
    if forward:
        return jnp.concatenate([delta, zero], axis=axis)
    return jnp.concatenate([zero, delta], axis=axis)

def curl_curl(padded):
    e_x = padded[..., 0, :, :, :]
    e_y = padded[..., 1, :, :, :]
    e_z = padded[..., 2, :, :, :]
    b_x = differ(e_z, -1, True) - differ(e_y, -3, True)
    b_y = differ(e_x, -3, True) - differ(e_z, -2, True)
    b_z = differ(e_y, -2, True) - differ(e_x, -1, True)
    c_x = differ(b_z, -1, False) - differ(b_y, -3, False)
    c_y = differ(b_x, -3, False) - differ(b_z, -2, False)
    c_z = differ(b_y, -2, False) - differ(b_x, -1, False)
    whole = jnp.stack([c_x, c_y, c_z], axis=-4)
    return whole[..., 1:-1, 1:-1, 1:-1]

def operator(padded, field, induct):
    curled = curl_curl(padded)
    real_part = curled[:, 0] - induct[None] * field[:, 1]
    imag_part = curled[:, 1] + induct[None] * field[:, 0]
    return jnp.stack([real_part, imag_part], axis=1)

def source_field(cells, z_pos, x_pos, y_pos, size_x, size_y, induct):
    plane = size_x * size_y
    src_z = cells // plane
    rest = cells % plane
    src_x = rest // size_y
    src_y = rest % size_y
    d_z = (z_pos[None, :] - src_z[:, None]).astype(jnp.float32)
    d_x = (x_pos[None, :] - src_x[:, None]).astype(jnp.float32)
    d_y = (y_pos[None, :] - src_y[:, None]).astype(jnp.float32)
    dist = jnp.sqrt(d_z[:, :, None, None] ** 2 + d_x[:, None, :, None] ** 2 + d_y[:, None, None, :] ** 2)
    primary = jnp.exp(-dist / ((size_x + size_y) / 8.0))
    weights = jnp.array([1.0, 0.5, 0.25], dtype=jnp.float32)
    real_part = (induct - 1.0)[None] * weights[None, :, None, None, None] * primary[:, None]
    return jnp.stack([real_part, 0.5 * real_part], axis=1)

def inner_basis(vectors, field):
    return jnp.einsum('kpczxy,spczxy->ks', vectors.astype(jnp.float32), field.astype(jnp.float32), precision=lax.Precision.HIGHEST, preferred_element_type=jnp.float32)

def combine(coeffs, vectors):
    return jnp.einsum('ks,kpczxy->spczxy', coeffs.astype(jnp.float32), vectors.astype(jnp.float32), precision=lax.Precision.HIGHEST, preferred_element_type=jnp.float32)

def per_source(left, right):
    return lax.optimization_barrier(jnp.sum(left * right, axis=(1, 2, 3, 4, 5)))

def expand(values):
    return values[:, None, None, None, None, None]

def small_solve(matrix, rhs):
    factor = jnp.linalg.cholesky(matrix)
    return jax.scipy.linalg.cho_solve((factor, True), rhs)

def reference(src_cell, basis, images, induction):
    induct = induction.astype(jnp.float32)
    z_pos = jnp.arange(NZ, dtype=jnp.int32)
    x_pos = jnp.arange(NX, dtype=jnp.int32)
    y_pos = jnp.arange(NY, dtype=jnp.int32)
    rhs = source_field(src_cell, z_pos, x_pos, y_pos, NX, NY, induct)
    gram = jnp.einsum('kpczxy,lpczxy->kl', images.astype(jnp.float32), images.astype(jnp.float32), preferred_element_type=jnp.float32)
    factor = jnp.linalg.cholesky(gram)
    h_zero = jax.scipy.linalg.cho_solve((factor, True), inner_basis(images, rhs))
    solution = combine(h_zero, basis)
    residual = rhs - combine(h_zero, images)
    widths = [(0, 0), (0, 0), (0, 0), (1, 1), (1, 1), (1, 1)]
    for cycle in range(CYCLES):
        beta = jnp.sqrt(per_source(residual, residual) + eps)
        krylov = [residual / expand(beta)]
        h_cols = []
        g_cols = []
        for step in range(ARNOLDI):
            current = krylov[step]
            work = operator(jnp.pad(current, widths), current, induct)
            g_now = jax.scipy.linalg.cho_solve((factor, True), inner_basis(images, work))
            work = work - combine(g_now, images)
            h_now = jnp.stack([per_source(vec, work) for vec in krylov])
            for index in range(step + 1):
                work = work - expand(h_now[index]) * krylov[index]
            h_next = jnp.sqrt(per_source(work, work) + eps)
            krylov.append(work / expand(h_next))
            pad_rows = jnp.zeros((ARNOLDI - step - 1, h_next.shape[0]), dtype=jnp.float32)
            h_cols.append(jnp.concatenate([h_now, h_next[None], pad_rows], axis=0))
            g_cols.append(g_now)
        hess = jnp.stack(h_cols, axis=1)
        g_all = jnp.stack(g_cols, axis=1)
        normal = jnp.einsum('ijs,iks->sjk', hess, hess, precision=lax.Precision.HIGHEST)
        target = beta[:, None] * jnp.transpose(hess[0])
        y_coef = jax.vmap(small_solve)(normal, target)
        update = expand(y_coef[:, 0]) * krylov[0]
        for step in range(1, ARNOLDI):
            update = update + expand(y_coef[:, step]) * krylov[step]
        u_coef = jnp.einsum('kjs,sj->ks', g_all, y_coef, precision=lax.Precision.HIGHEST)
        solution = solution + update - combine(u_coef, basis)
        first = jnp.zeros((ARNOLDI + 1, beta.shape[0]), dtype=jnp.float32).at[0].set(beta)
        t_coef = first - jnp.einsum('ijs,sj->is', hess, y_coef, precision=lax.Precision.HIGHEST)
        residual = expand(t_coef[0]) * krylov[0]
        for index in range(1, ARNOLDI + 1):
            residual = residual + expand(t_coef[index]) * krylov[index]
    return (solution, residual)
```

```python
import jax
import jax.numpy as jnp
from jax import lax
from jax.sharding import PartitionSpec as P

CYCLES = 2
ARNOLDI = 2


eps = 1e-06


def with_halo(x, sides, width):
    for axis, dim in sides:
        size, length = (lax.axis_size(axis), x.shape[dim])
        up = [(i, (i + 1) % size) for i in range(size - 1)]
        down = [(j, i) for i, j in up]
        last = lax.slice_in_dim(x, length - width, length, axis=dim)
        initial = lax.slice_in_dim(x, 0, width, axis=dim)
        before = lax.ppermute(last, axis, up)
        after = lax.ppermute(initial, axis, down)
        x = jnp.concatenate([before, x, after], axis=dim)
    return x


def differ(field, axis, forward):
    axis = field.ndim + axis
    count = field.shape[axis]
    delta = lax.slice_in_dim(field, 1, count, axis=axis) - lax.slice_in_dim(
        field, 0, count - 1, axis=axis
    )
    zero = jnp.zeros_like(lax.slice_in_dim(field, 0, 1, axis=axis))
    if forward:
        return jnp.concatenate([delta, zero], axis=axis)
    return jnp.concatenate([zero, delta], axis=axis)


def curl_curl(padded):
    e_x = padded[..., 0, :, :, :]
    e_y = padded[..., 1, :, :, :]
    e_z = padded[..., 2, :, :, :]
    b_x = differ(e_z, -1, True) - differ(e_y, -3, True)
    b_y = differ(e_x, -3, True) - differ(e_z, -2, True)
    b_z = differ(e_y, -2, True) - differ(e_x, -1, True)
    c_x = differ(b_z, -1, False) - differ(b_y, -3, False)
    c_y = differ(b_x, -3, False) - differ(b_z, -2, False)
    c_z = differ(b_y, -2, False) - differ(b_x, -1, False)
    whole = jnp.stack([c_x, c_y, c_z], axis=-4)
    return whole[..., 1:-1, 1:-1, 1:-1]


def apply_operator(field, induct):
    framed = with_halo(field, (("gx", 4), ("gy", 5)), 1)
    padded = jnp.pad(framed, [(0, 0), (0, 0), (0, 0), (1, 1), (0, 0), (0, 0)])
    curled = curl_curl(padded)
    real_part = curled[:, 0] - induct[None] * field[:, 1]
    imag_part = curled[:, 1] + induct[None] * field[:, 0]
    return jnp.stack([real_part, imag_part], axis=1)


def source_field(cells, z_pos, x_pos, y_pos, size_x, size_y, induct):
    plane = size_x * size_y
    src_z = cells // plane
    rest = cells % plane
    src_x = rest // size_y
    src_y = rest % size_y
    d_z = (z_pos[None, :] - src_z[:, None]).astype(jnp.float32)
    d_x = (x_pos[None, :] - src_x[:, None]).astype(jnp.float32)
    d_y = (y_pos[None, :] - src_y[:, None]).astype(jnp.float32)
    dist = jnp.sqrt(
        d_z[:, :, None, None] ** 2 + d_x[:, None, :, None] ** 2 + d_y[:, None, None, :] ** 2
    )
    primary = jnp.exp(-dist / ((size_x + size_y) / 8.0))
    weights = jnp.array([1.0, 0.5, 0.25], dtype=jnp.float32)
    real_part = (induct - 1.0)[None] * weights[None, :, None, None, None] * primary[:, None]
    return jnp.stack([real_part, 0.5 * real_part], axis=1)


def inner_basis(vectors, field):
    return jnp.einsum(
        "kpczxy,spczxy->ks",
        vectors,
        field,
        precision=lax.Precision.HIGHEST,
        preferred_element_type=jnp.float32,
    )


def combine(coeffs, vectors):
    return jnp.einsum(
        "ks,kpczxy->spczxy",
        coeffs,
        vectors,
        precision=lax.Precision.HIGHEST,
        preferred_element_type=jnp.float32,
    )


def per_source(left, right):
    return jnp.sum(left * right, axis=(1, 2, 3, 4, 5))


def expand(values):
    return values[:, None, None, None, None, None]


def small_solve(matrix, rhs):
    factor = jnp.linalg.cholesky(matrix)
    return jax.scipy.linalg.cho_solve((factor, True), rhs)


def all_sum(parts):
    flat = jnp.concatenate([jnp.ravel(part) for part in parts])
    count = flat.shape[0]
    rows = -(-count // 128)
    flat = jnp.pad(flat, (0, rows * 128 - count)).reshape(1, rows, 128)
    size = lax.axis_size("gx") * lax.axis_size("gy")
    sent = jnp.broadcast_to(flat, (size, rows, 128))
    total = jnp.sum(lax.all_to_all(sent, ("gx", "gy"), 0, 0), axis=0).reshape(-1)
    result = []
    start = 0
    for part in parts:
        result.append(total[start : start + part.size].reshape(part.shape))
        start += part.size
    return result


def on_device(src_cell, basis, images, induction):
    all_basis, all_images, gathered = (
        lax.all_gather(basis, "tx", axis=0, tiled=True),
        lax.all_gather(images, "tx", axis=0, tiled=True),
        lax.all_gather(induction, "tx", axis=1, tiled=True),
    )
    induct = gathered.astype(jnp.float32)
    depth = basis.shape[3]
    width_x = basis.shape[4]
    width_y = basis.shape[5]
    size_x = width_x * lax.axis_size("gx")
    size_y = width_y * lax.axis_size("gy")
    z_pos = jnp.arange(depth, dtype=jnp.int32)
    x_pos = lax.axis_index("gx") * width_x + jnp.arange(width_x, dtype=jnp.int32)
    y_pos = lax.axis_index("gy") * width_y + jnp.arange(width_y, dtype=jnp.int32)
    rhs = source_field(src_cell, z_pos, x_pos, y_pos, size_x, size_y, induct)
    gram_part = jnp.einsum(
        "kpczxy,lpczxy->kl", all_images, all_images, preferred_element_type=jnp.float32
    )
    gram, start_inner = all_sum((gram_part, inner_basis(all_images, rhs)))
    factor = jnp.linalg.cholesky(gram)
    h_zero = jax.scipy.linalg.cho_solve((factor, True), start_inner)
    residual = rhs - combine(h_zero, all_images)
    solution = combine(h_zero, all_basis)
    for cycle in range(CYCLES):
        beta = jnp.sqrt(all_sum([per_source(residual, residual)])[0] + eps)
        krylov = [residual / expand(beta)]
        h_cols = []
        g_cols = []
        for step in range(ARNOLDI):
            work = apply_operator(krylov[step], induct)
            sums = all_sum(
                [inner_basis(all_images, work), per_source(work, work)]
                + [per_source(vec, work) for vec in krylov]
                + [per_source(one, two) for one in krylov for two in krylov]
            )
            g_raw, w_norm = sums[0], sums[1]
            g_now = jax.scipy.linalg.cho_solve((factor, True), g_raw)
            count = step + 1
            h_now = jnp.stack(sums[2 : 2 + count])
            among = jnp.stack(sums[2 + count :]).reshape(count, count, -1)
            work = work - combine(g_now, all_images)
            for index in range(step + 1):
                work = work - expand(h_now[index]) * krylov[index]
            left = w_norm - jnp.sum(g_now * g_raw, axis=0) - 2.0 * jnp.sum(h_now * h_now, axis=0)
            left = left + jnp.sum(h_now[:, None] * h_now[None] * among, axis=(0, 1))
            h_next = jnp.sqrt(jnp.maximum(left, 0.0) + eps)
            krylov.append(work / expand(h_next))
            pad_rows = jnp.zeros((ARNOLDI - step - 1, h_next.shape[0]), dtype=jnp.float32)
            h_cols.append(jnp.concatenate([h_now, h_next[None], pad_rows], axis=0))
            g_cols.append(g_now)
        hess = jnp.stack(h_cols, axis=1)
        g_all = jnp.stack(g_cols, axis=1)
        normal = jnp.einsum("ijs,iks->sjk", hess, hess, precision=lax.Precision.HIGHEST)
        target = beta[:, None] * jnp.transpose(hess[0])
        y_coef = jax.vmap(small_solve)(normal, target)
        update = expand(y_coef[:, 0]) * krylov[0]
        step = 1
        update = update + expand(y_coef[:, step]) * krylov[step]
        u_coef = jnp.einsum("kjs,sj->ks", g_all, y_coef, precision=lax.Precision.HIGHEST)
        solution = solution + update - combine(u_coef, all_basis)
        first = jnp.zeros((ARNOLDI + 1, beta.shape[0]), dtype=jnp.float32).at[0].set(beta)
        t_coef = first - jnp.einsum("ijs,sj->is", hess, y_coef, precision=lax.Precision.HIGHEST)
        residual = expand(t_coef[0]) * krylov[0]
        for index in range(1, ARNOLDI + 1):
            residual = residual + expand(t_coef[index]) * krylov[index]
    return (solution, residual)


def solution(mesh):
    in_specs = (
        P("tx"),
        P("tx", None, None, None, "gx", "gy"),
        P("tx", None, None, None, "gx", "gy"),
        P(None, "tx", "gx", "gy"),
    )
    out_specs = (P("tx", None, None, None, "gx", "gy"), P("tx", None, None, None, "gx", "gy"))
    return jax.shard_map(
        on_device, mesh=mesh, in_specs=in_specs, out_specs=out_specs, check_vma=False
    )
```

```python
import functools

import jax
import jax.numpy as jnp
from jax import lax
from jax.experimental import pallas as pl
from jax.experimental.pallas import tpu as pltpu
from jax.sharding import PartitionSpec as P

EPS = 1e-06
VECS = 16
LOCAL = 4
ROWS = 48
BLOCK = 198
HALF = 99
PACKED = 13
WEIGHTS = (1.0, 0.5, 0.25)
HIGH = lax.Precision.HIGHEST
F32 = jnp.float32
BF16 = jnp.bfloat16


def iota(shape, axis):
    return lax.broadcasted_iota(jnp.int32, shape, axis)


def pick_matrix(dtype):
    col = iota((8, 128), 0)
    lane = iota((8, 128), 1)
    return jnp.where(lane == jnp.where(col < 4, col, col + 120), 1.0, 0.0).astype(dtype)


def nt_dot(left, right, precision=None):
    return lax.dot_general(
        left, right, (((1,), (1,)), ((), ())), precision=precision, preferred_element_type=F32
    )


def full_dot(left, right):
    return lax.dot_general(
        left, right, (((1,), (0,)), ((), ())), precision=HIGH, preferred_element_type=F32
    )


def pack_y_kernel(block_ref, out_ref):
    pick = pick_matrix(BF16)
    for tile in range(PACKED):
        first = tile * 16
        count = min(16, BLOCK - first)
        rows = block_ref[first : first + count].astype(F32).reshape(count * 8, 128).astype(BF16)
        picked = nt_dot(pick, rows)
        if count < 16:
            picked = jnp.concatenate([picked, jnp.zeros((8, 128 - count * 8), F32)], axis=1)
        out_ref[:, tile * 128 : (tile + 1) * 128] = picked.astype(BF16)


def pack_x_kernel(*refs):
    blocks, packed, lo_ref, hi_ref = refs[:4], refs[4:8], refs[8], refs[9]
    top = iota((1, 8, 128), 1) < 4
    for d in range(LOCAL):
        block = blocks[d]

        def body(step, carry, block=block, d=d):
            first = step * 3

            def pair(one, two, at, size):
                one = one.astype(F32)
                two = pltpu.roll(two.astype(F32), 4, 1)
                lo_ref[pl.ds(d * HALF + at, size)] = jnp.where(top, one, two).astype(BF16)
                hi_ref[pl.ds(d * HALF + at, size)] = jnp.where(top, two, one).astype(BF16)

            pair(block[pl.ds(first, 3)], block[pl.ds(first + 96, 3)], first, 3)
            return carry

        lax.fori_loop(0, 32, body, 0)
        one = block[192:195].astype(F32)
        two = pltpu.roll(block[195:198].astype(F32), 4, 1)
        lo_ref[d * HALF + 96 : d * HALF + 99] = jnp.where(top, one, two).astype(BF16)
        hi_ref[d * HALF + 96 : d * HALF + 99] = jnp.where(top, two, one).astype(BF16)
        for tile in range(PACKED):
            piece = packed[d][:, tile * 128 : (tile + 1) * 128]
            lo_ref[4 * HALF + d * PACKED + tile] = piece
            hi_ref[4 * HALF + d * PACKED + tile] = piece


def vector_row(blocks, d, kl, j):
    return blocks[d][kl * ROWS + j].astype(F32)


def inner_all(blocks, field, sums_ref):
    def body(j, accs):
        one, two = field(0, j), field(1, j)
        new = []
        for d in range(LOCAL):
            for kl in range(LOCAL):
                vec = vector_row(blocks, d, kl, j)
                at = 2 * (d * LOCAL + kl)
                new.append(accs[at] + vec * one)
                new.append(accs[at + 1] + vec * two)
        return tuple(new)

    zero = jnp.zeros((8, 128), F32)
    accs = lax.fori_loop(0, ROWS, body, (zero,) * (2 * VECS))
    for k in range(VECS):
        for s in range(2):
            sums_ref[s * VECS + k : s * VECS + k + 1] = jnp.sum(
                accs[2 * k + s], axis=0, keepdims=True
            )


def inner_pairs(pairs, sums_ref, first):
    count = len(pairs)
    for s in range(2):

        def body(j, accs, s=s):
            return tuple(
                acc + one(s, j) * two(s, j) for acc, (one, two) in zip(accs, pairs)
            )

        zero = jnp.zeros((8, 128), F32)
        accs = lax.fori_loop(0, ROWS, body, (zero,) * count)
        for i in range(count):
            at = first + s * count + i
            sums_ref[at : at + 1] = jnp.sum(accs[i], axis=0, keepdims=True)


def row_of_sums(sums_ref):
    return nt_dot(jnp.ones((8, 128), F32), sums_ref[...], HIGH)[0:1]


def entry(row, lane):
    return row[:, lane : lane + 1]


def column_of(row, first):
    part = row[:, first : first + VECS]
    eye = iota((VECS, VECS), 0) == iota((VECS, VECS), 1)
    return jnp.sum(jnp.where(eye, part, 0.0), axis=1, keepdims=True)


def solve(inverse, row, first):
    return jnp.sum(inverse[:, :VECS] * row[:, first : first + VECS], axis=1, keepdims=True)


def spread(value):
    return jnp.broadcast_to(value, (8, 128))


def grid_mask(size_x, size_y):
    row, lane = iota((16, 256), 0), iota((16, 256), 1)
    x_pos = lax.axis_index("gx") * 8 + jnp.where(row < 12, row, row - 16)
    y_pos = lax.axis_index("gy") * 128 + jnp.where(lane < 132, lane, lane - 256)
    inside = (x_pos >= 0) & (x_pos < size_x) & (y_pos >= 0) & (y_pos < size_y)
    inside = inside & ((lane < 132) | (lane >= 252))
    return x_pos, y_pos, inside


def primary_field(cell, z, x_pos, y_pos, size_x, size_y):
    plane = size_x * size_y
    src_z = cell // plane
    rest = cell % plane
    d_z = (z - src_z).astype(F32)
    d_x = (x_pos - rest // size_y).astype(F32)
    d_y = (y_pos - rest % size_y).astype(F32)
    dist = jnp.sqrt(d_z * d_z + d_x * d_x + d_y * d_y)
    return jnp.exp(-dist / ((size_x + size_y) / 8.0))


def combine_ext(coeffs, blocks, packed, ln_ref, hp_ref, interior, halo_x, unpacked_ref):
    top = iota((8, 128), 0) < 4

    def body(j, carry):
        inner = [jnp.zeros((8, 128), F32)] * 2
        straight = [jnp.zeros((8, 128), F32)] * 2
        rolled = [jnp.zeros((8, 128), F32)] * 2
        for d in range(LOCAL):
            for kl in range(LOCAL):
                k = d * LOCAL + kl
                vec = vector_row(blocks, d, kl, j)
                at = d * HALF + (kl % 2) * ROWS + j
                after, before = ln_ref[at].astype(F32), hp_ref[at].astype(F32)
                outer = straight if kl < 2 else rolled
                edge = jnp.where(top, after, before) if kl < 2 else jnp.where(top, before, after)
                for s in range(2):
                    inner[s] = inner[s] + coeffs[s][k] * vec
                    outer[s] = outer[s] + coeffs[s][k] * edge
        for s in range(2):
            interior(s, j, inner[s])
            halo_x(s, j, straight[s] + pltpu.roll(rolled[s], 4, 0))
        return carry

    lax.fori_loop(0, ROWS, body, 0)
    pick = pick_matrix(F32)
    from_next = iota((8, 128), 1) % 8 < 4
    for s in range(2):
        for tile in range(3):
            near = jnp.zeros((8, 128), F32)
            far = jnp.zeros((8, 128), F32)
            for d in range(LOCAL):
                for kl in range(LOCAL):
                    k = d * LOCAL + kl
                    t = kl * 3 + tile
                    at = 4 * HALF + d * PACKED + t
                    near = near + coeffs[s][k] * packed[d][:, t * 128 : (t + 1) * 128].astype(F32)
                    edge = jnp.where(from_next, ln_ref[at].astype(F32), hp_ref[at].astype(F32))
                    far = far + coeffs[s][k] * edge
            place = s * ROWS + tile * 16
            near = full_dot(jnp.transpose(near), pick).reshape(16, 8, 128)
            far = full_dot(jnp.transpose(far), pick).reshape(16, 8, 128)
            unpacked_ref[place : place + 16, 0:8] = near
            unpacked_ref[place : place + 16, 8:16] = far


def apply_operator(e_ref, m_ref, out_ref, mask):
    def ahead(f, axis):
        return pltpu.roll(f, f.shape[axis] - 1, axis)

    def behind(f, axis):
        return pltpu.roll(f, 1, axis)

    def body(index, carry):
        base = index * 24
        other = jnp.where(index % 2 == 0, base + 24, base - 24)
        sign = jnp.where(index % 2 == 0, -1.0, 1.0).astype(F32)
        zero = jnp.zeros((16, 256), F32)
        b_x_old = -e_ref[base + 8]
        b_y_old = e_ref[base]
        for z in range(8):
            e_x, e_y, e_z = e_ref[base + z], e_ref[base + 8 + z], e_ref[base + 16 + z]
            up_x = e_ref[base + z + 1] if z < 7 else zero
            up_y = e_ref[base + 8 + z + 1] if z < 7 else zero
            b_x = (ahead(e_z, 1) - e_z) - (up_y - e_y)
            b_y = (up_x - e_x) - (ahead(e_z, 0) - e_z)
            b_z = (ahead(e_y, 0) - e_y) - (ahead(e_x, 1) - e_x)
            c_x = (b_z - behind(b_z, 1)) - (b_y - b_y_old)
            c_y = (b_x - b_x_old) - (b_z - behind(b_z, 0))
            c_z = (b_y - behind(b_y, 0)) - (b_x - behind(b_x, 1))
            for c, value in enumerate((c_x, c_y, c_z)):
                at = c * 8 + z
                value = value + sign * (m_ref[at] * e_ref[other + at])
                out_ref[base + at] = jnp.where(mask, value, 0.0)
            b_x_old, b_y_old = b_x, b_y
        return carry

    lax.fori_loop(0, 4, body, 0)


def brick(ref):
    return lambda s, j: ref[s * ROWS + j, 0:8, 0:128]


def pick_layer(values, z):
    want = lax.rem(lax.axis_index("tx") - z // 2 + LOCAL, LOCAL)
    result = values[0]
    for d in range(1, LOCAL):
        result = jnp.where(want == d, values[d], result)
    return result


def gram_kernel(size_x, size_y, src_ref, *refs):
    blocks, out_ref, field_ref, sums_ref = refs[:4], refs[4], refs[5], refs[6]
    x_pos = lax.axis_index("gx") * 8 + iota((8, 128), 0)
    y_pos = lax.axis_index("gy") * 128 + iota((8, 128), 1)
    for z in range(8):
        prim = [
            primary_field(src_ref[s], z, x_pos, y_pos, size_x, size_y) for s in range(2)
        ]
        for c in range(3):
            m = pick_layer([b[192 + 2 * c + z % 2].astype(F32) for b in blocks], z)
            for s in range(2):
                real = (m - 1.0) * WEIGHTS[c] * prim[s]
                field_ref[s * ROWS + c * 8 + z] = real
                field_ref[s * ROWS + 24 + c * 8 + z] = 0.5 * real
    sums_ref[...] = jnp.zeros_like(sums_ref)
    inner_all(blocks, lambda s, j: field_ref[s * ROWS + j], sums_ref)

    def body(j, acc):
        rows = jnp.concatenate(
            [vector_row(blocks, d, kl, j) for d in range(LOCAL) for kl in range(LOCAL)], axis=0
        ).astype(BF16)
        return acc + nt_dot(rows, rows)

    gram = lax.fori_loop(0, ROWS, body, jnp.zeros((128, 128), F32))
    row, lane = iota((128, 128), 0), iota((128, 128), 1)
    gram = jnp.where(row % 8 == lane % 8, gram, 0.0).reshape(VECS, 8, 128)
    gram = jnp.sum(gram, axis=1)
    gram = full_dot(gram, jnp.where(row // 8 == lane % 16, 1.0, 0.0).astype(F32))
    gram = jnp.where(iota((VECS, 128), 1) // 16 == iota((VECS, 128), 0) % 8, gram, 0.0)
    gram = jnp.sum(gram.reshape(2, 8, 128), axis=1)
    rows = jnp.concatenate([gram, row_of_sums(sums_ref), jnp.zeros((1, 128), F32)], axis=0)
    out_ref[...] = jnp.broadcast_to(rows[None], out_ref.shape)


def invert(rows):
    lane, row = iota((VECS, 128), 1), iota((VECS, 128), 0)
    wide = jnp.where(row < 8, rows[0:1], rows[1:2])
    wide = jnp.where(lane // 16 == row % 8, wide, 0.0)
    fold = jnp.where(iota((128, 128), 0) % 16 == iota((128, 128), 1), 1.0, 0.0).astype(F32)
    work = full_dot(wide, fold) + jnp.where(lane == row + VECS, 1.0, 0.0)
    for j in range(VECS):
        pivot = work[j : j + 1] / work[j : j + 1, j : j + 1]
        work = jnp.where(row == j, pivot, work - work[:, j : j + 1] * pivot)
    return pltpu.roll(work, 128 - VECS, 1)


def begin_kernel(size_x, size_y, src_ref, got_ref, *refs):
    blocks, packed, ln_ref, hp_ref = refs[:4], refs[4:8], refs[8], refs[9]
    r_ref, q_ref, m_ref, inv_ref, state_ref, out_ref, side_ref, sums_ref = refs[10:]
    total = jnp.sum(got_ref[...], axis=0)
    inverse = invert(total[0:2])
    inv_ref[...] = inverse
    inner = total[2:3]
    x_pos, y_pos, mask = grid_mask(size_x, size_y)
    start = [solve(inverse, inner, s * VECS) for s in range(2)]
    lane = iota((VECS, 128), 1)
    state_ref[...] = jnp.where(lane == 2, start[0], jnp.where(lane == 3, start[1], 0.0))
    coeffs = [[spread(-start[s][k : k + 1]) for k in range(VECS)] for s in range(2)]

    def put(rows, columns):
        def store(s, j, value):
            r_ref[s * ROWS + j, rows, columns] = value

        return store

    combine_ext(
        coeffs, blocks, packed, ln_ref, hp_ref,
        put(slice(0, 8), slice(0, 128)), put(slice(8, 16), slice(0, 128)), side_ref,
    )
    top = iota((8, 128), 0) < 4
    from_next = iota((8, 128), 1) % 8 < 4
    pick = pick_matrix(F32)
    sides = []
    for d in range(LOCAL):
        at = 4 * HALF + d * PACKED + 12
        near = packed[d][:, 12 * 128 : 13 * 128].astype(F32)
        far = jnp.where(from_next, ln_ref[at].astype(F32), hp_ref[at].astype(F32))
        near = full_dot(jnp.transpose(near), pick)[:48].reshape(6, 8, 128)
        far = full_dot(jnp.transpose(far), pick)[:48].reshape(6, 8, 128)
        sides.append((near, far))
    for c in range(3):
        for z in range(8):
            at = 2 * c + z % 2
            quarters = []
            for d in range(LOCAL):
                inner_m = blocks[d][192 + at].astype(F32)
                row = d * HALF + 96 + at % 3
                after, before = ln_ref[row].astype(F32), hp_ref[row].astype(F32)
                if at < 3:
                    edge = jnp.where(top, after, before)
                else:
                    edge = pltpu.roll(jnp.where(top, before, after), 4, 0)
                left = jnp.concatenate([inner_m, edge], axis=0)
                right = jnp.concatenate([sides[d][0][at], sides[d][1][at]], axis=0)
                quarters.append(jnp.concatenate([left, right], axis=1))
            m_ref[c * 8 + z] = pick_layer(quarters, z)

    for s in range(2):

        def body(z, carry, s=s):
            prim = primary_field(src_ref[s], z, x_pos, y_pos, size_x, size_y)
            for c in range(3):
                at = c * 8 + z
                real = jnp.where(mask, (m_ref[at] - 1.0) * WEIGHTS[c] * prim, 0.0)
                for p in range(2):
                    place = s * ROWS + p * 24 + at
                    value = real if p == 0 else 0.5 * real
                    r_ref[place, :, 0:128] = r_ref[place, :, 0:128] + value[:, 0:128]
                    r_ref[place, :, 128:256] = side_ref[place] + value[:, 128:256]
            return carry

        lax.fori_loop(0, 8, body, 0)
    apply_operator(r_ref, m_ref, q_ref, mask)
    finish_first(blocks, r_ref, q_ref, sums_ref, out_ref)


def finish_first(blocks, r_ref, q_ref, sums_ref, out_ref):
    sums_ref[...] = jnp.zeros_like(sums_ref)
    r, q = brick(r_ref), brick(q_ref)
    inner_all(blocks, q, sums_ref)
    inner_pairs([(r, r), (r, q)], sums_ref, 32)
    out_ref[...] = jnp.broadcast_to(row_of_sums(sums_ref), out_ref.shape)


def first_kernel(size_x, size_y, got_ref, *refs):
    blocks, packed, ln_ref, hp_ref = refs[:4], refs[4:8], refs[8], refs[9]
    r_ref, q_ref, m_ref, inv_ref, old_ref = refs[10:15]
    u_ref, a_ref, state_ref, out_ref, side_ref, sums_ref = refs[15:]
    row = jnp.sum(got_ref[...], axis=0, keepdims=True)
    _, _, mask = grid_mask(size_x, size_y)
    lane = iota((VECS, 128), 1)
    state = old_ref[...]
    coeffs, q_scale, r_scale = [], [], []
    for s in range(2):
        rr, rq = entry(row, 32 + 2 * s), entry(row, 33 + 2 * s)
        beta = jnp.sqrt(rr + EPS)
        g_zero = solve(inv_ref[...], row, s * VECS) / beta
        h_00 = rq / (beta * beta)
        coeffs.append([spread(-g_zero[k : k + 1]) for k in range(VECS)])
        q_scale.append(spread(1.0 / beta))
        r_scale.append(spread(-h_00 / beta))
        state = jnp.where(lane == s, g_zero, state)
        state = jnp.where(lane == 8 + s, beta, state)
        state = jnp.where(lane == 10 + s, h_00, state)
        state = jnp.where(lane == 12 + s, rr, state)
    state_ref[...] = state

    def put(rows, columns):
        def store(s, j, value):
            at = s * ROWS + j
            value = value + q_scale[s] * q_ref[at, rows, columns]
            u_ref[at, rows, columns] = value + r_scale[s] * r_ref[at, rows, columns]

        return store

    combine_ext(
        coeffs, blocks, packed, ln_ref, hp_ref,
        put(slice(0, 8), slice(0, 128)), put(slice(8, 16), slice(0, 128)), side_ref,
    )
    for s in range(2):

        def body(j, carry, s=s):
            at = s * ROWS + j
            value = side_ref[at]
            for half in range(2):
                rows = slice(half * 8, half * 8 + 8)
                new = value[rows] + q_scale[s] * q_ref[at, rows, 128:256]
                u_ref[at, rows, 128:256] = new + r_scale[s] * r_ref[at, rows, 128:256]
            return carry

        lax.fori_loop(0, ROWS, body, 0)
    apply_operator(u_ref, m_ref, a_ref, mask)
    sums_ref[...] = jnp.zeros_like(sums_ref)
    r, u, a = brick(r_ref), brick(u_ref), brick(a_ref)
    inner_all(blocks, a, sums_ref)
    inner_pairs([(u, u), (r, u), (r, a), (u, a), (a, a)], sums_ref, 32)
    out_ref[...] = jnp.broadcast_to(row_of_sums(sums_ref), out_ref.shape)


def close_cycle(row, inverse, state, s):
    uu, ru, ra, ua, aa = [entry(row, 32 + 5 * s + i) for i in range(5)]
    g_zero = state[:, s : s + 1]
    beta, h_00, rr = [state[0:1, first + s : first + s + 1] for first in (8, 10, 12)]
    h_10 = jnp.sqrt(uu + EPS)
    inner = column_of(row, s * VECS) / h_10
    g_one = solve(inverse, row, s * VECS) / h_10
    h_01 = ra / (beta * h_10)
    h_11 = ua / (h_10 * h_10)
    left = aa / (h_10 * h_10) - jnp.sum(g_one * inner, axis=0, keepdims=True)
    left = left - 2.0 * (h_01 * h_01 + h_11 * h_11)
    left = left + h_01 * h_01 * (rr / (beta * beta)) + h_11 * h_11 * (uu / (h_10 * h_10))
    left = left + 2.0 * h_01 * h_11 * (ru / (beta * h_10))
    h_21_square = jnp.maximum(left, 0.0) + EPS
    n_00 = h_00 * h_00 + h_10 * h_10
    n_01 = h_00 * h_01 + h_10 * h_11
    n_11 = h_01 * h_01 + h_11 * h_11 + h_21_square
    l_00 = jnp.sqrt(n_00)
    l_10 = n_01 / l_00
    l_11 = jnp.sqrt(n_11 - l_10 * l_10)
    z_0 = beta * h_00 / l_00
    z_1 = (beta * h_01 - l_10 * z_0) / l_11
    y_1 = z_1 / l_11
    y_0 = (z_0 - l_10 * y_1) / l_00
    t_0 = beta - h_00 * y_0 - h_01 * y_1
    t_1 = -h_10 * y_0 - h_11 * y_1
    return {
        "r": (t_0 + y_1 * h_01) / beta,
        "u": (t_1 + y_1 * h_11) / h_10,
        "a": -y_1 / h_10,
        "c": y_1 * g_one,
        "sol_r": y_0 / beta,
        "sol_u": y_1 / h_10,
        "basis": state[:, 2 + s : 3 + s] - g_zero * y_0 - g_one * y_1,
    }


def next_kernel(size_x, size_y, got_ref, *refs):
    blocks, packed, ln_ref, hp_ref = refs[:4], refs[4:8], refs[8], refs[9]
    r_ref, u_ref, a_ref, m_ref, inv_ref, old_ref = refs[10:16]
    new_ref, q_ref, sol_ref, state_ref, out_ref, side_ref, sums_ref = refs[16:]
    row = jnp.sum(got_ref[...], axis=0, keepdims=True)
    _, _, mask = grid_mask(size_x, size_y)
    state = old_ref[...]
    small = [close_cycle(row, inv_ref[...], state, s) for s in range(2)]
    lane = iota((VECS, 128), 1)
    state_ref[...] = jnp.where(
        lane == 2, small[0]["basis"], jnp.where(lane == 3, small[1]["basis"], 0.0)
    )
    coeffs = [[spread(small[s]["c"][k : k + 1]) for k in range(VECS)] for s in range(2)]
    scale = [{name: spread(small[s][name]) for name in ("r", "u", "a", "sol_r", "sol_u")} for s in range(2)]

    def total(s, at, rows, columns, value):
        value = value + scale[s]["r"] * r_ref[at, rows, columns]
        value = value + scale[s]["u"] * u_ref[at, rows, columns]
        return value + scale[s]["a"] * a_ref[at, rows, columns]

    def put(rows, columns):
        def store(s, j, value):
            at = s * ROWS + j
            new_ref[at, rows, columns] = total(s, at, rows, columns, value)

        return store

    combine_ext(
        coeffs, blocks, packed, ln_ref, hp_ref,
        put(slice(0, 8), slice(0, 128)), put(slice(8, 16), slice(0, 128)), side_ref,
    )
    for s in range(2):

        def body(j, carry, s=s):
            at = s * ROWS + j
            value = side_ref[at]
            for half in range(2):
                rows = slice(half * 8, half * 8 + 8)
                new_ref[at, rows, 128:256] = total(s, at, rows, slice(128, 256), value[rows])
            sol_ref[at] = (
                scale[s]["sol_r"] * r_ref[at, 0:8, 0:128]
                + scale[s]["sol_u"] * u_ref[at, 0:8, 0:128]
            )
            return carry

        lax.fori_loop(0, ROWS, body, 0)
    apply_operator(new_ref, m_ref, q_ref, mask)
    finish_first(blocks, new_ref, q_ref, sums_ref, out_ref)


def last_kernel(got_ref, *refs):
    blocks, basis = refs[:4], refs[4:8]
    r_ref, u_ref, a_ref, inv_ref, old_ref, sol_ref = refs[8:14]
    solution_ref, residual_ref = refs[14:]
    row = jnp.sum(got_ref[...], axis=0, keepdims=True)
    state = old_ref[...]
    for s in range(2):
        small = close_cycle(row, inv_ref[...], state, s)
        coeffs = [spread(small["c"][k : k + 1]) for k in range(VECS)]
        base_coeffs = [spread(small["basis"][k : k + 1]) for k in range(VECS)]
        scale = {name: spread(small[name]) for name in ("r", "u", "a", "sol_r", "sol_u")}

        def body(j, carry, s=s, coeffs=coeffs, base_coeffs=base_coeffs, scale=scale):
            at = s * ROWS + j
            r, u, a = brick(r_ref)(s, j), brick(u_ref)(s, j), brick(a_ref)(s, j)
            value = scale["r"] * r + scale["u"] * u + scale["a"] * a
            field = sol_ref[at] + scale["sol_r"] * r + scale["sol_u"] * u
            for d in range(LOCAL):
                for kl in range(LOCAL):
                    k = d * LOCAL + kl
                    value = value + coeffs[k] * vector_row(blocks, d, kl, j)
                    field = field + base_coeffs[k] * vector_row(basis, d, kl, j)
            residual_ref[at] = value
            solution_ref[at] = field
            return carry

        lax.fori_loop(0, ROWS, body, 0)


def call(kernel, outs, args, scratch=(), smem=0):
    vmem = pl.BlockSpec(memory_space=pltpu.VMEM)
    return pl.pallas_call(
        kernel,
        out_shape=outs,
        in_specs=[pl.BlockSpec(memory_space=pltpu.SMEM)] * smem + [vmem] * (len(args) - smem),
        out_specs=jax.tree.map(lambda _: vmem, outs),
        scratch_shapes=list(scratch),
        compiler_params=pltpu.CompilerParams(vmem_limit_bytes=48 * 1024 * 1024),
    )(*args)


def shape(*dims, dtype=F32):
    return jax.ShapeDtypeStruct(dims, dtype)


def exchange(value):
    return lax.all_to_all(value, ("gx", "gy"), 0, 0)


def around(value, axis):
    up = [(i, i + 1) for i in range(lax.axis_size(axis) - 1)]
    return value, up, [(j, i) for i, j in up]


def gather(value):
    return [value] + [
        lax.ppermute(value, "tx", [(i, (i + d) % LOCAL) for i in range(LOCAL)])
        for d in range(1, LOCAL)
    ]


def on_device(src_cell, basis, images, induction):
    size_x, size_y = 8 * lax.axis_size("gx"), 128 * lax.axis_size("gy")
    peers = lax.axis_size("gx") * lax.axis_size("gy")
    block = jnp.concatenate(
        [images.reshape(LOCAL * ROWS, 8, 128), induction.reshape(6, 8, 128)], axis=0
    )
    blocks = gather(block)
    own = call(pack_y_kernel, shape(8, PACKED * 128, dtype=BF16), (block,))
    _, up, down = around(own, "gy")
    after, before = lax.ppermute(own, "gy", down), lax.ppermute(own, "gy", up)
    side = jnp.where(lax.broadcasted_iota(jnp.int32, own.shape, 0) < 4, after, before)
    packed = gather(side)

    half = shape(LOCAL * (HALF + PACKED), 8, 128, dtype=BF16)
    low, high = call(pack_x_kernel, (half, half), (*blocks, *packed))
    _, up, down = around(low, "gx")
    ln, hp = lax.ppermute(low, "gx", down), lax.ppermute(high, "gx", up)

    sums = pltpu.VMEM((128, 128), F32)
    side_scratch = pltpu.VMEM((2 * ROWS, 16, 128), F32)
    sent = call(
        functools.partial(gram_kernel, size_x, size_y),
        shape(peers, 4, 128),
        (src_cell, *blocks),
        (pltpu.VMEM((2 * ROWS, 8, 128), F32), sums),
        smem=1,
    )
    got = exchange(sent)
    wide = shape(2 * ROWS, 16, 256)
    line = shape(peers, 128)
    small = shape(VECS, 128)
    static = (*blocks, *packed, ln, hp)
    r, q, m, inverse, state, sent = call(
        functools.partial(begin_kernel, size_x, size_y),
        (wide, wide, shape(24, 16, 256), small, small, line),
        (src_cell, got, *static),
        (side_scratch, sums),
        smem=1,
    )
    bases = gather(basis.reshape(LOCAL * ROWS, 8, 128))

    def total(value):
        return exchange(value.reshape(peers, 1, 128)).reshape(peers, 128)

    def first(r, q, state, sent):
        return call(
            functools.partial(first_kernel, size_x, size_y),
            (wide, wide, small, line),
            (total(sent), *static, r, q, m, inverse, state),
            (side_scratch, sums),
        )

    u, a, state, sent = first(r, q, state, sent)
    r, q, field, state, sent = call(
        functools.partial(next_kernel, size_x, size_y),
        (wide, wide, shape(2 * ROWS, 8, 128), small, line),
        (total(sent), *static, r, u, a, m, inverse, state),
        (side_scratch, sums),
    )
    u, a, state, sent = first(r, q, state, sent)
    narrow = shape(2 * ROWS, 8, 128)
    field, residual = call(
        last_kernel,
        (narrow, narrow),
        (total(sent), *blocks, *bases, r, u, a, inverse, state, field),
    )
    full = (2, 2, 3, 8, 8, 128)
    return field.reshape(full), residual.reshape(full)


def solution(mesh):
    in_specs = (
        P("tx"),
        P("tx", None, None, None, "gx", "gy"),
        P("tx", None, None, None, "gx", "gy"),
        P(None, "tx", "gx", "gy"),
    )
    out_specs = (P("tx", None, None, None, "gx", "gy"), P("tx", None, None, None, "gx", "gy"))
    return jax.shard_map(
        on_device, mesh=mesh, in_specs=in_specs, out_specs=out_specs, check_vma=False
    )
```

```python
import functools

import jax
import jax.numpy as jnp
from jax import lax
from jax.experimental import pallas as pl
from jax.experimental.pallas import tpu as pltpu
from jax.sharding import PartitionSpec as P

EPS = 1e-06
VECS = 16
LOCAL = 4
ROWS = 48
BLOCK = 198
HALF = 99
PACKED = 13
WEIGHTS = (1.0, 0.5, 0.25)
HIGH = lax.Precision.HIGHEST
F32 = jnp.float32
BF16 = jnp.bfloat16


def iota(shape, axis):
    return lax.broadcasted_iota(jnp.int32, shape, axis)


def pick_matrix(dtype):
    col = iota((8, 128), 0)
    lane = iota((8, 128), 1)
    return jnp.where(lane == jnp.where(col < 4, col, col + 120), 1.0, 0.0).astype(dtype)


def nt_dot(left, right, precision=None):
    return lax.dot_general(
        left, right, (((1,), (1,)), ((), ())), precision=precision, preferred_element_type=F32
    )


def full_dot(left, right):
    return lax.dot_general(
        left, right, (((1,), (0,)), ((), ())), precision=HIGH, preferred_element_type=F32
    )


def owner(d):
    return lax.rem(lax.axis_index("tx") - d + LOCAL, LOCAL)


def pack_y_kernel(block_ref, out_ref):
    pick = pick_matrix(BF16)
    for tile in range(PACKED):
        first = tile * 16
        count = min(16, BLOCK - first)
        rows = block_ref[first : first + count].astype(F32).reshape(count * 8, 128).astype(BF16)
        picked = nt_dot(pick, rows)
        if count < 16:
            picked = jnp.concatenate([picked, jnp.zeros((8, 128 - count * 8), F32)], axis=1)
        out_ref[:, tile * 128 : (tile + 1) * 128] = picked.astype(BF16)


def pack_x_kernel(*refs):
    blocks, packed, lo_ref, hi_ref = refs[:4], refs[4], refs[5], refs[6]
    top = iota((1, 8, 128), 1) < 4
    for d in range(LOCAL):
        block = blocks[d]

        def body(step, carry, block=block, d=d):
            first = step * 3

            def pair(one, two, at, size):
                one = one.astype(F32)
                two = pltpu.roll(two.astype(F32), 4, 1)
                lo_ref[pl.ds(d * HALF + at, size)] = jnp.where(top, one, two).astype(BF16)
                hi_ref[pl.ds(d * HALF + at, size)] = jnp.where(top, two, one).astype(BF16)

            pair(block[pl.ds(first, 3)], block[pl.ds(first + 96, 3)], first, 3)
            return carry

        lax.fori_loop(0, 32, body, 0)
        one = block[192:195].astype(F32)
        two = pltpu.roll(block[195:198].astype(F32), 4, 1)
        lo_ref[d * HALF + 96 : d * HALF + 99] = jnp.where(top, one, two).astype(BF16)
        hi_ref[d * HALF + 96 : d * HALF + 99] = jnp.where(top, two, one).astype(BF16)
        for tile in range(PACKED):
            piece = packed[owner(d), :, tile * 128 : (tile + 1) * 128]
            lo_ref[4 * HALF + d * PACKED + tile] = piece
            hi_ref[4 * HALF + d * PACKED + tile] = piece


def vector_row(blocks, d, kl, j):
    return blocks[d][kl * ROWS + j].astype(F32)


def inner_all(blocks, field, sums_ref):
    def body(j, accs):
        one, two = field(0, j), field(1, j)
        new = []
        for d in range(LOCAL):
            for kl in range(LOCAL):
                vec = vector_row(blocks, d, kl, j)
                at = 2 * (d * LOCAL + kl)
                new.append(accs[at] + vec * one)
                new.append(accs[at + 1] + vec * two)
        return tuple(new)

    zero = jnp.zeros((8, 128), F32)
    accs = lax.fori_loop(0, ROWS, body, (zero,) * (2 * VECS))
    for k in range(VECS):
        for s in range(2):
            sums_ref[s * VECS + k : s * VECS + k + 1] = jnp.sum(
                accs[2 * k + s], axis=0, keepdims=True
            )


def inner_pairs(pairs, sums_ref, first):
    count = len(pairs)
    for s in range(2):

        def body(j, accs, s=s):
            return tuple(
                acc + one(s, j) * two(s, j) for acc, (one, two) in zip(accs, pairs)
            )

        zero = jnp.zeros((8, 128), F32)
        accs = lax.fori_loop(0, ROWS, body, (zero,) * count)
        for i in range(count):
            at = first + s * count + i
            sums_ref[at : at + 1] = jnp.sum(accs[i], axis=0, keepdims=True)


def row_of_sums(sums_ref):
    return nt_dot(jnp.ones((8, 128), F32), sums_ref[...], HIGH)[0:1]


def entry(row, lane):
    return row[:, lane : lane + 1]


def column_of(row, first):
    part = row[:, first : first + VECS]
    eye = iota((VECS, VECS), 0) == iota((VECS, VECS), 1)
    return jnp.sum(jnp.where(eye, part, 0.0), axis=1, keepdims=True)


def solve(inverse, row, first):
    return jnp.sum(inverse[:, :VECS] * row[:, first : first + VECS], axis=1, keepdims=True)


def spread(value):
    return jnp.broadcast_to(value, (8, 128))


def grid_mask(size_x, size_y):
    row, lane = iota((16, 256), 0), iota((16, 256), 1)
    x_pos = lax.axis_index("gx") * 8 + jnp.where(row < 12, row, row - 16)
    y_pos = lax.axis_index("gy") * 128 + jnp.where(lane < 132, lane, lane - 256)
    inside = (x_pos >= 0) & (x_pos < size_x) & (y_pos >= 0) & (y_pos < size_y)
    inside = inside & ((lane < 132) | (lane >= 252))
    return x_pos, y_pos, inside


def primary_field(cell, z, x_pos, y_pos, size_x, size_y):
    plane = size_x * size_y
    src_z = cell // plane
    rest = cell % plane
    d_z = (z - src_z).astype(F32)
    d_x = (x_pos - rest // size_y).astype(F32)
    d_y = (y_pos - rest % size_y).astype(F32)
    dist = jnp.sqrt(d_z * d_z + d_x * d_x + d_y * d_y)
    return jnp.exp(-dist / ((size_x + size_y) / 8.0))


def combine_ext(coeffs, blocks, packed, ln_ref, hp_ref, interior, halo_x, unpacked_ref):
    top = iota((8, 128), 0) < 4

    def body(j, carry):
        inner = [jnp.zeros((8, 128), F32)] * 2
        straight = [jnp.zeros((8, 128), F32)] * 2
        rolled = [jnp.zeros((8, 128), F32)] * 2
        for d in range(LOCAL):
            for kl in range(LOCAL):
                k = d * LOCAL + kl
                vec = vector_row(blocks, d, kl, j)
                at = d * HALF + (kl % 2) * ROWS + j
                after, before = ln_ref[at].astype(F32), hp_ref[at].astype(F32)
                outer = straight if kl < 2 else rolled
                edge = jnp.where(top, after, before) if kl < 2 else jnp.where(top, before, after)
                for s in range(2):
                    inner[s] = inner[s] + coeffs[s][k] * vec
                    outer[s] = outer[s] + coeffs[s][k] * edge
        for s in range(2):
            interior(s, j, inner[s])
            halo_x(s, j, straight[s] + pltpu.roll(rolled[s], 4, 0))
        return carry

    lax.fori_loop(0, ROWS, body, 0)
    pick = pick_matrix(F32)
    from_next = iota((8, 128), 1) % 8 < 4
    for s in range(2):
        for tile in range(3):
            near = jnp.zeros((8, 128), F32)
            far = jnp.zeros((8, 128), F32)
            for d in range(LOCAL):
                for kl in range(LOCAL):
                    k = d * LOCAL + kl
                    t = kl * 3 + tile
                    at = 4 * HALF + d * PACKED + t
                    near = near + coeffs[s][k] * packed[
                        owner(d), :, t * 128 : (t + 1) * 128
                    ].astype(F32)
                    edge = jnp.where(from_next, ln_ref[at].astype(F32), hp_ref[at].astype(F32))
                    far = far + coeffs[s][k] * edge
            place = s * ROWS + tile * 16
            near = full_dot(jnp.transpose(near), pick).reshape(16, 8, 128)
            far = full_dot(jnp.transpose(far), pick).reshape(16, 8, 128)
            unpacked_ref[place : place + 16, 0:8] = near
            unpacked_ref[place : place + 16, 8:16] = far


def apply_operator(e_ref, m_ref, out_ref, mask):
    def ahead(f, axis):
        return pltpu.roll(f, f.shape[axis] - 1, axis)

    def behind(f, axis):
        return pltpu.roll(f, 1, axis)

    def body(index, carry):
        base = index * 24
        other = jnp.where(index % 2 == 0, base + 24, base - 24)
        sign = jnp.where(index % 2 == 0, -1.0, 1.0).astype(F32)
        zero = jnp.zeros((16, 256), F32)
        b_x_old = -e_ref[base + 8]
        b_y_old = e_ref[base]
        for z in range(8):
            e_x, e_y, e_z = e_ref[base + z], e_ref[base + 8 + z], e_ref[base + 16 + z]
            up_x = e_ref[base + z + 1] if z < 7 else zero
            up_y = e_ref[base + 8 + z + 1] if z < 7 else zero
            b_x = (ahead(e_z, 1) - e_z) - (up_y - e_y)
            b_y = (up_x - e_x) - (ahead(e_z, 0) - e_z)
            b_z = (ahead(e_y, 0) - e_y) - (ahead(e_x, 1) - e_x)
            c_x = (b_z - behind(b_z, 1)) - (b_y - b_y_old)
            c_y = (b_x - b_x_old) - (b_z - behind(b_z, 0))
            c_z = (b_y - behind(b_y, 0)) - (b_x - behind(b_x, 1))
            for c, value in enumerate((c_x, c_y, c_z)):
                at = c * 8 + z
                value = value + sign * (m_ref[at] * e_ref[other + at])
                out_ref[base + at] = jnp.where(mask, value, 0.0)
            b_x_old, b_y_old = b_x, b_y
        return carry

    lax.fori_loop(0, 4, body, 0)


def brick(ref):
    return lambda s, j: ref[s * ROWS + j, 0:8, 0:128]


def pick_layer(values, z):
    want = lax.rem(lax.axis_index("tx") - z // 2 + LOCAL, LOCAL)
    result = values[0]
    for d in range(1, LOCAL):
        result = jnp.where(want == d, values[d], result)
    return result


def gram_kernel(size_x, size_y, src_ref, *refs):
    blocks, out_ref, field_ref, rows_ref = refs[:4], refs[4], refs[5], refs[6]
    x_pos = lax.axis_index("gx") * 8 + iota((8, 128), 0)
    y_pos = lax.axis_index("gy") * 128 + iota((8, 128), 1)
    for z in range(8):
        prim = [
            primary_field(src_ref[s], z, x_pos, y_pos, size_x, size_y) for s in range(2)
        ]
        for c in range(3):
            m = pick_layer([b[192 + 2 * c + z % 2].astype(F32) for b in blocks], z)
            for s in range(2):
                real = (m - 1.0) * WEIGHTS[c] * prim[s]
                field_ref[c * 8 + z, s * 8 : s * 8 + 8] = real
                field_ref[24 + c * 8 + z, s * 8 : s * 8 + 8] = 0.5 * real

    def body(j, carry):
        columns = pl.ds(pl.multiple_of(j * 128, 128), 128)
        for pair in range(VECS // 2):
            d, kl = pair // 2, 2 * (pair % 2)
            both = [vector_row(blocks, d, kl + i, j) for i in range(2)]
            rows_ref[16 * pair : 16 * pair + 16, columns] = jnp.concatenate(both).astype(BF16)
        rest = field_ref[j]
        for piece in range(3):
            part = rest.astype(BF16)
            rest = rest - part.astype(F32)
            first = 8 * VECS + 16 * piece
            rows_ref[first : first + 16, columns] = part
        return carry

    lax.fori_loop(0, ROWS, body, 0)
    full = nt_dot(rows_ref[0:128], rows_ref[...])
    row, lane = iota((128, 128), 0), iota((128, 128), 1)
    gram = jnp.where(row % 8 == lane % 8, full[:, 0:128], 0.0).reshape(VECS, 8, 128)
    gram = jnp.sum(gram, axis=1)
    gram = full_dot(gram, jnp.where(row // 8 == lane % 16, 1.0, 0.0).astype(F32))
    gram = jnp.where(iota((VECS, 128), 1) // 16 == iota((VECS, 128), 0) % 8, gram, 0.0)
    gram = jnp.sum(gram.reshape(2, 8, 128), axis=1)
    inner = full[:, 128:144] + full[:, 144:160] + full[:, 160:176]
    inner = jnp.where(iota((128, 16), 0) % 8 == iota((128, 16), 1) % 8, inner, 0.0)
    inner = jnp.sum(inner.reshape(VECS, 8, 16), axis=1)
    lines = []
    for s in range(2):
        chosen = jnp.where(iota((8, 16), 1) // 8 == s, 1.0, 0.0).astype(F32)
        lines.append(nt_dot(chosen, inner, HIGH)[0:1])
    line = jnp.concatenate(lines + [jnp.zeros((1, 96), F32)], axis=1)
    rows = jnp.concatenate([gram, line, jnp.zeros((1, 128), F32)], axis=0)
    out_ref[...] = jnp.broadcast_to(rows[None], out_ref.shape)


def invert(rows):
    lane, row = iota((VECS, 128), 1), iota((VECS, 128), 0)
    wide = jnp.where(row < 8, rows[0:1], rows[1:2])
    wide = jnp.where(lane // 16 == row % 8, wide, 0.0)
    fold = jnp.where(iota((128, 128), 0) % 16 == iota((128, 128), 1), 1.0, 0.0).astype(F32)
    work = full_dot(wide, fold) + jnp.where(lane == row + VECS, 1.0, 0.0)
    for j in range(VECS):
        pivot = work[j : j + 1] / work[j : j + 1, j : j + 1]
        work = jnp.where(row == j, pivot, work - work[:, j : j + 1] * pivot)
    return pltpu.roll(work, 128 - VECS, 1)


def begin_kernel(size_x, size_y, src_ref, got_ref, *refs):
    blocks, packed, ln_ref, hp_ref = refs[:4], refs[4], refs[5], refs[6]
    r_ref, q_ref, m_ref, inv_ref, state_ref, out_ref, side_ref, sums_ref = refs[7:]
    total = jnp.sum(got_ref[...], axis=0)
    inverse = invert(total[0:2])
    inv_ref[...] = inverse
    inner = total[2:3]
    x_pos, y_pos, mask = grid_mask(size_x, size_y)
    start = [solve(inverse, inner, s * VECS) for s in range(2)]
    lane = iota((VECS, 128), 1)
    state_ref[...] = jnp.where(lane == 2, start[0], jnp.where(lane == 3, start[1], 0.0))
    coeffs = [[spread(-start[s][k : k + 1]) for k in range(VECS)] for s in range(2)]

    def put(rows, columns):
        def store(s, j, value):
            r_ref[s * ROWS + j, rows, columns] = value

        return store

    combine_ext(
        coeffs, blocks, packed, ln_ref, hp_ref,
        put(slice(0, 8), slice(0, 128)), put(slice(8, 16), slice(0, 128)), side_ref,
    )
    top = iota((8, 128), 0) < 4
    from_next = iota((8, 128), 1) % 8 < 4
    pick = pick_matrix(F32)
    sides = []
    for d in range(LOCAL):
        at = 4 * HALF + d * PACKED + 12
        near = packed[owner(d), :, 12 * 128 : 13 * 128].astype(F32)
        far = jnp.where(from_next, ln_ref[at].astype(F32), hp_ref[at].astype(F32))
        near = full_dot(jnp.transpose(near), pick)[:48].reshape(6, 8, 128)
        far = full_dot(jnp.transpose(far), pick)[:48].reshape(6, 8, 128)
        sides.append((near, far))
    for c in range(3):
        for z in range(8):
            at = 2 * c + z % 2
            quarters = []
            for d in range(LOCAL):
                inner_m = blocks[d][192 + at].astype(F32)
                row = d * HALF + 96 + at % 3
                after, before = ln_ref[row].astype(F32), hp_ref[row].astype(F32)
                if at < 3:
                    edge = jnp.where(top, after, before)
                else:
                    edge = pltpu.roll(jnp.where(top, before, after), 4, 0)
                left = jnp.concatenate([inner_m, edge], axis=0)
                right = jnp.concatenate([sides[d][0][at], sides[d][1][at]], axis=0)
                quarters.append(jnp.concatenate([left, right], axis=1))
            m_ref[c * 8 + z] = pick_layer(quarters, z)

    for s in range(2):

        def body(z, carry, s=s):
            prim = primary_field(src_ref[s], z, x_pos, y_pos, size_x, size_y)
            for c in range(3):
                at = c * 8 + z
                real = jnp.where(mask, (m_ref[at] - 1.0) * WEIGHTS[c] * prim, 0.0)
                for p in range(2):
                    place = s * ROWS + p * 24 + at
                    value = real if p == 0 else 0.5 * real
                    r_ref[place, :, 0:128] = r_ref[place, :, 0:128] + value[:, 0:128]
                    r_ref[place, :, 128:256] = side_ref[place] + value[:, 128:256]
            return carry

        lax.fori_loop(0, 8, body, 0)
    apply_operator(r_ref, m_ref, q_ref, mask)
    finish_first(blocks, r_ref, q_ref, sums_ref, out_ref)


def finish_first(blocks, r_ref, q_ref, sums_ref, out_ref):
    sums_ref[...] = jnp.zeros_like(sums_ref)
    r, q = brick(r_ref), brick(q_ref)
    inner_all(blocks, q, sums_ref)
    inner_pairs([(r, r), (r, q)], sums_ref, 32)
    out_ref[...] = jnp.broadcast_to(row_of_sums(sums_ref), out_ref.shape)


def first_kernel(size_x, size_y, got_ref, *refs):
    blocks, packed, ln_ref, hp_ref = refs[:4], refs[4], refs[5], refs[6]
    r_ref, q_ref, m_ref, inv_ref, old_ref = refs[7:12]
    u_ref, a_ref, state_ref, out_ref, side_ref, sums_ref = refs[12:]
    row = jnp.sum(got_ref[...], axis=0, keepdims=True)
    _, _, mask = grid_mask(size_x, size_y)
    lane = iota((VECS, 128), 1)
    state = old_ref[...]
    coeffs, q_scale, r_scale = [], [], []
    for s in range(2):
        rr, rq = entry(row, 32 + 2 * s), entry(row, 33 + 2 * s)
        beta = jnp.sqrt(rr + EPS)
        g_zero = solve(inv_ref[...], row, s * VECS) / beta
        h_00 = rq / (beta * beta)
        coeffs.append([spread(-g_zero[k : k + 1]) for k in range(VECS)])
        q_scale.append(spread(1.0 / beta))
        r_scale.append(spread(-h_00 / beta))
        state = jnp.where(lane == s, g_zero, state)
        state = jnp.where(lane == 8 + s, beta, state)
        state = jnp.where(lane == 10 + s, h_00, state)
        state = jnp.where(lane == 12 + s, rr, state)
    state_ref[...] = state

    def put(rows, columns):
        def store(s, j, value):
            at = s * ROWS + j
            value = value + q_scale[s] * q_ref[at, rows, columns]
            u_ref[at, rows, columns] = value + r_scale[s] * r_ref[at, rows, columns]

        return store

    combine_ext(
        coeffs, blocks, packed, ln_ref, hp_ref,
        put(slice(0, 8), slice(0, 128)), put(slice(8, 16), slice(0, 128)), side_ref,
    )
    for s in range(2):

        def body(j, carry, s=s):
            at = s * ROWS + j
            value = side_ref[at]
            for half in range(2):
                rows = slice(half * 8, half * 8 + 8)
                new = value[rows] + q_scale[s] * q_ref[at, rows, 128:256]
                u_ref[at, rows, 128:256] = new + r_scale[s] * r_ref[at, rows, 128:256]
            return carry

        lax.fori_loop(0, ROWS, body, 0)
    apply_operator(u_ref, m_ref, a_ref, mask)
    sums_ref[...] = jnp.zeros_like(sums_ref)
    r, u, a = brick(r_ref), brick(u_ref), brick(a_ref)
    inner_all(blocks, a, sums_ref)
    inner_pairs([(u, u), (r, u), (r, a), (u, a), (a, a)], sums_ref, 32)
    out_ref[...] = jnp.broadcast_to(row_of_sums(sums_ref), out_ref.shape)


def close_cycle(row, inverse, state, s):
    uu, ru, ra, ua, aa = [entry(row, 32 + 5 * s + i) for i in range(5)]
    g_zero = state[:, s : s + 1]
    beta, h_00, rr = [state[0:1, first + s : first + s + 1] for first in (8, 10, 12)]
    h_10 = jnp.sqrt(uu + EPS)
    inner = column_of(row, s * VECS) / h_10
    g_one = solve(inverse, row, s * VECS) / h_10
    h_01 = ra / (beta * h_10)
    h_11 = ua / (h_10 * h_10)
    left = aa / (h_10 * h_10) - jnp.sum(g_one * inner, axis=0, keepdims=True)
    left = left - 2.0 * (h_01 * h_01 + h_11 * h_11)
    left = left + h_01 * h_01 * (rr / (beta * beta)) + h_11 * h_11 * (uu / (h_10 * h_10))
    left = left + 2.0 * h_01 * h_11 * (ru / (beta * h_10))
    h_21_square = jnp.maximum(left, 0.0) + EPS
    n_00 = h_00 * h_00 + h_10 * h_10
    n_01 = h_00 * h_01 + h_10 * h_11
    n_11 = h_01 * h_01 + h_11 * h_11 + h_21_square
    l_00 = jnp.sqrt(n_00)
    l_10 = n_01 / l_00
    l_11 = jnp.sqrt(n_11 - l_10 * l_10)
    z_0 = beta * h_00 / l_00
    z_1 = (beta * h_01 - l_10 * z_0) / l_11
    y_1 = z_1 / l_11
    y_0 = (z_0 - l_10 * y_1) / l_00
    t_0 = beta - h_00 * y_0 - h_01 * y_1
    t_1 = -h_10 * y_0 - h_11 * y_1
    return {
        "r": (t_0 + y_1 * h_01) / beta,
        "u": (t_1 + y_1 * h_11) / h_10,
        "a": -y_1 / h_10,
        "c": y_1 * g_one,
        "sol_r": y_0 / beta,
        "sol_u": y_1 / h_10,
        "basis": state[:, 2 + s : 3 + s] - g_zero * y_0 - g_one * y_1,
    }


def next_kernel(size_x, size_y, got_ref, *refs):
    blocks, packed, ln_ref, hp_ref = refs[:4], refs[4], refs[5], refs[6]
    r_ref, u_ref, a_ref, m_ref, inv_ref, old_ref = refs[7:13]
    new_ref, q_ref, sol_ref, state_ref, out_ref, side_ref, sums_ref = refs[13:]
    row = jnp.sum(got_ref[...], axis=0, keepdims=True)
    _, _, mask = grid_mask(size_x, size_y)
    state = old_ref[...]
    small = [close_cycle(row, inv_ref[...], state, s) for s in range(2)]
    lane = iota((VECS, 128), 1)
    state_ref[...] = jnp.where(
        lane == 2, small[0]["basis"], jnp.where(lane == 3, small[1]["basis"], 0.0)
    )
    coeffs = [[spread(small[s]["c"][k : k + 1]) for k in range(VECS)] for s in range(2)]
    scale = [{name: spread(small[s][name]) for name in ("r", "u", "a", "sol_r", "sol_u")} for s in range(2)]

    def total(s, at, rows, columns, value):
        value = value + scale[s]["r"] * r_ref[at, rows, columns]
        value = value + scale[s]["u"] * u_ref[at, rows, columns]
        return value + scale[s]["a"] * a_ref[at, rows, columns]

    def put(rows, columns):
        def store(s, j, value):
            at = s * ROWS + j
            new_ref[at, rows, columns] = total(s, at, rows, columns, value)

        return store

    combine_ext(
        coeffs, blocks, packed, ln_ref, hp_ref,
        put(slice(0, 8), slice(0, 128)), put(slice(8, 16), slice(0, 128)), side_ref,
    )
    for s in range(2):

        def body(j, carry, s=s):
            at = s * ROWS + j
            value = side_ref[at]
            for half in range(2):
                rows = slice(half * 8, half * 8 + 8)
                new_ref[at, rows, 128:256] = total(s, at, rows, slice(128, 256), value[rows])
            sol_ref[at] = (
                scale[s]["sol_r"] * r_ref[at, 0:8, 0:128]
                + scale[s]["sol_u"] * u_ref[at, 0:8, 0:128]
            )
            return carry

        lax.fori_loop(0, ROWS, body, 0)
    apply_operator(new_ref, m_ref, q_ref, mask)
    finish_first(blocks, new_ref, q_ref, sums_ref, out_ref)


def last_kernel(got_ref, *refs):
    blocks, basis = refs[:4], refs[4]
    r_ref, u_ref, a_ref, inv_ref, old_ref, sol_ref = refs[5:11]
    solution_ref, residual_ref = refs[11:]
    row = jnp.sum(got_ref[...], axis=0, keepdims=True)
    state = old_ref[...]
    for s in range(2):
        small = close_cycle(row, inv_ref[...], state, s)
        coeffs = [spread(small["c"][k : k + 1]) for k in range(VECS)]
        base_coeffs = [spread(small["basis"][k : k + 1]) for k in range(VECS)]
        scale = {name: spread(small[name]) for name in ("r", "u", "a", "sol_r", "sol_u")}

        def body(j, carry, s=s, coeffs=coeffs, base_coeffs=base_coeffs, scale=scale):
            at = s * ROWS + j
            r, u, a = brick(r_ref)(s, j), brick(u_ref)(s, j), brick(a_ref)(s, j)
            value = scale["r"] * r + scale["u"] * u + scale["a"] * a
            field = sol_ref[at] + scale["sol_r"] * r + scale["sol_u"] * u
            for d in range(LOCAL):
                for kl in range(LOCAL):
                    k = d * LOCAL + kl
                    value = value + coeffs[k] * vector_row(blocks, d, kl, j)
                    field = field + base_coeffs[k] * basis[
                        (owner(d) * LOCAL + kl) * ROWS + j
                    ].astype(F32)
            residual_ref[at] = value
            solution_ref[at] = field
            return carry

        lax.fori_loop(0, ROWS, body, 0)


def call(kernel, outs, args, scratch=(), smem=0):
    vmem = pl.BlockSpec(memory_space=pltpu.VMEM)
    return pl.pallas_call(
        kernel,
        out_shape=outs,
        in_specs=[pl.BlockSpec(memory_space=pltpu.SMEM)] * smem + [vmem] * (len(args) - smem),
        out_specs=jax.tree.map(lambda _: vmem, outs),
        scratch_shapes=list(scratch),
        compiler_params=pltpu.CompilerParams(vmem_limit_bytes=20 * 1024 * 1024),
    )(*args)


def shape(*dims, dtype=F32):
    return jax.ShapeDtypeStruct(dims, dtype)


def exchange(value):
    return lax.all_to_all(value, ("gx", "gy"), 0, 0)


def around(value, axis):
    up = [(i, i + 1) for i in range(lax.axis_size(axis) - 1)]
    return value, up, [(j, i) for i, j in up]


def gather(value):
    return [value] + [
        lax.ppermute(value, "tx", [(i, (i + d) % LOCAL) for i in range(LOCAL)])
        for d in range(1, LOCAL)
    ]


def on_device(src_cell, basis, images, induction):
    size_x, size_y = 8 * lax.axis_size("gx"), 128 * lax.axis_size("gy")
    peers = lax.axis_size("gx") * lax.axis_size("gy")
    block = jnp.concatenate(
        [images.reshape(LOCAL * ROWS, 8, 128), induction.reshape(6, 8, 128)], axis=0
    )
    blocks = gather(block)
    own = call(pack_y_kernel, shape(8, PACKED * 128, dtype=BF16), (block,))
    _, up, down = around(own, "gy")
    after, before = lax.ppermute(own, "gy", down), lax.ppermute(own, "gy", up)
    side = jnp.where(lax.broadcasted_iota(jnp.int32, own.shape, 0) < 4, after, before)
    packed = lax.all_to_all(jnp.broadcast_to(side, (LOCAL, *side.shape)), "tx", 0, 0)

    half = shape(LOCAL * (HALF + PACKED), 8, 128, dtype=BF16)
    low, high = call(pack_x_kernel, (half, half), (*blocks, packed))
    _, up, down = around(low, "gx")
    ln, hp = lax.ppermute(low, "gx", down), lax.ppermute(high, "gx", up)

    sums = pltpu.VMEM((128, 128), F32)
    side_scratch = pltpu.VMEM((2 * ROWS, 16, 128), F32)
    sent = call(
        functools.partial(gram_kernel, size_x, size_y),
        shape(peers, 4, 128),
        (src_cell, *blocks),
        (pltpu.VMEM((ROWS, 16, 128), F32), pltpu.VMEM((8 * VECS + 48, ROWS * 128), BF16)),
        smem=1,
    )
    got = exchange(sent)
    wide = shape(2 * ROWS, 16, 256)
    line = shape(peers, 128)
    small = shape(VECS, 128)
    static = (*blocks, packed, ln, hp)
    r, q, m, inverse, state, sent = call(
        functools.partial(begin_kernel, size_x, size_y),
        (wide, wide, shape(24, 16, 256), small, small, line),
        (src_cell, got, *static),
        (side_scratch, sums),
        smem=1,
    )
    own_basis, _ = lax.optimization_barrier((basis.reshape(LOCAL * ROWS, 8, 128), blocks[2]))
    bases = lax.all_gather(own_basis, "tx", tiled=True)

    def total(value):
        return exchange(value.reshape(peers, 1, 128)).reshape(peers, 128)

    def first(r, q, state, sent):
        return call(
            functools.partial(first_kernel, size_x, size_y),
            (wide, wide, small, line),
            (total(sent), *static, r, q, m, inverse, state),
            (side_scratch, sums),
        )

    u, a, state, sent = first(r, q, state, sent)
    r, q, field, state, sent = call(
        functools.partial(next_kernel, size_x, size_y),
        (wide, wide, shape(2 * ROWS, 8, 128), small, line),
        (total(sent), *static, r, u, a, m, inverse, state),
        (side_scratch, sums),
    )
    u, a, state, sent = first(r, q, state, sent)
    narrow = shape(2 * ROWS, 8, 128)
    field, residual = call(
        last_kernel,
        (narrow, narrow),
        (total(sent), *blocks, bases, r, u, a, inverse, state, field),
    )
    full = (2, 2, 3, 8, 8, 128)
    return field.reshape(full), residual.reshape(full)


def solution(mesh):
    in_specs = (
        P("tx"),
        P("tx", None, None, None, "gx", "gy"),
        P("tx", None, None, None, "gx", "gy"),
        P(None, "tx", "gx", "gy"),
    )
    out_specs = (P("tx", None, None, None, "gx", "gy"), P("tx", None, None, None, "gx", "gy"))
    return jax.shard_map(
        on_device, mesh=mesh, in_specs=in_specs, out_specs=out_specs, check_vma=False
    )
```

```python
import functools

import jax
import jax.numpy as jnp
from jax import lax
from jax.experimental import pallas as pl
from jax.experimental.pallas import tpu as pltpu
from jax.sharding import PartitionSpec as P

EPS = 1e-06
VECS = 16
LOCAL = 4
ROWS = 48
BLOCK = 198
HALF = 99
PACKED = 13
WEIGHTS = (1.0, 0.5, 0.25)
HIGH = lax.Precision.HIGHEST
F32 = jnp.float32
BF16 = jnp.bfloat16


def iota(shape, axis):
    return lax.broadcasted_iota(jnp.int32, shape, axis)


def pick_matrix(dtype):
    col = iota((8, 128), 0)
    lane = iota((8, 128), 1)
    return jnp.where(lane == jnp.where(col < 4, col, col + 120), 1.0, 0.0).astype(dtype)


def nt_dot(left, right, precision=None):
    return lax.dot_general(
        left, right, (((1,), (1,)), ((), ())), precision=precision, preferred_element_type=F32
    )


def full_dot(left, right):
    return lax.dot_general(
        left, right, (((1,), (0,)), ((), ())), precision=HIGH, preferred_element_type=F32
    )


def owner(d):
    return lax.rem(lax.axis_index("tx") - d + LOCAL, LOCAL)


def pack_y_kernel(block_ref, out_ref):
    pick = pick_matrix(BF16)
    for tile in range(PACKED):
        first = tile * 16
        count = min(16, BLOCK - first)
        rows = block_ref[first : first + count].astype(F32).reshape(count * 8, 128).astype(BF16)
        picked = nt_dot(pick, rows)
        if count < 16:
            picked = jnp.concatenate([picked, jnp.zeros((8, 128 - count * 8), F32)], axis=1)
        out_ref[:, tile * 128 : (tile + 1) * 128] = picked.astype(BF16)


def pack_x_kernel(*refs):
    blocks, packed, lo_ref, hi_ref = refs[:4], refs[4], refs[5], refs[6]
    top = iota((1, 8, 128), 1) < 4
    for d in range(LOCAL):
        block = blocks[d]

        def body(step, carry, block=block, d=d):
            first = step * 3

            def pair(one, two, at, size):
                one = one.astype(F32)
                two = pltpu.roll(two.astype(F32), 4, 1)
                lo_ref[pl.ds(d * HALF + at, size)] = jnp.where(top, one, two).astype(BF16)
                hi_ref[pl.ds(d * HALF + at, size)] = jnp.where(top, two, one).astype(BF16)

            pair(block[pl.ds(first, 3)], block[pl.ds(first + 96, 3)], first, 3)
            return carry

        lax.fori_loop(0, 32, body, 0)
        one = block[192:195].astype(F32)
        two = pltpu.roll(block[195:198].astype(F32), 4, 1)
        lo_ref[d * HALF + 96 : d * HALF + 99] = jnp.where(top, one, two).astype(BF16)
        hi_ref[d * HALF + 96 : d * HALF + 99] = jnp.where(top, two, one).astype(BF16)
        for tile in range(PACKED):
            piece = packed[owner(d), :, tile * 128 : (tile + 1) * 128]
            lo_ref[4 * HALF + d * PACKED + tile] = piece
            hi_ref[4 * HALF + d * PACKED + tile] = piece


def vector_row(blocks, d, kl, j):
    return blocks[d][kl * ROWS + j].astype(F32)


def inner_all(blocks, field, sums_ref):
    def body(j, accs):
        one, two = field(0, j), field(1, j)
        new = []
        for d in range(LOCAL):
            for kl in range(LOCAL):
                vec = vector_row(blocks, d, kl, j)
                at = 2 * (d * LOCAL + kl)
                new.append(accs[at] + vec * one)
                new.append(accs[at + 1] + vec * two)
        return tuple(new)

    zero = jnp.zeros((8, 128), F32)
    accs = lax.fori_loop(0, ROWS, body, (zero,) * (2 * VECS))
    for k in range(VECS):
        for s in range(2):
            sums_ref[s * VECS + k : s * VECS + k + 1] = jnp.sum(
                accs[2 * k + s], axis=0, keepdims=True
            )


def inner_pairs(pairs, sums_ref, first):
    count = len(pairs)
    for s in range(2):

        def body(j, accs, s=s):
            return tuple(
                acc + one(s, j) * two(s, j) for acc, (one, two) in zip(accs, pairs)
            )

        zero = jnp.zeros((8, 128), F32)
        accs = lax.fori_loop(0, ROWS, body, (zero,) * count)
        for i in range(count):
            at = first + s * count + i
            sums_ref[at : at + 1] = jnp.sum(accs[i], axis=0, keepdims=True)


def row_of_sums(sums_ref):
    return nt_dot(jnp.ones((8, 128), F32), sums_ref[...], HIGH)[0:1]


def entry(row, lane):
    return row[:, lane : lane + 1]


def column_of(row, first):
    part = row[:, first : first + VECS]
    eye = iota((VECS, VECS), 0) == iota((VECS, VECS), 1)
    return jnp.sum(jnp.where(eye, part, 0.0), axis=1, keepdims=True)


def solve(inverse, row, first):
    return jnp.sum(inverse[:, :VECS] * row[:, first : first + VECS], axis=1, keepdims=True)


def spread(value):
    return jnp.broadcast_to(value, (8, 128))


def grid_mask(size_x, size_y):
    row, lane = iota((16, 256), 0), iota((16, 256), 1)
    x_pos = lax.axis_index("gx") * 8 + jnp.where(row < 12, row, row - 16)
    y_pos = lax.axis_index("gy") * 128 + jnp.where(lane < 132, lane, lane - 256)
    inside = (x_pos >= 0) & (x_pos < size_x) & (y_pos >= 0) & (y_pos < size_y)
    inside = inside & ((lane < 132) | (lane >= 252))
    return x_pos, y_pos, inside


def primary_field(cell, z, x_pos, y_pos, size_x, size_y):
    plane = size_x * size_y
    src_z = cell // plane
    rest = cell % plane
    d_z = (z - src_z).astype(F32)
    d_x = (x_pos - rest // size_y).astype(F32)
    d_y = (y_pos - rest % size_y).astype(F32)
    dist = jnp.sqrt(d_z * d_z + d_x * d_x + d_y * d_y)
    return jnp.exp(-dist / ((size_x + size_y) / 8.0))


def combine_ext(coeffs, blocks, packed, ln_ref, hp_ref, interior, halo_x, unpacked_ref):
    top = iota((8, 128), 0) < 4

    def body(j, carry):
        inner = [jnp.zeros((8, 128), F32)] * 2
        straight = [jnp.zeros((8, 128), F32)] * 2
        rolled = [jnp.zeros((8, 128), F32)] * 2
        for d in range(LOCAL):
            for kl in range(LOCAL):
                k = d * LOCAL + kl
                vec = vector_row(blocks, d, kl, j)
                at = d * HALF + (kl % 2) * ROWS + j
                after, before = ln_ref[at].astype(F32), hp_ref[at].astype(F32)
                outer = straight if kl < 2 else rolled
                edge = jnp.where(top, after, before) if kl < 2 else jnp.where(top, before, after)
                for s in range(2):
                    inner[s] = inner[s] + coeffs[s][k] * vec
                    outer[s] = outer[s] + coeffs[s][k] * edge
        for s in range(2):
            interior(s, j, inner[s])
            halo_x(s, j, straight[s] + pltpu.roll(rolled[s], 4, 0))
        return carry

    lax.fori_loop(0, ROWS, body, 0)
    pick = pick_matrix(F32)
    from_next = iota((8, 128), 1) % 8 < 4
    for s in range(2):
        for tile in range(3):
            near = jnp.zeros((8, 128), F32)
            far = jnp.zeros((8, 128), F32)
            for d in range(LOCAL):
                for kl in range(LOCAL):
                    k = d * LOCAL + kl
                    t = kl * 3 + tile
                    at = 4 * HALF + d * PACKED + t
                    near = near + coeffs[s][k] * packed[
                        owner(d), :, t * 128 : (t + 1) * 128
                    ].astype(F32)
                    edge = jnp.where(from_next, ln_ref[at].astype(F32), hp_ref[at].astype(F32))
                    far = far + coeffs[s][k] * edge
            place = s * ROWS + tile * 16
            near = full_dot(jnp.transpose(near), pick).reshape(16, 8, 128)
            far = full_dot(jnp.transpose(far), pick).reshape(16, 8, 128)
            unpacked_ref[place : place + 16, 0:8] = near
            unpacked_ref[place : place + 16, 8:16] = far


def apply_operator(e_ref, m_ref, out_ref, mask):
    def ahead(f, axis):
        return pltpu.roll(f, f.shape[axis] - 1, axis)

    def behind(f, axis):
        return pltpu.roll(f, 1, axis)

    def body(index, carry):
        base = index * 24
        other = jnp.where(index % 2 == 0, base + 24, base - 24)
        sign = jnp.where(index % 2 == 0, -1.0, 1.0).astype(F32)
        zero = jnp.zeros((16, 256), F32)
        b_x_old = -e_ref[base + 8]
        b_y_old = e_ref[base]
        for z in range(8):
            e_x, e_y, e_z = e_ref[base + z], e_ref[base + 8 + z], e_ref[base + 16 + z]
            up_x = e_ref[base + z + 1] if z < 7 else zero
            up_y = e_ref[base + 8 + z + 1] if z < 7 else zero
            b_x = (ahead(e_z, 1) - e_z) - (up_y - e_y)
            b_y = (up_x - e_x) - (ahead(e_z, 0) - e_z)
            b_z = (ahead(e_y, 0) - e_y) - (ahead(e_x, 1) - e_x)
            c_x = (b_z - behind(b_z, 1)) - (b_y - b_y_old)
            c_y = (b_x - b_x_old) - (b_z - behind(b_z, 0))
            c_z = (b_y - behind(b_y, 0)) - (b_x - behind(b_x, 1))
            for c, value in enumerate((c_x, c_y, c_z)):
                at = c * 8 + z
                value = value + sign * (m_ref[at] * e_ref[other + at])
                out_ref[base + at] = jnp.where(mask, value, 0.0)
            b_x_old, b_y_old = b_x, b_y
        return carry

    lax.fori_loop(0, 4, body, 0)


def brick(ref):
    return lambda s, j: ref[s * ROWS + j, 0:8, 0:128]


def pick_layer(values, z):
    want = lax.rem(lax.axis_index("tx") - z // 2 + LOCAL, LOCAL)
    result = values[0]
    for d in range(1, LOCAL):
        result = jnp.where(want == d, values[d], result)
    return result


def gram_kernel(size_x, size_y, src_ref, *refs):
    blocks, out_ref, field_ref, rows_ref = refs[:4], refs[4], refs[5], refs[6]
    x_pos = lax.axis_index("gx") * 8 + iota((8, 128), 0)
    y_pos = lax.axis_index("gy") * 128 + iota((8, 128), 1)
    for z in range(8):
        prim = [
            primary_field(src_ref[s], z, x_pos, y_pos, size_x, size_y) for s in range(2)
        ]
        for c in range(3):
            m = pick_layer([b[192 + 2 * c + z % 2].astype(F32) for b in blocks], z)
            for s in range(2):
                real = (m - 1.0) * WEIGHTS[c] * prim[s]
                field_ref[c * 8 + z, s * 8 : s * 8 + 8] = real
                field_ref[24 + c * 8 + z, s * 8 : s * 8 + 8] = 0.5 * real

    def body(j, carry):
        columns = pl.ds(pl.multiple_of(j * 128, 128), 128)
        for pair in range(VECS // 2):
            d, kl = pair // 2, 2 * (pair % 2)
            both = [vector_row(blocks, d, kl + i, j) for i in range(2)]
            rows_ref[16 * pair : 16 * pair + 16, columns] = jnp.concatenate(both).astype(BF16)
        rest = field_ref[j]
        for piece in range(3):
            part = rest.astype(BF16)
            rest = rest - part.astype(F32)
            first = 8 * VECS + 16 * piece
            rows_ref[first : first + 16, columns] = part
        return carry

    lax.fori_loop(0, ROWS, body, 0)
    full = nt_dot(rows_ref[0:128], rows_ref[...])
    row, lane = iota((128, 128), 0), iota((128, 128), 1)
    gram = jnp.where(row % 8 == lane % 8, full[:, 0:128], 0.0).reshape(VECS, 8, 128)
    gram = jnp.sum(gram, axis=1)
    gram = full_dot(gram, jnp.where(row // 8 == lane % 16, 1.0, 0.0).astype(F32))
    gram = jnp.where(iota((VECS, 128), 1) // 16 == iota((VECS, 128), 0) % 8, gram, 0.0)
    gram = jnp.sum(gram.reshape(2, 8, 128), axis=1)
    inner = full[:, 128:144] + full[:, 144:160] + full[:, 160:176]
    inner = jnp.where(iota((128, 16), 0) % 8 == iota((128, 16), 1) % 8, inner, 0.0)
    inner = jnp.sum(inner.reshape(VECS, 8, 16), axis=1)
    lines = []
    for s in range(2):
        chosen = jnp.where(iota((8, 16), 1) // 8 == s, 1.0, 0.0).astype(F32)
        lines.append(nt_dot(chosen, inner, HIGH)[0:1])
    line = jnp.concatenate(lines + [jnp.zeros((1, 96), F32)], axis=1)
    rows = jnp.concatenate([gram, line, jnp.zeros((1, 128), F32)], axis=0)
    out_ref[...] = jnp.broadcast_to(rows[None], out_ref.shape)


def invert(rows):
    lane, row = iota((VECS, 128), 1), iota((VECS, 128), 0)
    wide = jnp.where(row < 8, rows[0:1], rows[1:2])
    wide = jnp.where(lane // 16 == row % 8, wide, 0.0)
    fold = jnp.where(iota((128, 128), 0) % 16 == iota((128, 128), 1), 1.0, 0.0).astype(F32)
    work = full_dot(wide, fold) + jnp.where(lane == row + VECS, 1.0, 0.0)
    for j in range(VECS):
        pivot = work[j : j + 1] / work[j : j + 1, j : j + 1]
        work = jnp.where(row == j, pivot, work - work[:, j : j + 1] * pivot)
    return pltpu.roll(work, 128 - VECS, 1)


def begin_kernel(size_x, size_y, src_ref, got_ref, *refs):
    blocks, packed, ln_ref, hp_ref = refs[:4], refs[4], refs[5], refs[6]
    r_ref, q_ref, m_ref, inv_ref, state_ref, out_ref, side_ref, sums_ref = refs[7:]
    total = jnp.sum(got_ref[...], axis=0)
    inverse = invert(total[0:2])
    inv_ref[...] = inverse
    inner = total[2:3]
    x_pos, y_pos, mask = grid_mask(size_x, size_y)
    start = [solve(inverse, inner, s * VECS) for s in range(2)]
    lane = iota((VECS, 128), 1)
    state_ref[...] = jnp.where(lane == 2, start[0], jnp.where(lane == 3, start[1], 0.0))
    coeffs = [[spread(-start[s][k : k + 1]) for k in range(VECS)] for s in range(2)]

    def put(rows, columns):
        def store(s, j, value):
            r_ref[s * ROWS + j, rows, columns] = value

        return store

    combine_ext(
        coeffs, blocks, packed, ln_ref, hp_ref,
        put(slice(0, 8), slice(0, 128)), put(slice(8, 16), slice(0, 128)), side_ref,
    )
    top = iota((8, 128), 0) < 4
    from_next = iota((8, 128), 1) % 8 < 4
    pick = pick_matrix(F32)
    sides = []
    for d in range(LOCAL):
        at = 4 * HALF + d * PACKED + 12
        near = packed[owner(d), :, 12 * 128 : 13 * 128].astype(F32)
        far = jnp.where(from_next, ln_ref[at].astype(F32), hp_ref[at].astype(F32))
        near = full_dot(jnp.transpose(near), pick)[:48].reshape(6, 8, 128)
        far = full_dot(jnp.transpose(far), pick)[:48].reshape(6, 8, 128)
        sides.append((near, far))
    for c in range(3):
        for z in range(8):
            at = 2 * c + z % 2
            quarters = []
            for d in range(LOCAL):
                inner_m = blocks[d][192 + at].astype(F32)
                row = d * HALF + 96 + at % 3
                after, before = ln_ref[row].astype(F32), hp_ref[row].astype(F32)
                if at < 3:
                    edge = jnp.where(top, after, before)
                else:
                    edge = pltpu.roll(jnp.where(top, before, after), 4, 0)
                left = jnp.concatenate([inner_m, edge], axis=0)
                right = jnp.concatenate([sides[d][0][at], sides[d][1][at]], axis=0)
                quarters.append(jnp.concatenate([left, right], axis=1))
            m_ref[c * 8 + z] = pick_layer(quarters, z)

    for s in range(2):

        def body(z, carry, s=s):
            prim = primary_field(src_ref[s], z, x_pos, y_pos, size_x, size_y)
            for c in range(3):
                at = c * 8 + z
                real = jnp.where(mask, (m_ref[at] - 1.0) * WEIGHTS[c] * prim, 0.0)
                for p in range(2):
                    place = s * ROWS + p * 24 + at
                    value = real if p == 0 else 0.5 * real
                    r_ref[place, :, 0:128] = r_ref[place, :, 0:128] + value[:, 0:128]
                    r_ref[place, :, 128:256] = side_ref[place] + value[:, 128:256]
            return carry

        lax.fori_loop(0, 8, body, 0)
    apply_operator(r_ref, m_ref, q_ref, mask)
    finish_first(blocks, r_ref, q_ref, sums_ref, out_ref)


def finish_first(blocks, r_ref, q_ref, sums_ref, out_ref):
    sums_ref[...] = jnp.zeros_like(sums_ref)
    r, q = brick(r_ref), brick(q_ref)
    inner_all(blocks, q, sums_ref)
    inner_pairs([(r, r), (r, q)], sums_ref, 32)
    out_ref[...] = jnp.broadcast_to(row_of_sums(sums_ref), out_ref.shape)


def first_kernel(size_x, size_y, got_ref, *refs):
    blocks, packed, ln_ref, hp_ref = refs[:4], refs[4], refs[5], refs[6]
    r_ref, q_ref, m_ref, inv_ref, old_ref = refs[7:12]
    u_ref, a_ref, state_ref, out_ref, side_ref, sums_ref = refs[12:]
    row = jnp.sum(got_ref[...], axis=0, keepdims=True)
    _, _, mask = grid_mask(size_x, size_y)
    lane = iota((VECS, 128), 1)
    state = old_ref[...]
    coeffs, q_scale, r_scale = [], [], []
    for s in range(2):
        rr, rq = entry(row, 32 + 2 * s), entry(row, 33 + 2 * s)
        beta = jnp.sqrt(rr + EPS)
        g_zero = solve(inv_ref[...], row, s * VECS) / beta
        h_00 = rq / (beta * beta)
        coeffs.append([spread(-g_zero[k : k + 1]) for k in range(VECS)])
        q_scale.append(spread(1.0 / beta))
        r_scale.append(spread(-h_00 / beta))
        state = jnp.where(lane == s, g_zero, state)
        state = jnp.where(lane == 8 + s, beta, state)
        state = jnp.where(lane == 10 + s, h_00, state)
        state = jnp.where(lane == 12 + s, rr, state)
    state_ref[...] = state

    def put(rows, columns):
        def store(s, j, value):
            at = s * ROWS + j
            value = value + q_scale[s] * q_ref[at, rows, columns]
            u_ref[at, rows, columns] = value + r_scale[s] * r_ref[at, rows, columns]

        return store

    combine_ext(
        coeffs, blocks, packed, ln_ref, hp_ref,
        put(slice(0, 8), slice(0, 128)), put(slice(8, 16), slice(0, 128)), side_ref,
    )
    for s in range(2):

        def body(j, carry, s=s):
            at = s * ROWS + j
            value = side_ref[at]
            for half in range(2):
                rows = slice(half * 8, half * 8 + 8)
                new = value[rows] + q_scale[s] * q_ref[at, rows, 128:256]
                u_ref[at, rows, 128:256] = new + r_scale[s] * r_ref[at, rows, 128:256]
            return carry

        lax.fori_loop(0, ROWS, body, 0)
    apply_operator(u_ref, m_ref, a_ref, mask)
    sums_ref[...] = jnp.zeros_like(sums_ref)
    r, u, a = brick(r_ref), brick(u_ref), brick(a_ref)
    inner_all(blocks, a, sums_ref)
    inner_pairs([(u, u), (r, u), (r, a), (u, a), (a, a)], sums_ref, 32)
    out_ref[...] = jnp.broadcast_to(row_of_sums(sums_ref), out_ref.shape)


def close_cycle(row, inverse, state, s):
    uu, ru, ra, ua, aa = [entry(row, 32 + 5 * s + i) for i in range(5)]
    g_zero = state[:, s : s + 1]
    beta, h_00, rr = [state[0:1, first + s : first + s + 1] for first in (8, 10, 12)]
    h_10 = jnp.sqrt(uu + EPS)
    inner = column_of(row, s * VECS) / h_10
    g_one = solve(inverse, row, s * VECS) / h_10
    h_01 = ra / (beta * h_10)
    h_11 = ua / (h_10 * h_10)
    left = aa / (h_10 * h_10) - jnp.sum(g_one * inner, axis=0, keepdims=True)
    left = left - 2.0 * (h_01 * h_01 + h_11 * h_11)
    left = left + h_01 * h_01 * (rr / (beta * beta)) + h_11 * h_11 * (uu / (h_10 * h_10))
    left = left + 2.0 * h_01 * h_11 * (ru / (beta * h_10))
    h_21_square = jnp.maximum(left, 0.0) + EPS
    n_00 = h_00 * h_00 + h_10 * h_10
    n_01 = h_00 * h_01 + h_10 * h_11
    n_11 = h_01 * h_01 + h_11 * h_11 + h_21_square
    l_00 = jnp.sqrt(n_00)
    l_10 = n_01 / l_00
    l_11 = jnp.sqrt(n_11 - l_10 * l_10)
    z_0 = beta * h_00 / l_00
    z_1 = (beta * h_01 - l_10 * z_0) / l_11
    y_1 = z_1 / l_11
    y_0 = (z_0 - l_10 * y_1) / l_00
    t_0 = beta - h_00 * y_0 - h_01 * y_1
    t_1 = -h_10 * y_0 - h_11 * y_1
    return {
        "r": (t_0 + y_1 * h_01) / beta,
        "u": (t_1 + y_1 * h_11) / h_10,
        "a": -y_1 / h_10,
        "c": y_1 * g_one,
        "sol_r": y_0 / beta,
        "sol_u": y_1 / h_10,
        "basis": state[:, 2 + s : 3 + s] - g_zero * y_0 - g_one * y_1,
    }


def next_kernel(size_x, size_y, got_ref, *refs):
    blocks, packed, ln_ref, hp_ref = refs[:4], refs[4], refs[5], refs[6]
    r_ref, u_ref, a_ref, m_ref, inv_ref, old_ref = refs[7:13]
    new_ref, q_ref, sol_ref, state_ref, out_ref, side_ref, sums_ref = refs[13:]
    row = jnp.sum(got_ref[...], axis=0, keepdims=True)
    _, _, mask = grid_mask(size_x, size_y)
    state = old_ref[...]
    small = [close_cycle(row, inv_ref[...], state, s) for s in range(2)]
    lane = iota((VECS, 128), 1)
    state_ref[...] = jnp.where(
        lane == 2, small[0]["basis"], jnp.where(lane == 3, small[1]["basis"], 0.0)
    )
    coeffs = [[spread(small[s]["c"][k : k + 1]) for k in range(VECS)] for s in range(2)]
    scale = [{name: spread(small[s][name]) for name in ("r", "u", "a", "sol_r", "sol_u")} for s in range(2)]

    def total(s, at, rows, columns, value):
        value = value + scale[s]["r"] * r_ref[at, rows, columns]
        value = value + scale[s]["u"] * u_ref[at, rows, columns]
        return value + scale[s]["a"] * a_ref[at, rows, columns]

    def put(rows, columns):
        def store(s, j, value):
            at = s * ROWS + j
            new_ref[at, rows, columns] = total(s, at, rows, columns, value)

        return store

    combine_ext(
        coeffs, blocks, packed, ln_ref, hp_ref,
        put(slice(0, 8), slice(0, 128)), put(slice(8, 16), slice(0, 128)), side_ref,
    )
    for s in range(2):

        def body(j, carry, s=s):
            at = s * ROWS + j
            value = side_ref[at]
            for half in range(2):
                rows = slice(half * 8, half * 8 + 8)
                new_ref[at, rows, 128:256] = total(s, at, rows, slice(128, 256), value[rows])
            sol_ref[at] = (
                scale[s]["sol_r"] * r_ref[at, 0:8, 0:128]
                + scale[s]["sol_u"] * u_ref[at, 0:8, 0:128]
            )
            return carry

        lax.fori_loop(0, ROWS, body, 0)
    apply_operator(new_ref, m_ref, q_ref, mask)
    finish_first(blocks, new_ref, q_ref, sums_ref, out_ref)


def last_kernel(got_ref, *refs):
    blocks, basis = refs[:4], refs[4]
    r_ref, u_ref, a_ref, inv_ref, old_ref, sol_ref = refs[5:11]
    solution_ref, residual_ref = refs[11:]
    row = jnp.sum(got_ref[...], axis=0, keepdims=True)
    state = old_ref[...]
    for s in range(2):
        small = close_cycle(row, inv_ref[...], state, s)
        coeffs = [spread(small["c"][k : k + 1]) for k in range(VECS)]
        base_coeffs = [spread(small["basis"][k : k + 1]) for k in range(VECS)]
        scale = {name: spread(small[name]) for name in ("r", "u", "a", "sol_r", "sol_u")}

        def body(j, carry, s=s, coeffs=coeffs, base_coeffs=base_coeffs, scale=scale):
            at = s * ROWS + j
            r, u, a = brick(r_ref)(s, j), brick(u_ref)(s, j), brick(a_ref)(s, j)
            value = scale["r"] * r + scale["u"] * u + scale["a"] * a
            field = sol_ref[at] + scale["sol_r"] * r + scale["sol_u"] * u
            for d in range(LOCAL):
                for kl in range(LOCAL):
                    k = d * LOCAL + kl
                    value = value + coeffs[k] * vector_row(blocks, d, kl, j)
                    field = field + base_coeffs[k] * basis[
                        (owner(d) * LOCAL + kl) * ROWS + j
                    ].astype(F32)
            residual_ref[at] = value
            solution_ref[at] = field
            return carry

        lax.fori_loop(0, ROWS, body, 0)


def call(kernel, outs, args, scratch=(), smem=0):
    vmem = pl.BlockSpec(memory_space=pltpu.VMEM)
    return pl.pallas_call(
        kernel,
        out_shape=outs,
        in_specs=[pl.BlockSpec(memory_space=pltpu.SMEM)] * smem + [vmem] * (len(args) - smem),
        out_specs=jax.tree.map(lambda _: vmem, outs),
        scratch_shapes=list(scratch),
        compiler_params=pltpu.CompilerParams(vmem_limit_bytes=20 * 1024 * 1024),
    )(*args)


def shape(*dims, dtype=F32):
    return jax.ShapeDtypeStruct(dims, dtype)


def exchange(value):
    return lax.all_to_all(value, ("gx", "gy"), 0, 0)


def around(value, axis):
    up = [(i, i + 1) for i in range(lax.axis_size(axis) - 1)]
    return value, up, [(j, i) for i, j in up]


def gather(value):
    return [value] + [
        lax.ppermute(value, "tx", [(i, (i + d) % LOCAL) for i in range(LOCAL)])
        for d in range(1, LOCAL)
    ]


def on_device(src_cell, basis, images, induction):
    size_x, size_y = 8 * lax.axis_size("gx"), 128 * lax.axis_size("gy")
    peers = lax.axis_size("gx") * lax.axis_size("gy")
    block = jnp.concatenate(
        [images.reshape(LOCAL * ROWS, 8, 128), induction.reshape(6, 8, 128)], axis=0
    )
    blocks = gather(block)
    own = call(pack_y_kernel, shape(8, PACKED * 128, dtype=BF16), (block,))
    _, up, down = around(own, "gy")
    after, before = lax.ppermute(own, "gy", down), lax.ppermute(own, "gy", up)
    side = jnp.where(lax.broadcasted_iota(jnp.int32, own.shape, 0) < 4, after, before)
    packed = lax.all_to_all(jnp.broadcast_to(side, (LOCAL, *side.shape)), "tx", 0, 0)

    half = shape(LOCAL * (HALF + PACKED), 8, 128, dtype=BF16)
    low, high = call(pack_x_kernel, (half, half), (*blocks, packed))
    low, high, own_basis = lax.optimization_barrier(
        (low, high, basis.reshape(LOCAL * ROWS, 8, 128))
    )
    bases = lax.all_gather(own_basis, "tx", tiled=True)
    _, up, down = around(low, "gx")
    ln, hp = lax.ppermute(low, "gx", down), lax.ppermute(high, "gx", up)

    sums = pltpu.VMEM((128, 128), F32)
    side_scratch = pltpu.VMEM((2 * ROWS, 16, 128), F32)
    sent = call(
        functools.partial(gram_kernel, size_x, size_y),
        shape(peers, 4, 128),
        (src_cell, *blocks),
        (pltpu.VMEM((ROWS, 16, 128), F32), pltpu.VMEM((8 * VECS + 48, ROWS * 128), BF16)),
        smem=1,
    )
    got = exchange(sent)
    wide = shape(2 * ROWS, 16, 256)
    line = shape(peers, 128)
    small = shape(VECS, 128)
    static = (*blocks, packed, ln, hp)
    r, q, m, inverse, state, sent = call(
        functools.partial(begin_kernel, size_x, size_y),
        (wide, wide, shape(24, 16, 256), small, small, line),
        (src_cell, got, *static),
        (side_scratch, sums),
        smem=1,
    )

    def total(value):
        return exchange(value.reshape(peers, 1, 128)).reshape(peers, 128)

    def first(r, q, state, sent):
        return call(
            functools.partial(first_kernel, size_x, size_y),
            (wide, wide, small, line),
            (total(sent), *static, r, q, m, inverse, state),
            (side_scratch, sums),
        )

    u, a, state, sent = first(r, q, state, sent)
    r, q, field, state, sent = call(
        functools.partial(next_kernel, size_x, size_y),
        (wide, wide, shape(2 * ROWS, 8, 128), small, line),
        (total(sent), *static, r, u, a, m, inverse, state),
        (side_scratch, sums),
    )
    u, a, state, sent = first(r, q, state, sent)
    narrow = shape(2 * ROWS, 8, 128)
    field, residual = call(
        last_kernel,
        (narrow, narrow),
        (total(sent), *blocks, bases, r, u, a, inverse, state, field),
    )
    full = (2, 2, 3, 8, 8, 128)
    return field.reshape(full), residual.reshape(full)


def solution(mesh):
    in_specs = (
        P("tx"),
        P("tx", None, None, None, "gx", "gy"),
        P("tx", None, None, None, "gx", "gy"),
        P(None, "tx", "gx", "gy"),
    )
    out_specs = (P("tx", None, None, None, "gx", "gy"), P("tx", None, None, None, "gx", "gy"))
    return jax.shard_map(
        on_device, mesh=mesh, in_specs=in_specs, out_specs=out_specs, check_vma=False
    )
```

```python
import functools

import jax
import jax.numpy as jnp
from jax import lax
from jax.experimental import pallas as pl
from jax.experimental.pallas import tpu as pltpu
from jax.sharding import PartitionSpec as P

EPS = 1e-06
VECS = 16
LOCAL = 4
ROWS = 48
BLOCK = 198
HALF = 99
PACKED = 13
WEIGHTS = (1.0, 0.5, 0.25)
HIGH = lax.Precision.HIGHEST
F32 = jnp.float32
BF16 = jnp.bfloat16


def iota(shape, axis):
    return lax.broadcasted_iota(jnp.int32, shape, axis)


def pick_matrix(dtype):
    col = iota((8, 128), 0)
    lane = iota((8, 128), 1)
    return jnp.where(lane == jnp.where(col < 4, col, col + 120), 1.0, 0.0).astype(dtype)


def nt_dot(left, right, precision=None):
    return lax.dot_general(
        left, right, (((1,), (1,)), ((), ())), precision=precision, preferred_element_type=F32
    )


def full_dot(left, right):
    return lax.dot_general(
        left, right, (((1,), (0,)), ((), ())), precision=HIGH, preferred_element_type=F32
    )


BLOCKS = 7
CUT = 2 * ROWS


def vector_row(blocks, d, kl, j):
    row = kl * ROWS + j
    if d != 2:
        return blocks[(0, 1, None, 2)[d]][row].astype(F32)
    return blocks[3][row].astype(F32) if kl < 2 else blocks[4][row - CUT].astype(F32)


def induction_row(blocks, d, at):
    if d != 2:
        return blocks[(0, 1, None, 2)[d]][LOCAL * ROWS + at].astype(F32)
    return blocks[4][LOCAL * ROWS - CUT + at].astype(F32)


def side_tile(blocks, d, tile):
    ref, first = ((5, 0), (3, CUT), (6, 0), (4, BLOCK - CUT))[d]
    return blocks[ref][first + tile]


def pack_y_kernel(block_ref, out_ref):
    pick = pick_matrix(BF16)
    for tile in range(PACKED):
        first = tile * 16
        count = min(16, BLOCK - first)
        rows = block_ref[first : first + count].astype(F32).reshape(count * 8, 128).astype(BF16)
        picked = nt_dot(pick, rows)
        if count < 16:
            picked = jnp.concatenate([picked, jnp.zeros((8, 128 - count * 8), F32)], axis=1)
        out_ref[tile] = picked.astype(BF16)


def pack_x_kernel(*refs):
    blocks, lo_ref, hi_ref = refs[:BLOCKS], refs[BLOCKS], refs[BLOCKS + 1]
    top = iota((8, 128), 0) < 4

    def pair(one, two, at):
        two = pltpu.roll(two, 4, 0)
        lo_ref[at] = jnp.where(top, one, two).astype(BF16)
        hi_ref[at] = jnp.where(top, two, one).astype(BF16)

    def body(j, carry):
        for d in range(LOCAL):
            for kl in range(2):
                pair(
                    vector_row(blocks, d, kl, j),
                    vector_row(blocks, d, kl + 2, j),
                    d * HALF + kl * ROWS + j,
                )
        return carry

    lax.fori_loop(0, ROWS, body, 0)
    for d in range(LOCAL):
        for i in range(3):
            pair(
                induction_row(blocks, d, i),
                induction_row(blocks, d, i + 3),
                d * HALF + CUT + i,
            )
        for tile in range(PACKED):
            piece = side_tile(blocks, d, tile)
            lo_ref[LOCAL * HALF + d * PACKED + tile] = piece
            hi_ref[LOCAL * HALF + d * PACKED + tile] = piece


def inner_all(blocks, field, sums_ref):
    def body(j, accs):
        one, two = field(0, j), field(1, j)
        new = []
        for d in range(LOCAL):
            for kl in range(LOCAL):
                vec = vector_row(blocks, d, kl, j)
                at = 2 * (d * LOCAL + kl)
                new.append(accs[at] + vec * one)
                new.append(accs[at + 1] + vec * two)
        return tuple(new)

    zero = jnp.zeros((8, 128), F32)
    accs = lax.fori_loop(0, ROWS, body, (zero,) * (2 * VECS))
    for k in range(VECS):
        for s in range(2):
            sums_ref[s * VECS + k : s * VECS + k + 1] = jnp.sum(
                accs[2 * k + s], axis=0, keepdims=True
            )


def inner_pairs(pairs, sums_ref, first):
    count = len(pairs)
    for s in range(2):

        def body(j, accs, s=s):
            return tuple(
                acc + one(s, j) * two(s, j) for acc, (one, two) in zip(accs, pairs)
            )

        zero = jnp.zeros((8, 128), F32)
        accs = lax.fori_loop(0, ROWS, body, (zero,) * count)
        for i in range(count):
            at = first + s * count + i
            sums_ref[at : at + 1] = jnp.sum(accs[i], axis=0, keepdims=True)


def row_of_sums(sums_ref):
    return nt_dot(jnp.ones((8, 128), F32), sums_ref[...], HIGH)[0:1]


def entry(row, lane):
    return row[:, lane : lane + 1]


def column_of(row, first):
    part = row[:, first : first + VECS]
    eye = iota((VECS, VECS), 0) == iota((VECS, VECS), 1)
    return jnp.sum(jnp.where(eye, part, 0.0), axis=1, keepdims=True)


def solve(inverse, row, first):
    return jnp.sum(inverse[:, :VECS] * row[:, first : first + VECS], axis=1, keepdims=True)


def spread(value):
    return jnp.broadcast_to(value, (8, 128))


def grid_mask(size_x, size_y):
    row, lane = iota((16, 256), 0), iota((16, 256), 1)
    x_pos = lax.axis_index("gx") * 8 + jnp.where(row < 12, row, row - 16)
    y_pos = lax.axis_index("gy") * 128 + jnp.where(lane < 132, lane, lane - 256)
    inside = (x_pos >= 0) & (x_pos < size_x) & (y_pos >= 0) & (y_pos < size_y)
    inside = inside & ((lane < 132) | (lane >= 252))
    return x_pos, y_pos, inside


def primary_field(cell, z, x_pos, y_pos, size_x, size_y):
    plane = size_x * size_y
    src_z = cell // plane
    rest = cell % plane
    d_z = (z - src_z).astype(F32)
    d_x = (x_pos - rest // size_y).astype(F32)
    d_y = (y_pos - rest % size_y).astype(F32)
    dist = jnp.sqrt(d_z * d_z + d_x * d_x + d_y * d_y)
    return jnp.exp(-dist / ((size_x + size_y) / 8.0))


def combine_ext(coeffs, blocks, ln_ref, hp_ref, interior, halo_x, unpacked_ref):
    top = iota((8, 128), 0) < 4

    def body(j, carry):
        inner = [jnp.zeros((8, 128), F32)] * 2
        straight = [jnp.zeros((8, 128), F32)] * 2
        rolled = [jnp.zeros((8, 128), F32)] * 2
        for d in range(LOCAL):
            for kl in range(LOCAL):
                k = d * LOCAL + kl
                vec = vector_row(blocks, d, kl, j)
                at = d * HALF + (kl % 2) * ROWS + j
                after, before = ln_ref[at].astype(F32), hp_ref[at].astype(F32)
                outer = straight if kl < 2 else rolled
                edge = jnp.where(top, after, before) if kl < 2 else jnp.where(top, before, after)
                for s in range(2):
                    inner[s] = inner[s] + coeffs[s][k] * vec
                    outer[s] = outer[s] + coeffs[s][k] * edge
        for s in range(2):
            interior(s, j, inner[s])
            halo_x(s, j, straight[s] + pltpu.roll(rolled[s], 4, 0))
        return carry

    lax.fori_loop(0, ROWS, body, 0)
    pick = pick_matrix(F32)
    from_next = iota((8, 128), 1) % 8 < 4
    for s in range(2):
        for tile in range(3):
            near = jnp.zeros((8, 128), F32)
            far = jnp.zeros((8, 128), F32)
            for d in range(LOCAL):
                for kl in range(LOCAL):
                    k = d * LOCAL + kl
                    t = kl * 3 + tile
                    at = 4 * HALF + d * PACKED + t
                    near = near + coeffs[s][k] * side_tile(blocks, d, t).astype(F32)
                    edge = jnp.where(from_next, ln_ref[at].astype(F32), hp_ref[at].astype(F32))
                    far = far + coeffs[s][k] * edge
            place = s * ROWS + tile * 16
            near = full_dot(jnp.transpose(near), pick).reshape(16, 8, 128)
            far = full_dot(jnp.transpose(far), pick).reshape(16, 8, 128)
            unpacked_ref[place : place + 16, 0:8] = near
            unpacked_ref[place : place + 16, 8:16] = far


def apply_operator(e_ref, m_ref, out_ref, mask):
    def ahead(f, axis):
        return pltpu.roll(f, f.shape[axis] - 1, axis)

    def behind(f, axis):
        return pltpu.roll(f, 1, axis)

    def body(index, carry):
        base = index * 24
        other = jnp.where(index % 2 == 0, base + 24, base - 24)
        sign = jnp.where(index % 2 == 0, -1.0, 1.0).astype(F32)
        zero = jnp.zeros((16, 256), F32)
        b_x_old = -e_ref[base + 8]
        b_y_old = e_ref[base]
        for z in range(8):
            e_x, e_y, e_z = e_ref[base + z], e_ref[base + 8 + z], e_ref[base + 16 + z]
            up_x = e_ref[base + z + 1] if z < 7 else zero
            up_y = e_ref[base + 8 + z + 1] if z < 7 else zero
            b_x = (ahead(e_z, 1) - e_z) - (up_y - e_y)
            b_y = (up_x - e_x) - (ahead(e_z, 0) - e_z)
            b_z = (ahead(e_y, 0) - e_y) - (ahead(e_x, 1) - e_x)
            c_x = (b_z - behind(b_z, 1)) - (b_y - b_y_old)
            c_y = (b_x - b_x_old) - (b_z - behind(b_z, 0))
            c_z = (b_y - behind(b_y, 0)) - (b_x - behind(b_x, 1))
            for c, value in enumerate((c_x, c_y, c_z)):
                at = c * 8 + z
                value = value + sign * (m_ref[at] * e_ref[other + at])
                out_ref[base + at] = jnp.where(mask, value, 0.0)
            b_x_old, b_y_old = b_x, b_y
        return carry

    lax.fori_loop(0, 4, body, 0)


def brick(ref):
    return lambda s, j: ref[s * ROWS + j, 0:8, 0:128]


def pick_layer(values, z):
    want = lax.rem(lax.axis_index("tx") - z // 2 + LOCAL, LOCAL)
    result = values[0]
    for d in range(1, LOCAL):
        result = jnp.where(want == d, values[d], result)
    return result


def gram_kernel(size_x, size_y, src_ref, *refs):
    blocks, out_ref, field_ref, rows_ref = refs[:BLOCKS], *refs[BLOCKS:]
    x_pos = lax.axis_index("gx") * 8 + iota((8, 128), 0)
    y_pos = lax.axis_index("gy") * 128 + iota((8, 128), 1)
    for z in range(8):
        prim = [
            primary_field(src_ref[s], z, x_pos, y_pos, size_x, size_y) for s in range(2)
        ]
        for c in range(3):
            m = pick_layer([induction_row(blocks, d, 2 * c + z % 2) for d in range(LOCAL)], z)
            for s in range(2):
                real = (m - 1.0) * WEIGHTS[c] * prim[s]
                field_ref[c * 8 + z, s * 8 : s * 8 + 8] = real
                field_ref[24 + c * 8 + z, s * 8 : s * 8 + 8] = 0.5 * real

    def body(j, carry):
        columns = pl.ds(pl.multiple_of(j * 128, 128), 128)
        for pair in range(VECS // 2):
            d, kl = pair // 2, 2 * (pair % 2)
            both = [vector_row(blocks, d, kl + i, j) for i in range(2)]
            rows_ref[16 * pair : 16 * pair + 16, columns] = jnp.concatenate(both).astype(BF16)
        rest = field_ref[j]
        for piece in range(3):
            part = rest.astype(BF16)
            rest = rest - part.astype(F32)
            first = 8 * VECS + 16 * piece
            rows_ref[first : first + 16, columns] = part
        return carry

    lax.fori_loop(0, ROWS, body, 0)
    full = nt_dot(rows_ref[0:128], rows_ref[...])
    row, lane = iota((128, 128), 0), iota((128, 128), 1)
    gram = jnp.where(row % 8 == lane % 8, full[:, 0:128], 0.0).reshape(VECS, 8, 128)
    gram = jnp.sum(gram, axis=1)
    gram = full_dot(gram, jnp.where(row // 8 == lane % 16, 1.0, 0.0).astype(F32))
    gram = jnp.where(iota((VECS, 128), 1) // 16 == iota((VECS, 128), 0) % 8, gram, 0.0)
    gram = jnp.sum(gram.reshape(2, 8, 128), axis=1)
    inner = full[:, 128:144] + full[:, 144:160] + full[:, 160:176]
    inner = jnp.where(iota((128, 16), 0) % 8 == iota((128, 16), 1) % 8, inner, 0.0)
    inner = jnp.sum(inner.reshape(VECS, 8, 16), axis=1)
    lines = []
    for s in range(2):
        chosen = jnp.where(iota((8, 16), 1) // 8 == s, 1.0, 0.0).astype(F32)
        lines.append(nt_dot(chosen, inner, HIGH)[0:1])
    line = jnp.concatenate(lines + [jnp.zeros((1, 96), F32)], axis=1)
    rows = jnp.concatenate([gram, line, jnp.zeros((1, 128), F32)], axis=0)
    out_ref[...] = jnp.broadcast_to(rows[None], out_ref.shape)


def invert(rows):
    lane, row = iota((VECS, 128), 1), iota((VECS, 128), 0)
    wide = jnp.where(row < 8, rows[0:1], rows[1:2])
    wide = jnp.where(lane // 16 == row % 8, wide, 0.0)
    fold = jnp.where(iota((128, 128), 0) % 16 == iota((128, 128), 1), 1.0, 0.0).astype(F32)
    work = full_dot(wide, fold) + jnp.where(lane == row + VECS, 1.0, 0.0)
    for j in range(VECS):
        pivot = work[j : j + 1] / work[j : j + 1, j : j + 1]
        work = jnp.where(row == j, pivot, work - work[:, j : j + 1] * pivot)
    return pltpu.roll(work, 128 - VECS, 1)


def begin_kernel(size_x, size_y, src_ref, got_ref, *refs):
    blocks, ln_ref, hp_ref = refs[:BLOCKS], refs[BLOCKS], refs[BLOCKS + 1]
    refs = refs[BLOCKS + 2 :]
    r_ref, q_ref, m_ref, inv_ref, state_ref, out_ref, side_ref, sums_ref = refs
    total = jnp.sum(got_ref[...], axis=0)
    inverse = invert(total[0:2])
    inv_ref[...] = inverse
    inner = total[2:3]
    x_pos, y_pos, mask = grid_mask(size_x, size_y)
    start = [solve(inverse, inner, s * VECS) for s in range(2)]
    lane = iota((VECS, 128), 1)
    state_ref[...] = jnp.where(lane == 2, start[0], jnp.where(lane == 3, start[1], 0.0))
    coeffs = [[spread(-start[s][k : k + 1]) for k in range(VECS)] for s in range(2)]

    def put(rows, columns):
        def store(s, j, value):
            r_ref[s * ROWS + j, rows, columns] = value

        return store

    combine_ext(
        coeffs, blocks, ln_ref, hp_ref,
        put(slice(0, 8), slice(0, 128)), put(slice(8, 16), slice(0, 128)), side_ref,
    )
    top = iota((8, 128), 0) < 4
    from_next = iota((8, 128), 1) % 8 < 4
    pick = pick_matrix(F32)
    sides = []
    for d in range(LOCAL):
        at = 4 * HALF + d * PACKED + 12
        near = side_tile(blocks, d, 12).astype(F32)
        far = jnp.where(from_next, ln_ref[at].astype(F32), hp_ref[at].astype(F32))
        near = full_dot(jnp.transpose(near), pick)[:48].reshape(6, 8, 128)
        far = full_dot(jnp.transpose(far), pick)[:48].reshape(6, 8, 128)
        sides.append((near, far))
    for c in range(3):
        for z in range(8):
            at = 2 * c + z % 2
            quarters = []
            for d in range(LOCAL):
                inner_m = induction_row(blocks, d, at)
                row = d * HALF + 96 + at % 3
                after, before = ln_ref[row].astype(F32), hp_ref[row].astype(F32)
                if at < 3:
                    edge = jnp.where(top, after, before)
                else:
                    edge = pltpu.roll(jnp.where(top, before, after), 4, 0)
                left = jnp.concatenate([inner_m, edge], axis=0)
                right = jnp.concatenate([sides[d][0][at], sides[d][1][at]], axis=0)
                quarters.append(jnp.concatenate([left, right], axis=1))
            m_ref[c * 8 + z] = pick_layer(quarters, z)

    for s in range(2):

        def body(z, carry, s=s):
            prim = primary_field(src_ref[s], z, x_pos, y_pos, size_x, size_y)
            for c in range(3):
                at = c * 8 + z
                real = jnp.where(mask, (m_ref[at] - 1.0) * WEIGHTS[c] * prim, 0.0)
                for p in range(2):
                    place = s * ROWS + p * 24 + at
                    value = real if p == 0 else 0.5 * real
                    r_ref[place, :, 0:128] = r_ref[place, :, 0:128] + value[:, 0:128]
                    r_ref[place, :, 128:256] = side_ref[place] + value[:, 128:256]
            return carry

        lax.fori_loop(0, 8, body, 0)
    apply_operator(r_ref, m_ref, q_ref, mask)
    finish_first(blocks, r_ref, q_ref, sums_ref, out_ref)


def finish_first(blocks, r_ref, q_ref, sums_ref, out_ref):
    sums_ref[...] = jnp.zeros_like(sums_ref)
    r, q = brick(r_ref), brick(q_ref)
    inner_all(blocks, q, sums_ref)
    inner_pairs([(r, r), (r, q)], sums_ref, 32)
    out_ref[...] = jnp.broadcast_to(row_of_sums(sums_ref), out_ref.shape)


def first_kernel(size_x, size_y, got_ref, *refs):
    blocks, ln_ref, hp_ref = refs[:BLOCKS], refs[BLOCKS], refs[BLOCKS + 1]
    refs = refs[BLOCKS + 2 :]
    r_ref, q_ref, m_ref, inv_ref, old_ref = refs[:5]
    u_ref, a_ref, state_ref, out_ref, side_ref, sums_ref = refs[5:]
    row = jnp.sum(got_ref[...], axis=0, keepdims=True)
    _, _, mask = grid_mask(size_x, size_y)
    lane = iota((VECS, 128), 1)
    state = old_ref[...]
    coeffs, q_scale, r_scale = [], [], []
    for s in range(2):
        rr, rq = entry(row, 32 + 2 * s), entry(row, 33 + 2 * s)
        beta = jnp.sqrt(rr + EPS)
        g_zero = solve(inv_ref[...], row, s * VECS) / beta
        h_00 = rq / (beta * beta)
        coeffs.append([spread(-g_zero[k : k + 1]) for k in range(VECS)])
        q_scale.append(spread(1.0 / beta))
        r_scale.append(spread(-h_00 / beta))
        state = jnp.where(lane == s, g_zero, state)
        state = jnp.where(lane == 8 + s, beta, state)
        state = jnp.where(lane == 10 + s, h_00, state)
        state = jnp.where(lane == 12 + s, rr, state)
    state_ref[...] = state

    def put(rows, columns):
        def store(s, j, value):
            at = s * ROWS + j
            value = value + q_scale[s] * q_ref[at, rows, columns]
            u_ref[at, rows, columns] = value + r_scale[s] * r_ref[at, rows, columns]

        return store

    combine_ext(
        coeffs, blocks, ln_ref, hp_ref,
        put(slice(0, 8), slice(0, 128)), put(slice(8, 16), slice(0, 128)), side_ref,
    )
    for s in range(2):

        def body(j, carry, s=s):
            at = s * ROWS + j
            value = side_ref[at]
            for half in range(2):
                rows = slice(half * 8, half * 8 + 8)
                new = value[rows] + q_scale[s] * q_ref[at, rows, 128:256]
                u_ref[at, rows, 128:256] = new + r_scale[s] * r_ref[at, rows, 128:256]
            return carry

        lax.fori_loop(0, ROWS, body, 0)
    apply_operator(u_ref, m_ref, a_ref, mask)
    sums_ref[...] = jnp.zeros_like(sums_ref)
    r, u, a = brick(r_ref), brick(u_ref), brick(a_ref)
    inner_all(blocks, a, sums_ref)
    inner_pairs([(u, u), (r, u), (r, a), (u, a), (a, a)], sums_ref, 32)
    out_ref[...] = jnp.broadcast_to(row_of_sums(sums_ref), out_ref.shape)


def close_cycle(row, inverse, state, s):
    uu, ru, ra, ua, aa = [entry(row, 32 + 5 * s + i) for i in range(5)]
    g_zero = state[:, s : s + 1]
    beta, h_00, rr = [state[0:1, first + s : first + s + 1] for first in (8, 10, 12)]
    h_10 = jnp.sqrt(uu + EPS)
    inner = column_of(row, s * VECS) / h_10
    g_one = solve(inverse, row, s * VECS) / h_10
    h_01 = ra / (beta * h_10)
    h_11 = ua / (h_10 * h_10)
    left = aa / (h_10 * h_10) - jnp.sum(g_one * inner, axis=0, keepdims=True)
    left = left - 2.0 * (h_01 * h_01 + h_11 * h_11)
    left = left + h_01 * h_01 * (rr / (beta * beta)) + h_11 * h_11 * (uu / (h_10 * h_10))
    left = left + 2.0 * h_01 * h_11 * (ru / (beta * h_10))
    h_21_square = jnp.maximum(left, 0.0) + EPS
    n_00 = h_00 * h_00 + h_10 * h_10
    n_01 = h_00 * h_01 + h_10 * h_11
    n_11 = h_01 * h_01 + h_11 * h_11 + h_21_square
    l_00 = jnp.sqrt(n_00)
    l_10 = n_01 / l_00
    l_11 = jnp.sqrt(n_11 - l_10 * l_10)
    z_0 = beta * h_00 / l_00
    z_1 = (beta * h_01 - l_10 * z_0) / l_11
    y_1 = z_1 / l_11
    y_0 = (z_0 - l_10 * y_1) / l_00
    t_0 = beta - h_00 * y_0 - h_01 * y_1
    t_1 = -h_10 * y_0 - h_11 * y_1
    return {
        "r": (t_0 + y_1 * h_01) / beta,
        "u": (t_1 + y_1 * h_11) / h_10,
        "a": -y_1 / h_10,
        "c": y_1 * g_one,
        "sol_r": y_0 / beta,
        "sol_u": y_1 / h_10,
        "basis": state[:, 2 + s : 3 + s] - g_zero * y_0 - g_one * y_1,
    }


def next_kernel(size_x, size_y, got_ref, *refs):
    blocks, ln_ref, hp_ref = refs[:BLOCKS], refs[BLOCKS], refs[BLOCKS + 1]
    refs = refs[BLOCKS + 2 :]
    r_ref, u_ref, a_ref, m_ref, inv_ref, old_ref = refs[:6]
    new_ref, q_ref, sol_ref, state_ref, out_ref, side_ref, sums_ref = refs[6:]
    row = jnp.sum(got_ref[...], axis=0, keepdims=True)
    _, _, mask = grid_mask(size_x, size_y)
    state = old_ref[...]
    small = [close_cycle(row, inv_ref[...], state, s) for s in range(2)]
    lane = iota((VECS, 128), 1)
    state_ref[...] = jnp.where(
        lane == 2, small[0]["basis"], jnp.where(lane == 3, small[1]["basis"], 0.0)
    )
    coeffs = [[spread(small[s]["c"][k : k + 1]) for k in range(VECS)] for s in range(2)]
    scale = [{name: spread(small[s][name]) for name in ("r", "u", "a", "sol_r", "sol_u")} for s in range(2)]

    def total(s, at, rows, columns, value):
        value = value + scale[s]["r"] * r_ref[at, rows, columns]
        value = value + scale[s]["u"] * u_ref[at, rows, columns]
        return value + scale[s]["a"] * a_ref[at, rows, columns]

    def put(rows, columns):
        def store(s, j, value):
            at = s * ROWS + j
            new_ref[at, rows, columns] = total(s, at, rows, columns, value)

        return store

    combine_ext(
        coeffs, blocks, ln_ref, hp_ref,
        put(slice(0, 8), slice(0, 128)), put(slice(8, 16), slice(0, 128)), side_ref,
    )
    for s in range(2):

        def body(j, carry, s=s):
            at = s * ROWS + j
            value = side_ref[at]
            for half in range(2):
                rows = slice(half * 8, half * 8 + 8)
                new_ref[at, rows, 128:256] = total(s, at, rows, slice(128, 256), value[rows])
            sol_ref[at] = (
                scale[s]["sol_r"] * r_ref[at, 0:8, 0:128]
                + scale[s]["sol_u"] * u_ref[at, 0:8, 0:128]
            )
            return carry

        lax.fori_loop(0, ROWS, body, 0)
    apply_operator(new_ref, m_ref, q_ref, mask)
    finish_first(blocks, new_ref, q_ref, sums_ref, out_ref)


def basis_row(basis, d, kl, j):
    row = kl * ROWS + j
    if d == 0:
        return basis[0][row].astype(F32)
    first = {1: 1, 3: 3, 2: 5}[d]
    return basis[first][row].astype(F32) if kl < 2 else basis[first + 1][row - CUT].astype(F32)


def last_kernel(got_ref, *refs):
    blocks, basis, refs = refs[:BLOCKS], refs[BLOCKS : BLOCKS + 7], refs[BLOCKS + 7 :]
    r_ref, u_ref, a_ref, inv_ref, old_ref, sol_ref = refs[:6]
    solution_ref, residual_ref = refs[6:]
    row = jnp.sum(got_ref[...], axis=0, keepdims=True)
    state = old_ref[...]
    for s in range(2):
        small = close_cycle(row, inv_ref[...], state, s)
        coeffs = [spread(small["c"][k : k + 1]) for k in range(VECS)]
        base_coeffs = [spread(small["basis"][k : k + 1]) for k in range(VECS)]
        scale = {name: spread(small[name]) for name in ("r", "u", "a", "sol_r", "sol_u")}

        def body(j, carry, s=s, coeffs=coeffs, base_coeffs=base_coeffs, scale=scale):
            at = s * ROWS + j
            r, u, a = brick(r_ref)(s, j), brick(u_ref)(s, j), brick(a_ref)(s, j)
            value = scale["r"] * r + scale["u"] * u + scale["a"] * a
            field = sol_ref[at] + scale["sol_r"] * r + scale["sol_u"] * u
            for d in range(LOCAL):
                for kl in range(LOCAL):
                    k = d * LOCAL + kl
                    value = value + coeffs[k] * vector_row(blocks, d, kl, j)
                    field = field + base_coeffs[k] * basis_row(basis, d, kl, j)
            residual_ref[at] = value
            solution_ref[at] = field
            return carry

        lax.fori_loop(0, ROWS, body, 0)


def call(kernel, outs, args, scratch=(), smem=0):
    vmem = pl.BlockSpec(memory_space=pltpu.VMEM)
    return pl.pallas_call(
        kernel,
        out_shape=outs,
        in_specs=[pl.BlockSpec(memory_space=pltpu.SMEM)] * smem + [vmem] * (len(args) - smem),
        out_specs=jax.tree.map(lambda _: vmem, outs),
        scratch_shapes=list(scratch),
        compiler_params=pltpu.CompilerParams(vmem_limit_bytes=20 * 1024 * 1024),
    )(*args)


def shape(*dims, dtype=F32):
    return jax.ShapeDtypeStruct(dims, dtype)


def exchange(value):
    return lax.all_to_all(value, ("gx", "gy"), 0, 0)


def steps(axis, wrap=False):
    size = lax.axis_size(axis)
    up = [(i, (i + 1) % size) for i in range(size if wrap else size - 1)]
    return up, [(j, i) for i, j in up]


def tied(first, *rest):
    return lax.optimization_barrier((first, *rest))


def on_device(src_cell, basis, images, induction):
    size_x, size_y = 8 * lax.axis_size("gx"), 128 * lax.axis_size("gy")
    peers = lax.axis_size("gx") * lax.axis_size("gy")
    block = jnp.concatenate(
        [images.reshape(LOCAL * ROWS, 8, 128), induction.reshape(6, 8, 128)], axis=0
    )
    right, left = steps("tx", wrap=True)
    one = lax.ppermute(block, "tx", right)
    three = lax.ppermute(block, "tx", left)
    own = call(pack_y_kernel, shape(PACKED, 8, 128, dtype=BF16), (block,))
    up, down = steps("gy")
    after, before = lax.ppermute(own, "gy", down), lax.ppermute(own, "gy", up)
    side = jnp.where(lax.broadcasted_iota(jnp.int32, own.shape, 1) < 4, after, before)
    far_low = lax.ppermute(jnp.concatenate([one[:CUT], side]), "tx", right)
    far_high = lax.ppermute(jnp.concatenate([three[CUT:], side]), "tx", left)
    far_side = lax.ppermute(side, "tx", [(i, (i + 2) % LOCAL) for i in range(LOCAL)])
    blocks = (block, one, three, far_low, far_high, side, far_side)

    half = shape(LOCAL * (HALF + PACKED), 8, 128, dtype=BF16)
    low, high = call(pack_x_kernel, (half, half), blocks)
    up, down = steps("gx")
    ln, hp = lax.ppermute(low, "gx", down), lax.ppermute(high, "gx", up)

    sums = pltpu.VMEM((128, 128), F32)
    side_scratch = pltpu.VMEM((2 * ROWS, 16, 128), F32)
    sent = call(
        functools.partial(gram_kernel, size_x, size_y),
        shape(peers, 4, 128),
        (src_cell, *blocks),
        (pltpu.VMEM((ROWS, 16, 128), F32), pltpu.VMEM((8 * VECS + 48, ROWS * 128), BF16)),
        smem=1,
    )
    got = exchange(sent)
    wide = shape(2 * ROWS, 16, 256)
    line = shape(peers, 128)
    small = shape(VECS, 128)
    static = (*blocks, ln, hp)
    own_basis = basis.reshape(LOCAL * ROWS, 8, 128)

    def total(value):
        return exchange(value.reshape(peers, 1, 128)).reshape(peers, 128)

    got, piece = tied(got, own_basis[:CUT])
    one_low, three_low = lax.ppermute(piece, "tx", right), lax.ppermute(piece, "tx", left)
    r, q, m, inverse, state, sent = call(
        functools.partial(begin_kernel, size_x, size_y),
        (wide, wide, shape(24, 16, 256), small, small, line),
        (src_cell, got, *static),
        (side_scratch, sums),
        smem=1,
    )

    def first(r, q, state, got):
        return call(
            functools.partial(first_kernel, size_x, size_y),
            (wide, wide, small, line),
            (got, *static, r, q, m, inverse, state),
            (side_scratch, sums),
        )

    sent, one_low, three_low = tied(sent, one_low, three_low)
    got, piece = tied(total(sent), own_basis[CUT:])
    one_high, three_high = lax.ppermute(piece, "tx", right), lax.ppermute(piece, "tx", left)
    u, a, state, sent = first(r, q, state, got)
    sent, one_high, three_high = tied(sent, one_high, three_high)
    got, one_low, three_high = tied(total(sent), one_low, three_high)
    two_low, two_high = lax.ppermute(one_low, "tx", right), lax.ppermute(three_high, "tx", left)
    r, q, field, state, sent = call(
        functools.partial(next_kernel, size_x, size_y),
        (wide, wide, shape(2 * ROWS, 8, 128), small, line),
        (got, *static, r, u, a, m, inverse, state),
        (side_scratch, sums),
    )
    sent, two_low, two_high = tied(sent, two_low, two_high)
    u, a, state, sent = first(r, q, state, total(sent))
    bases = (own_basis, one_low, one_high, three_low, three_high, two_low, two_high)
    narrow = shape(2 * ROWS, 8, 128)
    field, residual = call(
        last_kernel,
        (narrow, narrow),
        (total(sent), *blocks, *bases, r, u, a, inverse, state, field),
    )
    full = (2, 2, 3, 8, 8, 128)
    return field.reshape(full), residual.reshape(full)


def solution(mesh):
    in_specs = (
        P("tx"),
        P("tx", None, None, None, "gx", "gy"),
        P("tx", None, None, None, "gx", "gy"),
        P(None, "tx", "gx", "gy"),
    )
    out_specs = (P("tx", None, None, None, "gx", "gy"), P("tx", None, None, None, "gx", "gy"))
    return jax.shard_map(
        on_device, mesh=mesh, in_specs=in_specs, out_specs=out_specs, check_vma=False
    )
```

```python
import functools

import jax
import jax.numpy as jnp
from jax import lax
from jax.experimental import pallas as pl
from jax.experimental.pallas import tpu as pltpu
from jax.sharding import PartitionSpec as P

EPS = 1e-06
VECS = 16
LOCAL = 4
ROWS = 48
BLOCK = 198
HALF = 99
PACKED = 13
WEIGHTS = (1.0, 0.5, 0.25)
HIGH = lax.Precision.HIGHEST
F32 = jnp.float32
BF16 = jnp.bfloat16


def iota(shape, axis):
    return lax.broadcasted_iota(jnp.int32, shape, axis)


def pick_matrix(dtype):
    col = iota((8, 128), 0)
    lane = iota((8, 128), 1)
    return jnp.where(lane == jnp.where(col < 4, col, col + 120), 1.0, 0.0).astype(dtype)


def nt_dot(left, right, precision=None):
    return lax.dot_general(
        left, right, (((1,), (1,)), ((), ())), precision=precision, preferred_element_type=F32
    )


def full_dot(left, right):
    return lax.dot_general(
        left, right, (((1,), (0,)), ((), ())), precision=HIGH, preferred_element_type=F32
    )


BLOCKS = 7
CUT = 2 * ROWS


def vector_row(blocks, d, kl, j):
    row = kl * ROWS + j
    if d != 2:
        return blocks[(0, 1, None, 2)[d]][row].astype(F32)
    return blocks[3][row].astype(F32) if kl < 2 else blocks[4][row - CUT].astype(F32)


def induction_row(blocks, d, at):
    if d != 2:
        return blocks[(0, 1, None, 2)[d]][LOCAL * ROWS + at].astype(F32)
    return blocks[4][LOCAL * ROWS - CUT + at].astype(F32)


def side_tile(blocks, d, tile):
    ref, first = ((5, 0), (3, CUT), (6, 0), (4, BLOCK - CUT))[d]
    return blocks[ref][first + tile]


def pack_y_kernel(block_ref, out_ref):
    pick = pick_matrix(BF16)
    for tile in range(PACKED):
        first = tile * 16
        count = min(16, BLOCK - first)
        rows = block_ref[first : first + count].astype(F32).reshape(count * 8, 128).astype(BF16)
        picked = nt_dot(pick, rows)
        if count < 16:
            picked = jnp.concatenate([picked, jnp.zeros((8, 128 - count * 8), F32)], axis=1)
        out_ref[tile] = picked.astype(BF16)


def pack_x_kernel(*refs):
    blocks, lo_ref, hi_ref = refs[:BLOCKS], refs[BLOCKS], refs[BLOCKS + 1]
    top = iota((8, 128), 0) < 4

    def pair(one, two, at):
        two = pltpu.roll(two, 4, 0)
        lo_ref[at] = jnp.where(top, one, two).astype(BF16)
        hi_ref[at] = jnp.where(top, two, one).astype(BF16)

    def body(j, carry):
        for d in range(LOCAL):
            for kl in range(2):
                pair(
                    vector_row(blocks, d, kl, j),
                    vector_row(blocks, d, kl + 2, j),
                    d * HALF + kl * ROWS + j,
                )
        return carry

    lax.fori_loop(0, ROWS, body, 0)
    for d in range(LOCAL):
        for i in range(3):
            pair(
                induction_row(blocks, d, i),
                induction_row(blocks, d, i + 3),
                d * HALF + CUT + i,
            )
        for tile in range(PACKED):
            piece = side_tile(blocks, d, tile)
            lo_ref[LOCAL * HALF + d * PACKED + tile] = piece
            hi_ref[LOCAL * HALF + d * PACKED + tile] = piece


def inner_all(c_ref, field, sums_ref):
    def body(j, accs):
        one, two = field(0, j), field(1, j)
        new = []
        for k in range(VECS):
            vec = c_ref[k * ROWS + j]
            new.append(accs[2 * k] + vec * one)
            new.append(accs[2 * k + 1] + vec * two)
        return tuple(new)

    zero = jnp.zeros((8, 128), F32)
    accs = lax.fori_loop(0, ROWS, body, (zero,) * (2 * VECS))
    for k in range(VECS):
        for s in range(2):
            sums_ref[s * VECS + k : s * VECS + k + 1] = jnp.sum(
                accs[2 * k + s], axis=0, keepdims=True
            )


def inner_pairs(pairs, sums_ref, first):
    count = len(pairs)
    for s in range(2):

        def body(j, accs, s=s):
            return tuple(
                acc + one(s, j) * two(s, j) for acc, (one, two) in zip(accs, pairs)
            )

        zero = jnp.zeros((8, 128), F32)
        accs = lax.fori_loop(0, ROWS, body, (zero,) * count)
        for i in range(count):
            at = first + s * count + i
            sums_ref[at : at + 1] = jnp.sum(accs[i], axis=0, keepdims=True)


def row_of_sums(sums_ref):
    return nt_dot(jnp.ones((8, 128), F32), sums_ref[...], HIGH)[0:1]


def entry(row, lane):
    return row[:, lane : lane + 1]


def column_of(row, first):
    part = row[:, first : first + VECS]
    eye = iota((VECS, VECS), 0) == iota((VECS, VECS), 1)
    return jnp.sum(jnp.where(eye, part, 0.0), axis=1, keepdims=True)


def solve(inverse, row, first):
    return jnp.sum(inverse[:, :VECS] * row[:, first : first + VECS], axis=1, keepdims=True)


def spread(value):
    return jnp.broadcast_to(value, (8, 128))


def grid_mask(size_x, size_y):
    row, lane = iota((16, 256), 0), iota((16, 256), 1)
    x_pos = lax.axis_index("gx") * 8 + jnp.where(row < 12, row, row - 16)
    y_pos = lax.axis_index("gy") * 128 + jnp.where(lane < 132, lane, lane - 256)
    inside = (x_pos >= 0) & (x_pos < size_x) & (y_pos >= 0) & (y_pos < size_y)
    inside = inside & ((lane < 132) | (lane >= 252))
    return x_pos, y_pos, inside


def primary_field(cell, z, x_pos, y_pos, size_x, size_y):
    plane = size_x * size_y
    src_z = cell // plane
    rest = cell % plane
    d_z = (z - src_z).astype(F32)
    d_x = (x_pos - rest // size_y).astype(F32)
    d_y = (y_pos - rest % size_y).astype(F32)
    dist = jnp.sqrt(d_z * d_z + d_x * d_x + d_y * d_y)
    return jnp.exp(-dist / ((size_x + size_y) / 8.0))


def unpack_once(blocks, ln_ref, hp_ref, c_ref, x_ref, near_ref, far_ref):
    top = iota((8, 128), 0) < 4

    def body(j, carry):
        for d in range(LOCAL):
            for kl in range(LOCAL):
                k = d * LOCAL + kl
                c_ref[k * ROWS + j] = vector_row(blocks, d, kl, j)
                at = d * HALF + (kl % 2) * ROWS + j
                after, before = ln_ref[at].astype(F32), hp_ref[at].astype(F32)
                if kl < 2:
                    x_ref[k * ROWS + j] = jnp.where(top, after, before)
                else:
                    x_ref[k * ROWS + j] = pltpu.roll(jnp.where(top, before, after), 4, 0)
        return carry

    lax.fori_loop(0, ROWS, body, 0)
    from_next = iota((8, 128), 1) % 8 < 4
    for d in range(LOCAL):
        for t in range(PACKED - 1):
            at = LOCAL * HALF + d * PACKED + t
            near_ref[d * 12 + t] = side_tile(blocks, d, t).astype(F32)
            far_ref[d * 12 + t] = jnp.where(
                from_next, ln_ref[at].astype(F32), hp_ref[at].astype(F32)
            )


def combine_ext(coeffs, fields, interior, halo_x, unpacked_ref):
    c_ref, x_ref, near_ref, far_ref = fields

    def body(j, carry):
        inner = [jnp.zeros((8, 128), F32)] * 2
        outer = [jnp.zeros((8, 128), F32)] * 2
        for k in range(VECS):
            vec, edge = c_ref[k * ROWS + j], x_ref[k * ROWS + j]
            for s in range(2):
                inner[s] = inner[s] + coeffs[s][k] * vec
                outer[s] = outer[s] + coeffs[s][k] * edge
        for s in range(2):
            interior(s, j, inner[s])
            halo_x(s, j, outer[s])
        return carry

    lax.fori_loop(0, ROWS, body, 0)
    pick = pick_matrix(F32)
    for s in range(2):
        for tile in range(3):
            near = jnp.zeros((8, 128), F32)
            far = jnp.zeros((8, 128), F32)
            for k in range(VECS):
                near = near + coeffs[s][k] * near_ref[k * 3 + tile]
                far = far + coeffs[s][k] * far_ref[k * 3 + tile]
            place = s * ROWS + tile * 16
            near = full_dot(jnp.transpose(near), pick).reshape(16, 8, 128)
            far = full_dot(jnp.transpose(far), pick).reshape(16, 8, 128)
            unpacked_ref[place : place + 16, 0:8] = near
            unpacked_ref[place : place + 16, 8:16] = far


def apply_operator(e_ref, m_ref, out_ref, mask):
    def ahead(f, axis):
        return pltpu.roll(f, f.shape[axis] - 1, axis)

    def behind(f, axis):
        return pltpu.roll(f, 1, axis)

    def body(index, carry):
        base = index * 24
        other = jnp.where(index % 2 == 0, base + 24, base - 24)
        sign = jnp.where(index % 2 == 0, -1.0, 1.0).astype(F32)
        zero = jnp.zeros((16, 256), F32)
        b_x_old = -e_ref[base + 8]
        b_y_old = e_ref[base]
        for z in range(8):
            e_x, e_y, e_z = e_ref[base + z], e_ref[base + 8 + z], e_ref[base + 16 + z]
            up_x = e_ref[base + z + 1] if z < 7 else zero
            up_y = e_ref[base + 8 + z + 1] if z < 7 else zero
            b_x = (ahead(e_z, 1) - e_z) - (up_y - e_y)
            b_y = (up_x - e_x) - (ahead(e_z, 0) - e_z)
            b_z = (ahead(e_y, 0) - e_y) - (ahead(e_x, 1) - e_x)
            c_x = (b_z - behind(b_z, 1)) - (b_y - b_y_old)
            c_y = (b_x - b_x_old) - (b_z - behind(b_z, 0))
            c_z = (b_y - behind(b_y, 0)) - (b_x - behind(b_x, 1))
            for c, value in enumerate((c_x, c_y, c_z)):
                at = c * 8 + z
                value = value + sign * (m_ref[at] * e_ref[other + at])
                out_ref[base + at] = jnp.where(mask, value, 0.0)
            b_x_old, b_y_old = b_x, b_y
        return carry

    lax.fori_loop(0, 4, body, 0)


def brick(ref):
    return lambda s, j: ref[s * ROWS + j, 0:8, 0:128]


def pick_layer(values, z):
    want = lax.rem(lax.axis_index("tx") - z // 2 + LOCAL, LOCAL)
    result = values[0]
    for d in range(1, LOCAL):
        result = jnp.where(want == d, values[d], result)
    return result


def gram_kernel(size_x, size_y, src_ref, *refs):
    blocks, out_ref, field_ref, rows_ref = refs[:BLOCKS], *refs[BLOCKS:]
    x_pos = lax.axis_index("gx") * 8 + iota((8, 128), 0)
    y_pos = lax.axis_index("gy") * 128 + iota((8, 128), 1)
    for z in range(8):
        prim = [
            primary_field(src_ref[s], z, x_pos, y_pos, size_x, size_y) for s in range(2)
        ]
        for c in range(3):
            m = pick_layer([induction_row(blocks, d, 2 * c + z % 2) for d in range(LOCAL)], z)
            for s in range(2):
                real = (m - 1.0) * WEIGHTS[c] * prim[s]
                field_ref[c * 8 + z, s * 8 : s * 8 + 8] = real
                field_ref[24 + c * 8 + z, s * 8 : s * 8 + 8] = 0.5 * real

    def body(j, carry):
        columns = pl.ds(pl.multiple_of(j * 128, 128), 128)
        for pair in range(VECS // 2):
            d, kl = pair // 2, 2 * (pair % 2)
            both = [vector_row(blocks, d, kl + i, j) for i in range(2)]
            rows_ref[16 * pair : 16 * pair + 16, columns] = jnp.concatenate(both).astype(BF16)
        rest = field_ref[j]
        for piece in range(3):
            part = rest.astype(BF16)
            rest = rest - part.astype(F32)
            first = 8 * VECS + 16 * piece
            rows_ref[first : first + 16, columns] = part
        return carry

    lax.fori_loop(0, ROWS, body, 0)
    full = nt_dot(rows_ref[0:128], rows_ref[...])
    row, lane = iota((128, 128), 0), iota((128, 128), 1)
    gram = jnp.where(row % 8 == lane % 8, full[:, 0:128], 0.0).reshape(VECS, 8, 128)
    gram = jnp.sum(gram, axis=1)
    gram = full_dot(gram, jnp.where(row // 8 == lane % 16, 1.0, 0.0).astype(F32))
    gram = jnp.where(iota((VECS, 128), 1) // 16 == iota((VECS, 128), 0) % 8, gram, 0.0)
    gram = jnp.sum(gram.reshape(2, 8, 128), axis=1)
    inner = full[:, 128:144] + full[:, 144:160] + full[:, 160:176]
    inner = jnp.where(iota((128, 16), 0) % 8 == iota((128, 16), 1) % 8, inner, 0.0)
    inner = jnp.sum(inner.reshape(VECS, 8, 16), axis=1)
    lines = []
    for s in range(2):
        chosen = jnp.where(iota((8, 16), 1) // 8 == s, 1.0, 0.0).astype(F32)
        lines.append(nt_dot(chosen, inner, HIGH)[0:1])
    line = jnp.concatenate(lines + [jnp.zeros((1, 96), F32)], axis=1)
    rows = jnp.concatenate([gram, line, jnp.zeros((1, 128), F32)], axis=0)
    out_ref[...] = jnp.broadcast_to(rows[None], out_ref.shape)


def invert(rows):
    lane, row = iota((VECS, 128), 1), iota((VECS, 128), 0)
    wide = jnp.where(row < 8, rows[0:1], rows[1:2])
    wide = jnp.where(lane // 16 == row % 8, wide, 0.0)
    fold = jnp.where(iota((128, 128), 0) % 16 == iota((128, 128), 1), 1.0, 0.0).astype(F32)
    work = full_dot(wide, fold) + jnp.where(lane == row + VECS, 1.0, 0.0)
    for j in range(VECS):
        pivot = work[j : j + 1] / work[j : j + 1, j : j + 1]
        work = jnp.where(row == j, pivot, work - work[:, j : j + 1] * pivot)
    return pltpu.roll(work, 128 - VECS, 1)


def begin_kernel(size_x, size_y, src_ref, got_ref, *refs):
    blocks, ln_ref, hp_ref = refs[:BLOCKS], refs[BLOCKS], refs[BLOCKS + 1]
    refs = refs[BLOCKS + 2 :]
    r_ref, q_ref, m_ref, inv_ref, state_ref, out_ref = refs[:6]
    fields, side_ref, sums_ref = refs[6:10], refs[10], refs[11]
    unpack_once(blocks, ln_ref, hp_ref, *fields)
    total = jnp.sum(got_ref[...], axis=0)
    inverse = invert(total[0:2])
    inv_ref[...] = inverse
    inner = total[2:3]
    x_pos, y_pos, mask = grid_mask(size_x, size_y)
    start = [solve(inverse, inner, s * VECS) for s in range(2)]
    lane = iota((VECS, 128), 1)
    state_ref[...] = jnp.where(lane == 2, start[0], jnp.where(lane == 3, start[1], 0.0))
    coeffs = [[spread(-start[s][k : k + 1]) for k in range(VECS)] for s in range(2)]

    def put(rows, columns):
        def store(s, j, value):
            r_ref[s * ROWS + j, rows, columns] = value

        return store

    combine_ext(
        coeffs, fields,
        put(slice(0, 8), slice(0, 128)), put(slice(8, 16), slice(0, 128)), side_ref,
    )
    top = iota((8, 128), 0) < 4
    from_next = iota((8, 128), 1) % 8 < 4
    pick = pick_matrix(F32)
    sides = []
    for d in range(LOCAL):
        at = 4 * HALF + d * PACKED + 12
        near = side_tile(blocks, d, 12).astype(F32)
        far = jnp.where(from_next, ln_ref[at].astype(F32), hp_ref[at].astype(F32))
        near = full_dot(jnp.transpose(near), pick)[:48].reshape(6, 8, 128)
        far = full_dot(jnp.transpose(far), pick)[:48].reshape(6, 8, 128)
        sides.append((near, far))
    for c in range(3):
        for z in range(8):
            at = 2 * c + z % 2
            quarters = []
            for d in range(LOCAL):
                inner_m = induction_row(blocks, d, at)
                row = d * HALF + 96 + at % 3
                after, before = ln_ref[row].astype(F32), hp_ref[row].astype(F32)
                if at < 3:
                    edge = jnp.where(top, after, before)
                else:
                    edge = pltpu.roll(jnp.where(top, before, after), 4, 0)
                left = jnp.concatenate([inner_m, edge], axis=0)
                right = jnp.concatenate([sides[d][0][at], sides[d][1][at]], axis=0)
                quarters.append(jnp.concatenate([left, right], axis=1))
            m_ref[c * 8 + z] = pick_layer(quarters, z)

    for s in range(2):

        def body(z, carry, s=s):
            prim = primary_field(src_ref[s], z, x_pos, y_pos, size_x, size_y)
            for c in range(3):
                at = c * 8 + z
                real = jnp.where(mask, (m_ref[at] - 1.0) * WEIGHTS[c] * prim, 0.0)
                for p in range(2):
                    place = s * ROWS + p * 24 + at
                    value = real if p == 0 else 0.5 * real
                    r_ref[place, :, 0:128] = r_ref[place, :, 0:128] + value[:, 0:128]
                    r_ref[place, :, 128:256] = side_ref[place] + value[:, 128:256]
            return carry

        lax.fori_loop(0, 8, body, 0)
    apply_operator(r_ref, m_ref, q_ref, mask)
    finish_first(fields[0], r_ref, q_ref, sums_ref, out_ref)


def finish_first(c_ref, r_ref, q_ref, sums_ref, out_ref):
    sums_ref[...] = jnp.zeros_like(sums_ref)
    r, q = brick(r_ref), brick(q_ref)
    inner_all(c_ref, q, sums_ref)
    inner_pairs([(r, r), (r, q)], sums_ref, 32)
    out_ref[...] = jnp.broadcast_to(row_of_sums(sums_ref), out_ref.shape)


def first_kernel(size_x, size_y, got_ref, *refs):
    fields, refs = refs[:4], refs[4:]
    r_ref, q_ref, m_ref, inv_ref, old_ref = refs[:5]
    u_ref, a_ref, state_ref, out_ref, side_ref, sums_ref = refs[5:]
    row = jnp.sum(got_ref[...], axis=0, keepdims=True)
    _, _, mask = grid_mask(size_x, size_y)
    lane = iota((VECS, 128), 1)
    state = old_ref[...]
    coeffs, q_scale, r_scale = [], [], []
    for s in range(2):
        rr, rq = entry(row, 32 + 2 * s), entry(row, 33 + 2 * s)
        beta = jnp.sqrt(rr + EPS)
        g_zero = solve(inv_ref[...], row, s * VECS) / beta
        h_00 = rq / (beta * beta)
        coeffs.append([spread(-g_zero[k : k + 1]) for k in range(VECS)])
        q_scale.append(spread(1.0 / beta))
        r_scale.append(spread(-h_00 / beta))
        state = jnp.where(lane == s, g_zero, state)
        state = jnp.where(lane == 8 + s, beta, state)
        state = jnp.where(lane == 10 + s, h_00, state)
        state = jnp.where(lane == 12 + s, rr, state)
    state_ref[...] = state

    def put(rows, columns):
        def store(s, j, value):
            at = s * ROWS + j
            value = value + q_scale[s] * q_ref[at, rows, columns]
            u_ref[at, rows, columns] = value + r_scale[s] * r_ref[at, rows, columns]

        return store

    combine_ext(
        coeffs, fields,
        put(slice(0, 8), slice(0, 128)), put(slice(8, 16), slice(0, 128)), side_ref,
    )
    for s in range(2):

        def body(j, carry, s=s):
            at = s * ROWS + j
            value = side_ref[at]
            for half in range(2):
                rows = slice(half * 8, half * 8 + 8)
                new = value[rows] + q_scale[s] * q_ref[at, rows, 128:256]
                u_ref[at, rows, 128:256] = new + r_scale[s] * r_ref[at, rows, 128:256]
            return carry

        lax.fori_loop(0, ROWS, body, 0)
    apply_operator(u_ref, m_ref, a_ref, mask)
    sums_ref[...] = jnp.zeros_like(sums_ref)
    r, u, a = brick(r_ref), brick(u_ref), brick(a_ref)
    inner_all(fields[0], a, sums_ref)
    inner_pairs([(u, u), (r, u), (r, a), (u, a), (a, a)], sums_ref, 32)
    out_ref[...] = jnp.broadcast_to(row_of_sums(sums_ref), out_ref.shape)


def close_cycle(row, inverse, state, s):
    uu, ru, ra, ua, aa = [entry(row, 32 + 5 * s + i) for i in range(5)]
    g_zero = state[:, s : s + 1]
    beta, h_00, rr = [state[0:1, first + s : first + s + 1] for first in (8, 10, 12)]
    h_10 = jnp.sqrt(uu + EPS)
    inner = column_of(row, s * VECS) / h_10
    g_one = solve(inverse, row, s * VECS) / h_10
    h_01 = ra / (beta * h_10)
    h_11 = ua / (h_10 * h_10)
    left = aa / (h_10 * h_10) - jnp.sum(g_one * inner, axis=0, keepdims=True)
    left = left - 2.0 * (h_01 * h_01 + h_11 * h_11)
    left = left + h_01 * h_01 * (rr / (beta * beta)) + h_11 * h_11 * (uu / (h_10 * h_10))
    left = left + 2.0 * h_01 * h_11 * (ru / (beta * h_10))
    h_21_square = jnp.maximum(left, 0.0) + EPS
    n_00 = h_00 * h_00 + h_10 * h_10
    n_01 = h_00 * h_01 + h_10 * h_11
    n_11 = h_01 * h_01 + h_11 * h_11 + h_21_square
    l_00 = jnp.sqrt(n_00)
    l_10 = n_01 / l_00
    l_11 = jnp.sqrt(n_11 - l_10 * l_10)
    z_0 = beta * h_00 / l_00
    z_1 = (beta * h_01 - l_10 * z_0) / l_11
    y_1 = z_1 / l_11
    y_0 = (z_0 - l_10 * y_1) / l_00
    t_0 = beta - h_00 * y_0 - h_01 * y_1
    t_1 = -h_10 * y_0 - h_11 * y_1
    return {
        "r": (t_0 + y_1 * h_01) / beta,
        "u": (t_1 + y_1 * h_11) / h_10,
        "a": -y_1 / h_10,
        "c": y_1 * g_one,
        "sol_r": y_0 / beta,
        "sol_u": y_1 / h_10,
        "basis": state[:, 2 + s : 3 + s] - g_zero * y_0 - g_one * y_1,
    }


def next_kernel(size_x, size_y, got_ref, *refs):
    fields, refs = refs[:4], refs[4:]
    r_ref, u_ref, a_ref, m_ref, inv_ref, old_ref = refs[:6]
    new_ref, q_ref, sol_ref, state_ref, out_ref, side_ref, sums_ref = refs[6:]
    row = jnp.sum(got_ref[...], axis=0, keepdims=True)
    _, _, mask = grid_mask(size_x, size_y)
    state = old_ref[...]
    small = [close_cycle(row, inv_ref[...], state, s) for s in range(2)]
    lane = iota((VECS, 128), 1)
    state_ref[...] = jnp.where(
        lane == 2, small[0]["basis"], jnp.where(lane == 3, small[1]["basis"], 0.0)
    )
    coeffs = [[spread(small[s]["c"][k : k + 1]) for k in range(VECS)] for s in range(2)]
    scale = [{name: spread(small[s][name]) for name in ("r", "u", "a", "sol_r", "sol_u")} for s in range(2)]

    def total(s, at, rows, columns, value):
        value = value + scale[s]["r"] * r_ref[at, rows, columns]
        value = value + scale[s]["u"] * u_ref[at, rows, columns]
        return value + scale[s]["a"] * a_ref[at, rows, columns]

    def put(rows, columns):
        def store(s, j, value):
            at = s * ROWS + j
            new_ref[at, rows, columns] = total(s, at, rows, columns, value)

        return store

    combine_ext(
        coeffs, fields,
        put(slice(0, 8), slice(0, 128)), put(slice(8, 16), slice(0, 128)), side_ref,
    )
    for s in range(2):

        def body(j, carry, s=s):
            at = s * ROWS + j
            value = side_ref[at]
            for half in range(2):
                rows = slice(half * 8, half * 8 + 8)
                new_ref[at, rows, 128:256] = total(s, at, rows, slice(128, 256), value[rows])
            sol_ref[at] = (
                scale[s]["sol_r"] * r_ref[at, 0:8, 0:128]
                + scale[s]["sol_u"] * u_ref[at, 0:8, 0:128]
            )
            return carry

        lax.fori_loop(0, ROWS, body, 0)
    apply_operator(new_ref, m_ref, q_ref, mask)
    finish_first(fields[0], new_ref, q_ref, sums_ref, out_ref)


def basis_row(basis, d, kl, j):
    row = kl * ROWS + j
    if d == 0:
        return basis[0][row].astype(F32)
    first = {1: 1, 3: 3, 2: 5}[d]
    return basis[first][row].astype(F32) if kl < 2 else basis[first + 1][row - CUT].astype(F32)


def last_kernel(got_ref, c_ref, *refs):
    basis, refs = refs[:7], refs[7:]
    r_ref, u_ref, a_ref, inv_ref, old_ref, sol_ref = refs[:6]
    solution_ref, residual_ref = refs[6:]
    row = jnp.sum(got_ref[...], axis=0, keepdims=True)
    state = old_ref[...]
    small = [close_cycle(row, inv_ref[...], state, s) for s in range(2)]
    coeffs = [[spread(one["c"][k : k + 1]) for k in range(VECS)] for one in small]
    basis_coeffs = [[spread(one["basis"][k : k + 1]) for k in range(VECS)] for one in small]
    names = ("r", "u", "a", "sol_r", "sol_u")
    scale = [{name: spread(one[name]) for name in names} for one in small]

    def residual_body(j, carry):
        values = []
        for s in range(2):
            r, u, a = brick(r_ref)(s, j), brick(u_ref)(s, j), brick(a_ref)(s, j)
            values.append(scale[s]["r"] * r + scale[s]["u"] * u + scale[s]["a"] * a)
        for k in range(VECS):
            vec = c_ref[k * ROWS + j]
            for s in range(2):
                values[s] = values[s] + coeffs[s][k] * vec
        for s in range(2):
            residual_ref[s * ROWS + j] = values[s]
        return carry

    def solution_body(j, carry):
        values = []
        for s in range(2):
            r, u = brick(r_ref)(s, j), brick(u_ref)(s, j)
            old = sol_ref[s * ROWS + j]
            values.append(old + scale[s]["sol_r"] * r + scale[s]["sol_u"] * u)
        for d in range(LOCAL):
            for kl in range(LOCAL):
                vec = basis_row(basis, d, kl, j)
                for s in range(2):
                    values[s] = values[s] + basis_coeffs[s][d * LOCAL + kl] * vec
        for s in range(2):
            solution_ref[s * ROWS + j] = values[s]
        return carry

    lax.fori_loop(0, ROWS, residual_body, 0)
    lax.fori_loop(0, ROWS, solution_body, 0)


def call(kernel, outs, args, scratch=(), smem=0):
    vmem = pl.BlockSpec(memory_space=pltpu.VMEM)
    return pl.pallas_call(
        kernel,
        out_shape=outs,
        in_specs=[pl.BlockSpec(memory_space=pltpu.SMEM)] * smem + [vmem] * (len(args) - smem),
        out_specs=jax.tree.map(lambda _: vmem, outs),
        scratch_shapes=list(scratch),
        compiler_params=pltpu.CompilerParams(vmem_limit_bytes=20 * 1024 * 1024),
    )(*args)


def shape(*dims, dtype=F32):
    return jax.ShapeDtypeStruct(dims, dtype)


def exchange(value):
    return lax.all_to_all(value, ("gx", "gy"), 0, 0)


def steps(axis, wrap=False):
    size = lax.axis_size(axis)
    up = [(i, (i + 1) % size) for i in range(size if wrap else size - 1)]
    return up, [(j, i) for i, j in up]


def tied(first, *rest):
    return lax.optimization_barrier((first, *rest))


def on_device(src_cell, basis, images, induction):
    size_x, size_y = 8 * lax.axis_size("gx"), 128 * lax.axis_size("gy")
    peers = lax.axis_size("gx") * lax.axis_size("gy")
    block = jnp.concatenate(
        [images.reshape(LOCAL * ROWS, 8, 128), induction.reshape(6, 8, 128)], axis=0
    )
    right, left = steps("tx", wrap=True)
    one = lax.ppermute(block, "tx", right)
    three = lax.ppermute(block, "tx", left)
    own = call(pack_y_kernel, shape(PACKED, 8, 128, dtype=BF16), (block,))
    up, down = steps("gy")
    after, before = lax.ppermute(own, "gy", down), lax.ppermute(own, "gy", up)
    side = jnp.where(lax.broadcasted_iota(jnp.int32, own.shape, 1) < 4, after, before)
    far_side = lax.ppermute(side, "tx", [(i, (i + 2) % LOCAL) for i in range(LOCAL)])
    far_side, one, three = tied(far_side, one, three)
    far_low = lax.ppermute(jnp.concatenate([one[:CUT], side]), "tx", right)
    far_high = lax.ppermute(jnp.concatenate([three[CUT:], side]), "tx", left)
    blocks = (block, one, three, far_low, far_high, side, far_side)

    half = shape(LOCAL * (HALF + PACKED), 8, 128, dtype=BF16)
    low, high = call(pack_x_kernel, (half, half), blocks)
    up, down = steps("gx")
    ln, hp = lax.ppermute(low, "gx", down), lax.ppermute(high, "gx", up)

    sums = pltpu.VMEM((128, 128), F32)
    side_scratch = pltpu.VMEM((2 * ROWS, 16, 128), F32)
    sent = call(
        functools.partial(gram_kernel, size_x, size_y),
        shape(peers, 4, 128),
        (src_cell, *blocks),
        (pltpu.VMEM((ROWS, 16, 128), F32), pltpu.VMEM((8 * VECS + 48, ROWS * 128), BF16)),
        smem=1,
    )
    got = exchange(sent)
    wide = shape(2 * ROWS, 16, 256)
    line = shape(peers, 128)
    small = shape(VECS, 128)
    own_basis = basis.reshape(LOCAL * ROWS, 8, 128)

    def total(value):
        return exchange(value.reshape(peers, 1, 128)).reshape(peers, 128)

    got, piece = tied(got, own_basis[:CUT])
    one_low, three_low = lax.ppermute(piece, "tx", right), lax.ppermute(piece, "tx", left)
    whole, tiles = shape(VECS * ROWS, 8, 128), shape(3 * VECS, 8, 128)
    r, q, m, inverse, state, sent, *fields = call(
        functools.partial(begin_kernel, size_x, size_y),
        (wide, wide, shape(24, 16, 256), small, small, line, whole, whole, tiles, tiles),
        (src_cell, got, *blocks, ln, hp),
        (side_scratch, sums),
        smem=1,
    )

    def first(r, q, state, got):
        return call(
            functools.partial(first_kernel, size_x, size_y),
            (wide, wide, small, line),
            (got, *fields, r, q, m, inverse, state),
            (side_scratch, sums),
        )

    sent, one_low, three_low = tied(sent, one_low, three_low)
    got, piece = tied(total(sent), own_basis[CUT:])
    one_high, three_high = lax.ppermute(piece, "tx", right), lax.ppermute(piece, "tx", left)
    u, a, state, sent = first(r, q, state, got)
    sent, one_high, three_high = tied(sent, one_high, three_high)
    got, one_low, three_high = tied(total(sent), one_low, three_high)
    two_low, two_high = lax.ppermute(one_low, "tx", right), lax.ppermute(three_high, "tx", left)
    r, q, field, state, sent = call(
        functools.partial(next_kernel, size_x, size_y),
        (wide, wide, shape(2 * ROWS, 8, 128), small, line),
        (got, *fields, r, u, a, m, inverse, state),
        (side_scratch, sums),
    )
    sent, two_low, two_high = tied(sent, two_low, two_high)
    u, a, state, sent = first(r, q, state, total(sent))
    bases = (own_basis, one_low, one_high, three_low, three_high, two_low, two_high)
    narrow = shape(2 * ROWS, 8, 128)
    field, residual = call(
        last_kernel,
        (narrow, narrow),
        (total(sent), fields[0], *bases, r, u, a, inverse, state, field),
    )
    full = (2, 2, 3, 8, 8, 128)
    return field.reshape(full), residual.reshape(full)


def solution(mesh):
    in_specs = (
        P("tx"),
        P("tx", None, None, None, "gx", "gy"),
        P("tx", None, None, None, "gx", "gy"),
        P(None, "tx", "gx", "gy"),
    )
    out_specs = (P("tx", None, None, None, "gx", "gy"), P("tx", None, None, None, "gx", "gy"))
    return jax.shard_map(
        on_device, mesh=mesh, in_specs=in_specs, out_specs=out_specs, check_vma=False
    )
```

```python
import functools

import jax
import jax.numpy as jnp
from jax import lax
from jax.experimental import pallas as pl
from jax.experimental.pallas import tpu as pltpu
from jax.sharding import PartitionSpec as P

EPS = 1e-06
VECS = 16
LOCAL = 4
ROWS = 48
BLOCK = 198
HALF = 99
PACKED = 13
WEIGHTS = (1.0, 0.5, 0.25)
HIGH = lax.Precision.HIGHEST
F32 = jnp.float32
BF16 = jnp.bfloat16


def iota(shape, axis):
    return lax.broadcasted_iota(jnp.int32, shape, axis)


def pick_matrix(dtype):
    col = iota((8, 128), 0)
    lane = iota((8, 128), 1)
    return jnp.where(lane == jnp.where(col < 4, col, col + 120), 1.0, 0.0).astype(dtype)


def nt_dot(left, right, precision=None):
    return lax.dot_general(
        left, right, (((1,), (1,)), ((), ())), precision=precision, preferred_element_type=F32
    )


def full_dot(left, right):
    return lax.dot_general(
        left, right, (((1,), (0,)), ((), ())), precision=HIGH, preferred_element_type=F32
    )


BLOCKS = 7
CUT = 2 * ROWS


def vector_row(blocks, d, kl, j):
    row = kl * ROWS + j
    if d != 2:
        return blocks[(0, 1, None, 2)[d]][row].astype(F32)
    return blocks[3][row].astype(F32) if kl < 2 else blocks[4][row - CUT].astype(F32)


def induction_row(blocks, d, at):
    if d != 2:
        return blocks[(0, 1, None, 2)[d]][LOCAL * ROWS + at].astype(F32)
    return blocks[4][LOCAL * ROWS - CUT + at].astype(F32)


def side_tile(blocks, d, tile):
    ref, first = ((5, 0), (3, CUT), (6, 0), (4, BLOCK - CUT))[d]
    return blocks[ref][first + tile]


def pack_y_kernel(block_ref, out_ref):
    pick = pick_matrix(BF16)
    for tile in range(PACKED):
        first = tile * 16
        count = min(16, BLOCK - first)
        rows = block_ref[first : first + count].astype(F32).reshape(count * 8, 128).astype(BF16)
        picked = nt_dot(pick, rows)
        if count < 16:
            picked = jnp.concatenate([picked, jnp.zeros((8, 128 - count * 8), F32)], axis=1)
        out_ref[tile] = picked.astype(BF16)


EARLY, LATE = (0, 1, 3), (2,)
EARLY_SIDES, LATE_SIDES = (0,), (1, 2, 3)


def halo_row(halos, d, row):
    ref = 2 if d == 2 else 0
    at = (0 if d == 2 else EARLY.index(d)) * HALF + row
    return halos[ref][at].astype(F32), halos[ref + 1][at].astype(F32)


def halo_side(halos, d, tile):
    ref = 0 if d == 0 else 2
    at = (len(EARLY) * HALF if d == 0 else HALF + LATE_SIDES.index(d) * PACKED) + tile
    after, before = halos[ref][at].astype(F32), halos[ref + 1][at].astype(F32)
    return jnp.where(iota((8, 128), 1) % 8 < 4, after, before)


def pack_x_kernel(group, sides, *refs):
    blocks, (lo_ref, hi_ref) = refs[:-2], refs[-2:]
    top = iota((8, 128), 0) < 4

    def pair(one, two, at):
        two = pltpu.roll(two, 4, 0)
        lo_ref[at] = jnp.where(top, one, two).astype(BF16)
        hi_ref[at] = jnp.where(top, two, one).astype(BF16)

    def body(j, carry):
        for place, d in enumerate(group):
            for kl in range(2):
                pair(
                    vector_row(blocks, d, kl, j),
                    vector_row(blocks, d, kl + 2, j),
                    place * HALF + kl * ROWS + j,
                )
        return carry

    lax.fori_loop(0, ROWS, body, 0)
    for place, d in enumerate(group):
        for i in range(3):
            pair(
                induction_row(blocks, d, i),
                induction_row(blocks, d, i + 3),
                place * HALF + CUT + i,
            )
    for place, d in enumerate(sides):
        for tile in range(PACKED):
            piece = side_tile(blocks, d, tile)
            lo_ref[len(group) * HALF + place * PACKED + tile] = piece
            hi_ref[len(group) * HALF + place * PACKED + tile] = piece


def inner_all(c_ref, field, sums_ref):
    def body(j, accs):
        one, two = field(0, j), field(1, j)
        new = []
        for k in range(VECS):
            vec = c_ref[k * ROWS + j]
            new.append(accs[2 * k] + vec * one)
            new.append(accs[2 * k + 1] + vec * two)
        return tuple(new)

    zero = jnp.zeros((8, 128), F32)
    accs = lax.fori_loop(0, ROWS, body, (zero,) * (2 * VECS))
    for k in range(VECS):
        for s in range(2):
            sums_ref[s * VECS + k : s * VECS + k + 1] = jnp.sum(
                accs[2 * k + s], axis=0, keepdims=True
            )


def inner_pairs(pairs, sums_ref, first):
    count = len(pairs)
    for s in range(2):

        def body(j, accs, s=s):
            return tuple(
                acc + one(s, j) * two(s, j) for acc, (one, two) in zip(accs, pairs)
            )

        zero = jnp.zeros((8, 128), F32)
        accs = lax.fori_loop(0, ROWS, body, (zero,) * count)
        for i in range(count):
            at = first + s * count + i
            sums_ref[at : at + 1] = jnp.sum(accs[i], axis=0, keepdims=True)


def row_of_sums(sums_ref):
    return nt_dot(jnp.ones((8, 128), F32), sums_ref[...], HIGH)[0:1]


def entry(row, lane):
    return row[:, lane : lane + 1]


def column_of(row, first):
    part = row[:, first : first + VECS]
    eye = iota((VECS, VECS), 0) == iota((VECS, VECS), 1)
    return jnp.sum(jnp.where(eye, part, 0.0), axis=1, keepdims=True)


def solve(inverse, row, first):
    return jnp.sum(inverse[:, :VECS] * row[:, first : first + VECS], axis=1, keepdims=True)


def spread(value):
    return jnp.broadcast_to(value, (8, 128))


def grid_mask(size_x, size_y):
    row, lane = iota((16, 256), 0), iota((16, 256), 1)
    x_pos = lax.axis_index("gx") * 8 + jnp.where(row < 12, row, row - 16)
    y_pos = lax.axis_index("gy") * 128 + jnp.where(lane < 132, lane, lane - 256)
    inside = (x_pos >= 0) & (x_pos < size_x) & (y_pos >= 0) & (y_pos < size_y)
    inside = inside & ((lane < 132) | (lane >= 252))
    return x_pos, y_pos, inside


def primary_field(cell, z, x_pos, y_pos, size_x, size_y):
    plane = size_x * size_y
    src_z = cell // plane
    rest = cell % plane
    d_z = (z - src_z).astype(F32)
    d_x = (x_pos - rest // size_y).astype(F32)
    d_y = (y_pos - rest % size_y).astype(F32)
    dist = jnp.sqrt(d_z * d_z + d_x * d_x + d_y * d_y)
    return jnp.exp(-dist / ((size_x + size_y) / 8.0))


def unpack_once(blocks, halos, c_ref, x_ref, near_ref, far_ref):
    top = iota((8, 128), 0) < 4

    def body(j, carry):
        for d in range(LOCAL):
            for kl in range(LOCAL):
                k = d * LOCAL + kl
                c_ref[k * ROWS + j] = vector_row(blocks, d, kl, j)
                after, before = halo_row(halos, d, (kl % 2) * ROWS + j)
                if kl < 2:
                    x_ref[k * ROWS + j] = jnp.where(top, after, before)
                else:
                    x_ref[k * ROWS + j] = pltpu.roll(jnp.where(top, before, after), 4, 0)
        return carry

    lax.fori_loop(0, ROWS, body, 0)
    for d in range(LOCAL):
        for t in range(PACKED - 1):
            near_ref[d * 12 + t] = side_tile(blocks, d, t).astype(F32)
            far_ref[d * 12 + t] = halo_side(halos, d, t)


AT_ONCE = 4


def plus(total, term):
    return term if total is None else total + term


def combine_ext(coeffs, fields, interior, halo_x, unpacked_ref):
    c_ref, x_ref, near_ref, far_ref = fields

    def body(step, carry):
        rows = [step * AT_ONCE + i for i in range(AT_ONCE)]
        inner = [[None] * AT_ONCE, [None] * AT_ONCE]
        outer = [[None] * AT_ONCE, [None] * AT_ONCE]
        for k in range(VECS):
            for i, j in enumerate(rows):
                vec, edge = c_ref[k * ROWS + j], x_ref[k * ROWS + j]
                for s in range(2):
                    inner[s][i] = plus(inner[s][i], coeffs[s][k] * vec)
                    outer[s][i] = plus(outer[s][i], coeffs[s][k] * edge)
        for i, j in enumerate(rows):
            for s in range(2):
                interior(s, j, inner[s][i])
                halo_x(s, j, outer[s][i])
        return carry

    lax.fori_loop(0, ROWS // AT_ONCE, body, 0)
    pick = pick_matrix(F32)
    for s in range(2):
        for tile in range(3):
            near = jnp.zeros((8, 128), F32)
            far = jnp.zeros((8, 128), F32)
            for k in range(VECS):
                near = near + coeffs[s][k] * near_ref[k * 3 + tile]
                far = far + coeffs[s][k] * far_ref[k * 3 + tile]
            place = s * ROWS + tile * 16
            near = full_dot(jnp.transpose(near), pick).reshape(16, 8, 128)
            far = full_dot(jnp.transpose(far), pick).reshape(16, 8, 128)
            unpacked_ref[place : place + 16, 0:8] = near
            unpacked_ref[place : place + 16, 8:16] = far


def apply_operator(e_ref, m_ref, out_ref, mask):
    def ahead(f, axis):
        return pltpu.roll(f, f.shape[axis] - 1, axis)

    def behind(f, axis):
        return pltpu.roll(f, 1, axis)

    def body(index, carry):
        base = index * 24
        other = jnp.where(index % 2 == 0, base + 24, base - 24)
        sign = jnp.where(index % 2 == 0, -1.0, 1.0).astype(F32)
        zero = jnp.zeros((16, 256), F32)
        b_x_old = -e_ref[base + 8]
        b_y_old = e_ref[base]
        for z in range(8):
            e_x, e_y, e_z = e_ref[base + z], e_ref[base + 8 + z], e_ref[base + 16 + z]
            up_x = e_ref[base + z + 1] if z < 7 else zero
            up_y = e_ref[base + 8 + z + 1] if z < 7 else zero
            b_x = (ahead(e_z, 1) - e_z) - (up_y - e_y)
            b_y = (up_x - e_x) - (ahead(e_z, 0) - e_z)
            b_z = (ahead(e_y, 0) - e_y) - (ahead(e_x, 1) - e_x)
            c_x = (b_z - behind(b_z, 1)) - (b_y - b_y_old)
            c_y = (b_x - b_x_old) - (b_z - behind(b_z, 0))
            c_z = (b_y - behind(b_y, 0)) - (b_x - behind(b_x, 1))
            for c, value in enumerate((c_x, c_y, c_z)):
                at = c * 8 + z
                value = value + sign * (m_ref[at] * e_ref[other + at])
                out_ref[base + at] = jnp.where(mask, value, 0.0)
            b_x_old, b_y_old = b_x, b_y
        return carry

    lax.fori_loop(0, 4, body, 0)


def brick(ref):
    return lambda s, j: ref[s * ROWS + j, 0:8, 0:128]


def pick_layer(values, z):
    want = lax.rem(lax.axis_index("tx") - z // 2 + LOCAL, LOCAL)
    result = values[0]
    for d in range(1, LOCAL):
        result = jnp.where(want == d, values[d], result)
    return result


def gram_kernel(size_x, size_y, src_ref, *refs):
    blocks, out_ref, field_ref, rows_ref = refs[:BLOCKS], *refs[BLOCKS:]
    x_pos = lax.axis_index("gx") * 8 + iota((8, 128), 0)
    y_pos = lax.axis_index("gy") * 128 + iota((8, 128), 1)
    for z in range(8):
        prim = [
            primary_field(src_ref[s], z, x_pos, y_pos, size_x, size_y) for s in range(2)
        ]
        for c in range(3):
            m = pick_layer([induction_row(blocks, d, 2 * c + z % 2) for d in range(LOCAL)], z)
            for s in range(2):
                real = (m - 1.0) * WEIGHTS[c] * prim[s]
                field_ref[c * 8 + z, s * 8 : s * 8 + 8] = real
                field_ref[24 + c * 8 + z, s * 8 : s * 8 + 8] = 0.5 * real

    def body(j, carry):
        columns = pl.ds(pl.multiple_of(j * 128, 128), 128)
        for pair in range(VECS // 2):
            d, kl = pair // 2, 2 * (pair % 2)
            both = [vector_row(blocks, d, kl + i, j) for i in range(2)]
            rows_ref[16 * pair : 16 * pair + 16, columns] = jnp.concatenate(both).astype(BF16)
        rest = field_ref[j]
        for piece in range(3):
            part = rest.astype(BF16)
            rest = rest - part.astype(F32)
            first = 8 * VECS + 16 * piece
            rows_ref[first : first + 16, columns] = part
        return carry

    lax.fori_loop(0, ROWS, body, 0)
    full = nt_dot(rows_ref[0:128], rows_ref[...])
    row, lane = iota((128, 128), 0), iota((128, 128), 1)
    gram = jnp.where(row % 8 == lane % 8, full[:, 0:128], 0.0).reshape(VECS, 8, 128)
    gram = jnp.sum(gram, axis=1)
    gram = full_dot(gram, jnp.where(row // 8 == lane % 16, 1.0, 0.0).astype(F32))
    gram = jnp.where(iota((VECS, 128), 1) // 16 == iota((VECS, 128), 0) % 8, gram, 0.0)
    gram = jnp.sum(gram.reshape(2, 8, 128), axis=1)
    inner = full[:, 128:144] + full[:, 144:160] + full[:, 160:176]
    inner = jnp.where(iota((128, 16), 0) % 8 == iota((128, 16), 1) % 8, inner, 0.0)
    inner = jnp.sum(inner.reshape(VECS, 8, 16), axis=1)
    lines = []
    for s in range(2):
        chosen = jnp.where(iota((8, 16), 1) // 8 == s, 1.0, 0.0).astype(F32)
        lines.append(nt_dot(chosen, inner, HIGH)[0:1])
    line = jnp.concatenate(lines + [jnp.zeros((1, 96), F32)], axis=1)
    rows = jnp.concatenate([gram, line, jnp.zeros((1, 128), F32)], axis=0)
    out_ref[...] = jnp.broadcast_to(rows[None], out_ref.shape)


def invert(rows):
    lane, row = iota((VECS, 128), 1), iota((VECS, 128), 0)
    wide = jnp.where(row < 8, rows[0:1], rows[1:2])
    wide = jnp.where(lane // 16 == row % 8, wide, 0.0)
    fold = jnp.where(iota((128, 128), 0) % 16 == iota((128, 128), 1), 1.0, 0.0).astype(F32)
    work = full_dot(wide, fold) + jnp.where(lane == row + VECS, 1.0, 0.0)
    for j in range(VECS):
        pivot = work[j : j + 1] / work[j : j + 1, j : j + 1]
        work = jnp.where(row == j, pivot, work - work[:, j : j + 1] * pivot)
    return pltpu.roll(work, 128 - VECS, 1)


def prepare_kernel(size_x, size_y, src_ref, *refs):
    blocks, halos, refs = refs[:BLOCKS], refs[BLOCKS : BLOCKS + 4], refs[BLOCKS + 4 :]
    m_ref, rhs_ref, fields = refs[0], refs[1], refs[2:]
    unpack_once(blocks, halos, *fields)
    x_pos, y_pos, mask = grid_mask(size_x, size_y)
    top = iota((8, 128), 0) < 4
    pick = pick_matrix(F32)
    sides = []
    for d in range(LOCAL):
        near, far = side_tile(blocks, d, 12).astype(F32), halo_side(halos, d, 12)
        near = full_dot(jnp.transpose(near), pick)[:48].reshape(6, 8, 128)
        far = full_dot(jnp.transpose(far), pick)[:48].reshape(6, 8, 128)
        sides.append((near, far))
    for c in range(3):
        for z in range(8):
            at = 2 * c + z % 2
            quarters = []
            for d in range(LOCAL):
                inner_m = induction_row(blocks, d, at)
                after, before = halo_row(halos, d, CUT + at % 3)
                if at < 3:
                    edge = jnp.where(top, after, before)
                else:
                    edge = pltpu.roll(jnp.where(top, before, after), 4, 0)
                left = jnp.concatenate([inner_m, edge], axis=0)
                right = jnp.concatenate([sides[d][0][at], sides[d][1][at]], axis=0)
                quarters.append(jnp.concatenate([left, right], axis=1))
            m_ref[c * 8 + z] = pick_layer(quarters, z)
    for s in range(2):

        def body(z, carry, s=s):
            prim = primary_field(src_ref[s], z, x_pos, y_pos, size_x, size_y)
            for c in range(3):
                at = c * 8 + z
                real = (m_ref[at] - 1.0) * WEIGHTS[c] * prim
                rhs_ref[s * 24 + at] = jnp.where(mask, real, 0.0)
            return carry

        lax.fori_loop(0, 8, body, 0)


def begin_kernel(size_x, size_y, got_ref, *refs):
    fields, m_ref, rhs_ref = refs[:4], refs[4], refs[5]
    r_ref, q_ref, inv_ref, state_ref, out_ref, side_ref, sums_ref = refs[6:]
    total = jnp.sum(got_ref[...], axis=0)
    inverse = invert(total[0:2])
    inv_ref[...] = inverse
    inner = total[2:3]
    _, _, mask = grid_mask(size_x, size_y)
    start = [solve(inverse, inner, s * VECS) for s in range(2)]
    lane = iota((VECS, 128), 1)
    state_ref[...] = jnp.where(lane == 2, start[0], jnp.where(lane == 3, start[1], 0.0))
    coeffs = [[spread(-start[s][k : k + 1]) for k in range(VECS)] for s in range(2)]

    def rhs(s, j, rows, columns):
        value = rhs_ref[s * 24 + lax.rem(j, 24), rows, columns]
        return jnp.where(j < 24, value, 0.5 * value)

    def put(rows, columns):
        def store(s, j, value):
            r_ref[s * ROWS + j, rows, columns] = value + rhs(s, j, rows, columns)

        return store

    combine_ext(
        coeffs, fields,
        put(slice(0, 8), slice(0, 128)), put(slice(8, 16), slice(0, 128)), side_ref,
    )
    for s in range(2):

        def body(j, carry, s=s):
            at = s * ROWS + j
            r_ref[at, :, 128:256] = side_ref[at] + rhs(s, j, slice(0, 16), slice(128, 256))
            return carry

        lax.fori_loop(0, ROWS, body, 0)
    apply_operator(r_ref, m_ref, q_ref, mask)
    finish_first(fields[0], r_ref, q_ref, sums_ref, out_ref)


def finish_first(c_ref, r_ref, q_ref, sums_ref, out_ref):
    sums_ref[...] = jnp.zeros_like(sums_ref)
    r, q = brick(r_ref), brick(q_ref)
    inner_all(c_ref, q, sums_ref)
    inner_pairs([(r, r), (r, q)], sums_ref, 32)
    out_ref[...] = jnp.broadcast_to(row_of_sums(sums_ref), out_ref.shape)


def first_kernel(size_x, size_y, got_ref, *refs):
    fields, refs = refs[:4], refs[4:]
    r_ref, q_ref, m_ref, inv_ref, old_ref = refs[:5]
    u_ref, a_ref, state_ref, out_ref, side_ref, sums_ref = refs[5:]
    row = jnp.sum(got_ref[...], axis=0, keepdims=True)
    _, _, mask = grid_mask(size_x, size_y)
    lane = iota((VECS, 128), 1)
    state = old_ref[...]
    coeffs, q_scale, r_scale = [], [], []
    for s in range(2):
        rr, rq = entry(row, 32 + 2 * s), entry(row, 33 + 2 * s)
        beta = jnp.sqrt(rr + EPS)
        g_zero = solve(inv_ref[...], row, s * VECS) / beta
        h_00 = rq / (beta * beta)
        coeffs.append([spread(-g_zero[k : k + 1]) for k in range(VECS)])
        q_scale.append(spread(1.0 / beta))
        r_scale.append(spread(-h_00 / beta))
        state = jnp.where(lane == s, g_zero, state)
        state = jnp.where(lane == 8 + s, beta, state)
        state = jnp.where(lane == 10 + s, h_00, state)
        state = jnp.where(lane == 12 + s, rr, state)
    state_ref[...] = state

    def put(rows, columns):
        def store(s, j, value):
            at = s * ROWS + j
            value = value + q_scale[s] * q_ref[at, rows, columns]
            u_ref[at, rows, columns] = value + r_scale[s] * r_ref[at, rows, columns]

        return store

    combine_ext(
        coeffs, fields,
        put(slice(0, 8), slice(0, 128)), put(slice(8, 16), slice(0, 128)), side_ref,
    )
    for s in range(2):

        def body(j, carry, s=s):
            at = s * ROWS + j
            value = side_ref[at]
            for half in range(2):
                rows = slice(half * 8, half * 8 + 8)
                new = value[rows] + q_scale[s] * q_ref[at, rows, 128:256]
                u_ref[at, rows, 128:256] = new + r_scale[s] * r_ref[at, rows, 128:256]
            return carry

        lax.fori_loop(0, ROWS, body, 0)
    apply_operator(u_ref, m_ref, a_ref, mask)
    sums_ref[...] = jnp.zeros_like(sums_ref)
    r, u, a = brick(r_ref), brick(u_ref), brick(a_ref)
    inner_all(fields[0], a, sums_ref)
    inner_pairs([(u, u), (r, u), (r, a), (u, a), (a, a)], sums_ref, 32)
    out_ref[...] = jnp.broadcast_to(row_of_sums(sums_ref), out_ref.shape)


def close_cycle(row, inverse, state, s):
    uu, ru, ra, ua, aa = [entry(row, 32 + 5 * s + i) for i in range(5)]
    g_zero = state[:, s : s + 1]
    beta, h_00, rr = [state[0:1, first + s : first + s + 1] for first in (8, 10, 12)]
    h_10 = jnp.sqrt(uu + EPS)
    inner = column_of(row, s * VECS) / h_10
    g_one = solve(inverse, row, s * VECS) / h_10
    h_01 = ra / (beta * h_10)
    h_11 = ua / (h_10 * h_10)
    left = aa / (h_10 * h_10) - jnp.sum(g_one * inner, axis=0, keepdims=True)
    left = left - 2.0 * (h_01 * h_01 + h_11 * h_11)
    left = left + h_01 * h_01 * (rr / (beta * beta)) + h_11 * h_11 * (uu / (h_10 * h_10))
    left = left + 2.0 * h_01 * h_11 * (ru / (beta * h_10))
    h_21_square = jnp.maximum(left, 0.0) + EPS
    n_00 = h_00 * h_00 + h_10 * h_10
    n_01 = h_00 * h_01 + h_10 * h_11
    n_11 = h_01 * h_01 + h_11 * h_11 + h_21_square
    l_00 = jnp.sqrt(n_00)
    l_10 = n_01 / l_00
    l_11 = jnp.sqrt(n_11 - l_10 * l_10)
    z_0 = beta * h_00 / l_00
    z_1 = (beta * h_01 - l_10 * z_0) / l_11
    y_1 = z_1 / l_11
    y_0 = (z_0 - l_10 * y_1) / l_00
    t_0 = beta - h_00 * y_0 - h_01 * y_1
    t_1 = -h_10 * y_0 - h_11 * y_1
    return {
        "r": (t_0 + y_1 * h_01) / beta,
        "u": (t_1 + y_1 * h_11) / h_10,
        "a": -y_1 / h_10,
        "c": y_1 * g_one,
        "sol_r": y_0 / beta,
        "sol_u": y_1 / h_10,
        "basis": state[:, 2 + s : 3 + s] - g_zero * y_0 - g_one * y_1,
    }


def next_kernel(size_x, size_y, got_ref, *refs):
    fields, refs = refs[:4], refs[4:]
    r_ref, u_ref, a_ref, m_ref, inv_ref, old_ref = refs[:6]
    new_ref, q_ref, sol_ref, state_ref, out_ref, side_ref, sums_ref = refs[6:]
    row = jnp.sum(got_ref[...], axis=0, keepdims=True)
    _, _, mask = grid_mask(size_x, size_y)
    state = old_ref[...]
    small = [close_cycle(row, inv_ref[...], state, s) for s in range(2)]
    lane = iota((VECS, 128), 1)
    state_ref[...] = jnp.where(
        lane == 2, small[0]["basis"], jnp.where(lane == 3, small[1]["basis"], 0.0)
    )
    coeffs = [[spread(small[s]["c"][k : k + 1]) for k in range(VECS)] for s in range(2)]
    scale = [{name: spread(small[s][name]) for name in ("r", "u", "a", "sol_r", "sol_u")} for s in range(2)]

    def total(s, at, rows, columns, value):
        value = value + scale[s]["r"] * r_ref[at, rows, columns]
        value = value + scale[s]["u"] * u_ref[at, rows, columns]
        return value + scale[s]["a"] * a_ref[at, rows, columns]

    def put(rows, columns):
        def store(s, j, value):
            at = s * ROWS + j
            new_ref[at, rows, columns] = total(s, at, rows, columns, value)

        return store

    combine_ext(
        coeffs, fields,
        put(slice(0, 8), slice(0, 128)), put(slice(8, 16), slice(0, 128)), side_ref,
    )
    for s in range(2):

        def body(j, carry, s=s):
            at = s * ROWS + j
            value = side_ref[at]
            for half in range(2):
                rows = slice(half * 8, half * 8 + 8)
                new_ref[at, rows, 128:256] = total(s, at, rows, slice(128, 256), value[rows])
            sol_ref[at] = (
                scale[s]["sol_r"] * r_ref[at, 0:8, 0:128]
                + scale[s]["sol_u"] * u_ref[at, 0:8, 0:128]
            )
            return carry

        lax.fori_loop(0, ROWS, body, 0)
    apply_operator(new_ref, m_ref, q_ref, mask)
    finish_first(fields[0], new_ref, q_ref, sums_ref, out_ref)


def basis_row(basis, d, kl, j):
    row = kl * ROWS + j
    if d == 0:
        return basis[0][row].astype(F32)
    first = {1: 1, 3: 3, 2: 5}[d]
    return basis[first][row].astype(F32) if kl < 2 else basis[first + 1][row - CUT].astype(F32)


def last_kernel(got_ref, c_ref, *refs):
    basis, refs = refs[:7], refs[7:]
    r_ref, u_ref, a_ref, inv_ref, old_ref, sol_ref = refs[:6]
    solution_ref, residual_ref = refs[6:]
    row = jnp.sum(got_ref[...], axis=0, keepdims=True)
    state = old_ref[...]
    small = [close_cycle(row, inv_ref[...], state, s) for s in range(2)]
    coeffs = [[spread(one["c"][k : k + 1]) for k in range(VECS)] for one in small]
    basis_coeffs = [[spread(one["basis"][k : k + 1]) for k in range(VECS)] for one in small]
    names = ("r", "u", "a", "sol_r", "sol_u")
    scale = [{name: spread(one[name]) for name in names} for one in small]

    def residual_body(step, carry):
        rows = [step * AT_ONCE + i for i in range(AT_ONCE)]
        values = [[], []]
        for s in range(2):
            for j in rows:
                r, u, a = brick(r_ref)(s, j), brick(u_ref)(s, j), brick(a_ref)(s, j)
                values[s].append(scale[s]["r"] * r + scale[s]["u"] * u + scale[s]["a"] * a)
        for k in range(VECS):
            for i, j in enumerate(rows):
                vec = c_ref[k * ROWS + j]
                for s in range(2):
                    values[s][i] = values[s][i] + coeffs[s][k] * vec
        for s in range(2):
            for i, j in enumerate(rows):
                residual_ref[s * ROWS + j] = values[s][i]
        return carry

    def solution_body(step, carry):
        rows = [step * AT_ONCE + i for i in range(AT_ONCE)]
        values = [[], []]
        for s in range(2):
            for j in rows:
                r, u = brick(r_ref)(s, j), brick(u_ref)(s, j)
                old = sol_ref[s * ROWS + j]
                values[s].append(old + scale[s]["sol_r"] * r + scale[s]["sol_u"] * u)
        for d in range(LOCAL):
            for kl in range(LOCAL):
                for i, j in enumerate(rows):
                    vec = basis_row(basis, d, kl, j)
                    for s in range(2):
                        values[s][i] = values[s][i] + basis_coeffs[s][d * LOCAL + kl] * vec
        for s in range(2):
            for i, j in enumerate(rows):
                solution_ref[s * ROWS + j] = values[s][i]
        return carry

    lax.fori_loop(0, ROWS // AT_ONCE, residual_body, 0)
    lax.fori_loop(0, ROWS // AT_ONCE, solution_body, 0)


def call(kernel, outs, args, scratch=(), smem=0):
    vmem = pl.BlockSpec(memory_space=pltpu.VMEM)
    return pl.pallas_call(
        kernel,
        out_shape=outs,
        in_specs=[pl.BlockSpec(memory_space=pltpu.SMEM)] * smem + [vmem] * (len(args) - smem),
        out_specs=jax.tree.map(lambda _: vmem, outs),
        scratch_shapes=list(scratch),
        compiler_params=pltpu.CompilerParams(vmem_limit_bytes=20 * 1024 * 1024),
    )(*args)


def shape(*dims, dtype=F32):
    return jax.ShapeDtypeStruct(dims, dtype)


def exchange(value):
    return lax.all_to_all(value, ("gx", "gy"), 0, 0)


def steps(axis, wrap=False):
    size = lax.axis_size(axis)
    up = [(i, (i + 1) % size) for i in range(size if wrap else size - 1)]
    return up, [(j, i) for i, j in up]


def tied(first, *rest):
    return lax.optimization_barrier((first, *rest))


def on_device(src_cell, basis, images, induction):
    size_x, size_y = 8 * lax.axis_size("gx"), 128 * lax.axis_size("gy")
    peers = lax.axis_size("gx") * lax.axis_size("gy")
    right, left = steps("tx", wrap=True)
    block = jnp.concatenate(
        [images.reshape(LOCAL * ROWS, 8, 128), induction.reshape(6, 8, 128)], axis=0
    )
    own = call(pack_y_kernel, shape(PACKED, 8, 128, dtype=BF16), (block,))
    one = lax.ppermute(block, "tx", right)
    three = lax.ppermute(block, "tx", left)
    up, down = steps("gy")
    after, before = lax.ppermute(own, "gy", down), lax.ppermute(own, "gy", up)
    side = jnp.where(lax.broadcasted_iota(jnp.int32, own.shape, 1) < 4, after, before)
    far_side = lax.ppermute(side, "tx", [(i, (i + 2) % LOCAL) for i in range(LOCAL)])
    far_side, one, three = tied(far_side, one, three)
    far_low = lax.ppermute(jnp.concatenate([one[:CUT], side]), "tx", right)
    far_high = lax.ppermute(jnp.concatenate([three[CUT:], side]), "tx", left)
    up, down = steps("gx")

    def exchange_x(group, sides, sources):
        count = len(group) * HALF + len(sides) * PACKED
        half = shape(count, 8, 128, dtype=BF16)
        low, high = call(functools.partial(pack_x_kernel, group, sides), (half, half), sources)
        return lax.ppermute(low, "gx", down), lax.ppermute(high, "gx", up)

    early = exchange_x(EARLY, EARLY_SIDES, (block, one, three, side, side, side))
    blocks = (block, one, three, far_low, far_high, side, far_side)

    late = exchange_x(LATE, LATE_SIDES, blocks)

    sums = pltpu.VMEM((128, 128), F32)
    side_scratch = pltpu.VMEM((2 * ROWS, 16, 128), F32)
    sent = call(
        functools.partial(gram_kernel, size_x, size_y),
        shape(peers, 4, 128),
        (src_cell, *blocks),
        (pltpu.VMEM((ROWS, 16, 128), F32), pltpu.VMEM((8 * VECS + 48, ROWS * 128), BF16)),
        smem=1,
    )
    got = exchange(sent)
    whole, tiles = shape(VECS * ROWS, 8, 128), shape(3 * VECS, 8, 128)
    m, rhs, *fields = call(
        functools.partial(prepare_kernel, size_x, size_y),
        (shape(24, 16, 256), shape(ROWS, 16, 256), whole, whole, tiles, tiles),
        (src_cell, *blocks, *early, *late),
        smem=1,
    )
    wide = shape(2 * ROWS, 16, 256)
    line = shape(peers, 128)
    small = shape(VECS, 128)
    own_basis = basis.reshape(LOCAL * ROWS, 8, 128)

    def total(value):
        return exchange(value.reshape(peers, 1, 128)).reshape(peers, 128)

    got, piece = tied(got, own_basis[:CUT])
    one_low, three_low = lax.ppermute(piece, "tx", right), lax.ppermute(piece, "tx", left)
    r, q, inverse, state, sent = call(
        functools.partial(begin_kernel, size_x, size_y),
        (wide, wide, small, small, line),
        (got, *fields, m, rhs),
        (side_scratch, sums),
    )

    def first(r, q, state, got):
        return call(
            functools.partial(first_kernel, size_x, size_y),
            (wide, wide, small, line),
            (got, *fields, r, q, m, inverse, state),
            (side_scratch, sums),
        )

    sent, one_low, three_low = tied(sent, one_low, three_low)
    got, piece = tied(total(sent), own_basis[CUT:])
    one_high, three_high = lax.ppermute(piece, "tx", right), lax.ppermute(piece, "tx", left)
    u, a, state, sent = first(r, q, state, got)
    sent, one_high, three_high = tied(sent, one_high, three_high)
    got, one_low, three_high = tied(total(sent), one_low, three_high)
    two_low, two_high = lax.ppermute(one_low, "tx", right), lax.ppermute(three_high, "tx", left)
    r, q, field, state, sent = call(
        functools.partial(next_kernel, size_x, size_y),
        (wide, wide, shape(2 * ROWS, 8, 128), small, line),
        (got, *fields, r, u, a, m, inverse, state),
        (side_scratch, sums),
    )
    sent, two_low, two_high = tied(sent, two_low, two_high)
    u, a, state, sent = first(r, q, state, total(sent))
    bases = (own_basis, one_low, one_high, three_low, three_high, two_low, two_high)
    narrow = shape(2 * ROWS, 8, 128)
    field, residual = call(
        last_kernel,
        (narrow, narrow),
        (total(sent), fields[0], *bases, r, u, a, inverse, state, field),
    )
    full = (2, 2, 3, 8, 8, 128)
    return field.reshape(full), residual.reshape(full)


def solution(mesh):
    in_specs = (
        P("tx"),
        P("tx", None, None, None, "gx", "gy"),
        P("tx", None, None, None, "gx", "gy"),
        P(None, "tx", "gx", "gy"),
    )
    out_specs = (P("tx", None, None, None, "gx", "gy"), P("tx", None, None, None, "gx", "gy"))
    return jax.shard_map(
        on_device, mesh=mesh, in_specs=in_specs, out_specs=out_specs, check_vma=False
    )
```

```python
import functools

import jax
import jax.numpy as jnp
from jax import lax
from jax.experimental import pallas as pl
from jax.experimental.pallas import tpu as pltpu
from jax.sharding import PartitionSpec as P

EPS = 1e-06
VECS = 16
LOCAL = 4
ROWS = 48
BLOCK = 198
HALF = 99
PACKED = 13
WEIGHTS = (1.0, 0.5, 0.25)
AT_ONCE = 4
HIGH = lax.Precision.HIGHEST
F32 = jnp.float32
BF16 = jnp.bfloat16


def iota(shape, axis):
    return lax.broadcasted_iota(jnp.int32, shape, axis)


def pick_matrix(dtype):
    col = iota((8, 128), 0)
    lane = iota((8, 128), 1)
    return jnp.where(lane == jnp.where(col < 4, col, col + 120), 1.0, 0.0).astype(dtype)


def nt_dot(left, right, precision=None):
    return lax.dot_general(
        left, right, (((1,), (1,)), ((), ())), precision=precision, preferred_element_type=F32
    )


def full_dot(left, right):
    return lax.dot_general(
        left, right, (((1,), (0,)), ((), ())), precision=HIGH, preferred_element_type=F32
    )


BLOCKS = 7
CUT = 2 * ROWS


def vector_row(blocks, d, kl, j):
    row = kl * ROWS + j
    if d != 2:
        return blocks[(0, 1, None, 2)[d]][row].astype(F32)
    return blocks[3][row].astype(F32) if kl < 2 else blocks[4][row - CUT].astype(F32)


def induction_row(blocks, d, at):
    if d != 2:
        return blocks[(0, 1, None, 2)[d]][LOCAL * ROWS + at].astype(F32)
    return blocks[4][LOCAL * ROWS - CUT + at].astype(F32)


def side_tile(blocks, d, tile):
    ref, first = ((5, 0), (3, CUT), (6, 0), (4, BLOCK - CUT))[d]
    return blocks[ref][first + tile]


def pack_y_kernel(block_ref, out_ref):
    pick = pick_matrix(BF16)
    for tile in range(PACKED):
        first = tile * 16
        count = min(16, BLOCK - first)
        rows = block_ref[first : first + count].astype(F32).reshape(count * 8, 128).astype(BF16)
        picked = nt_dot(pick, rows)
        if count < 16:
            picked = jnp.concatenate([picked, jnp.zeros((8, 128 - count * 8), F32)], axis=1)
        out_ref[tile] = picked.astype(BF16)


EARLY, LATE = (0, 1, 3), (2,)
EARLY_SIDES, LATE_SIDES = (0,), (1, 2, 3)


def halo_row(halos, d, row):
    ref = 2 if d == 2 else 0
    at = (0 if d == 2 else EARLY.index(d)) * HALF + row
    return halos[ref][at].astype(F32), halos[ref + 1][at].astype(F32)


def halo_side(halos, d, tile):
    ref = 0 if d == 0 else 2
    at = (len(EARLY) * HALF if d == 0 else HALF + LATE_SIDES.index(d) * PACKED) + tile
    after, before = halos[ref][at].astype(F32), halos[ref + 1][at].astype(F32)
    return jnp.where(iota((8, 128), 1) % 8 < 4, after, before)


def pack_x_kernel(group, sides, *refs):
    blocks, (lo_ref, hi_ref) = refs[:-2], refs[-2:]
    top = iota((8, 128), 0) < 4

    def pair(one, two, at):
        two = pltpu.roll(two, 4, 0)
        lo_ref[at] = jnp.where(top, one, two).astype(BF16)
        hi_ref[at] = jnp.where(top, two, one).astype(BF16)

    def body(j, carry):
        for place, d in enumerate(group):
            for kl in range(2):
                pair(
                    vector_row(blocks, d, kl, j),
                    vector_row(blocks, d, kl + 2, j),
                    place * HALF + kl * ROWS + j,
                )
        return carry

    lax.fori_loop(0, ROWS, body, 0)
    for place, d in enumerate(group):
        for i in range(3):
            pair(
                induction_row(blocks, d, i),
                induction_row(blocks, d, i + 3),
                place * HALF + CUT + i,
            )
    for place, d in enumerate(sides):
        for tile in range(PACKED):
            piece = side_tile(blocks, d, tile)
            lo_ref[len(group) * HALF + place * PACKED + tile] = piece
            hi_ref[len(group) * HALF + place * PACKED + tile] = piece


def inner_all(c_ref, field, sums_ref):
    def body(step, accs):
        accs = list(accs)
        for j in (2 * step, 2 * step + 1):
            one, two = field(0, j), field(1, j)
            for k in range(VECS):
                vec = c_ref[k * ROWS + j]
                accs[2 * k] = accs[2 * k] + vec * one
                accs[2 * k + 1] = accs[2 * k + 1] + vec * two
        return tuple(accs)

    zero = jnp.zeros((8, 128), F32)
    accs = lax.fori_loop(0, ROWS // 2, body, (zero,) * (2 * VECS))
    for k in range(VECS):
        for s in range(2):
            sums_ref[s * VECS + k : s * VECS + k + 1] = jnp.sum(
                accs[2 * k + s], axis=0, keepdims=True
            )


def inner_pairs(pairs, sums_ref, first):
    count = len(pairs)

    def body(step, accs):
        new = []
        for s in range(2):
            for i, (one, two) in enumerate(pairs):
                acc = accs[s * count + i]
                for row in range(AT_ONCE):
                    j = step * AT_ONCE + row
                    acc = acc + one(s, j) * two(s, j)
                new.append(acc)
        return tuple(new)

    accs = lax.fori_loop(0, ROWS // AT_ONCE, body, (jnp.zeros((8, 128), F32),) * (2 * count))
    for i, acc in enumerate(accs):
        sums_ref[first + i : first + i + 1] = jnp.sum(acc, axis=0, keepdims=True)


def row_of_sums(sums_ref):
    return nt_dot(jnp.ones((8, 128), F32), sums_ref[...], HIGH)[0:1]


def entry(row, lane):
    return row[:, lane : lane + 1]


def column_of(row, first):
    part = row[:, first : first + VECS]
    eye = iota((VECS, VECS), 0) == iota((VECS, VECS), 1)
    return jnp.sum(jnp.where(eye, part, 0.0), axis=1, keepdims=True)


def solve(inverse, row, first):
    return jnp.sum(inverse[:, :VECS] * row[:, first : first + VECS], axis=1, keepdims=True)


def spread(value):
    return jnp.broadcast_to(value, (8, 128))


def grid_mask(size_x, size_y):
    row, lane = iota((16, 256), 0), iota((16, 256), 1)
    x_pos = lax.axis_index("gx") * 8 + jnp.where(row < 12, row, row - 16)
    y_pos = lax.axis_index("gy") * 128 + jnp.where(lane < 132, lane, lane - 256)
    inside = (x_pos >= 0) & (x_pos < size_x) & (y_pos >= 0) & (y_pos < size_y)
    inside = inside & ((lane < 132) | (lane >= 252))
    return x_pos, y_pos, inside


def primary_field(cell, z, x_pos, y_pos, size_x, size_y):
    plane = size_x * size_y
    src_z = cell // plane
    rest = cell % plane
    d_z = (z - src_z).astype(F32)
    d_x = (x_pos - rest // size_y).astype(F32)
    d_y = (y_pos - rest % size_y).astype(F32)
    dist = jnp.sqrt(d_z * d_z + d_x * d_x + d_y * d_y)
    return jnp.exp(-dist / ((size_x + size_y) / 8.0))


def unpack_once(blocks, halos, c_ref, x_ref, near_ref, far_ref):
    top = iota((8, 128), 0) < 4

    def body(j, carry):
        for d in range(LOCAL):
            for kl in range(LOCAL):
                k = d * LOCAL + kl
                c_ref[k * ROWS + j] = vector_row(blocks, d, kl, j)
                after, before = halo_row(halos, d, (kl % 2) * ROWS + j)
                if kl < 2:
                    x_ref[k * ROWS + j] = jnp.where(top, after, before)
                else:
                    x_ref[k * ROWS + j] = pltpu.roll(jnp.where(top, before, after), 4, 0)
        return carry

    lax.fori_loop(0, ROWS, body, 0, unroll=2)
    for d in range(LOCAL):
        for t in range(PACKED - 1):
            near_ref[d * 12 + t] = side_tile(blocks, d, t).astype(F32)
            far_ref[d * 12 + t] = halo_side(halos, d, t)


def plus(total, term):
    return term if total is None else total + term


def combine_ext(coeffs, fields, interior, halo_x, unpacked_ref):
    c_ref, x_ref, near_ref, far_ref = fields

    def body(step, carry):
        rows = [step * AT_ONCE + i for i in range(AT_ONCE)]
        inner = [[None] * AT_ONCE, [None] * AT_ONCE]
        outer = [[None] * AT_ONCE, [None] * AT_ONCE]
        for k in range(VECS):
            for i, j in enumerate(rows):
                vec, edge = c_ref[k * ROWS + j], x_ref[k * ROWS + j]
                for s in range(2):
                    inner[s][i] = plus(inner[s][i], coeffs[s][k] * vec)
                    outer[s][i] = plus(outer[s][i], coeffs[s][k] * edge)
        for i, j in enumerate(rows):
            for s in range(2):
                interior(s, j, inner[s][i])
                halo_x(s, j, outer[s][i])
        return carry

    lax.fori_loop(0, ROWS // AT_ONCE, body, 0)
    pick = pick_matrix(F32)
    for s in range(2):
        for tile in range(3):
            near = jnp.zeros((8, 128), F32)
            far = jnp.zeros((8, 128), F32)
            for k in range(VECS):
                near = near + coeffs[s][k] * near_ref[k * 3 + tile]
                far = far + coeffs[s][k] * far_ref[k * 3 + tile]
            place = s * ROWS + tile * 16
            near = full_dot(jnp.transpose(near), pick).reshape(16, 8, 128)
            far = full_dot(jnp.transpose(far), pick).reshape(16, 8, 128)
            unpacked_ref[place : place + 16, 0:8] = near
            unpacked_ref[place : place + 16, 8:16] = far


def apply_operator(e_ref, m_ref, out_ref, mask):
    def ahead(f, axis):
        return pltpu.roll(f, f.shape[axis] - 1, axis)

    def behind(f, axis):
        return pltpu.roll(f, 1, axis)

    def body(index, carry):
        base = index * 24
        other = jnp.where(index % 2 == 0, base + 24, base - 24)
        sign = jnp.where(index % 2 == 0, -1.0, 1.0).astype(F32)
        zero = jnp.zeros((16, 256), F32)
        b_x_old = -e_ref[base + 8]
        b_y_old = e_ref[base]
        for z in range(8):
            e_x, e_y, e_z = e_ref[base + z], e_ref[base + 8 + z], e_ref[base + 16 + z]
            up_x = e_ref[base + z + 1] if z < 7 else zero
            up_y = e_ref[base + 8 + z + 1] if z < 7 else zero
            b_x = (ahead(e_z, 1) - e_z) - (up_y - e_y)
            b_y = (up_x - e_x) - (ahead(e_z, 0) - e_z)
            b_z = (ahead(e_y, 0) - e_y) - (ahead(e_x, 1) - e_x)
            c_x = (b_z - behind(b_z, 1)) - (b_y - b_y_old)
            c_y = (b_x - b_x_old) - (b_z - behind(b_z, 0))
            c_z = (b_y - behind(b_y, 0)) - (b_x - behind(b_x, 1))
            for c, value in enumerate((c_x, c_y, c_z)):
                at = c * 8 + z
                value = value + sign * (m_ref[at] * e_ref[other + at])
                out_ref[base + at] = jnp.where(mask, value, 0.0)
            b_x_old, b_y_old = b_x, b_y
        return carry

    lax.fori_loop(0, 4, body, 0)


def brick(ref):
    return lambda s, j: ref[s * ROWS + j, 0:8, 0:128]


def pick_layer(values, z):
    want = lax.rem(lax.axis_index("tx") - z // 2 + LOCAL, LOCAL)
    result = values[0]
    for d in range(1, LOCAL):
        result = jnp.where(want == d, values[d], result)
    return result


def gram_kernel(size_x, size_y, src_ref, *refs):
    blocks, out_ref, field_ref, rows_ref = refs[:BLOCKS], *refs[BLOCKS:]
    x_pos = lax.axis_index("gx") * 8 + iota((8, 128), 0)
    y_pos = lax.axis_index("gy") * 128 + iota((8, 128), 1)
    for z in range(8):
        prim = [
            primary_field(src_ref[s], z, x_pos, y_pos, size_x, size_y) for s in range(2)
        ]
        for c in range(3):
            m = pick_layer([induction_row(blocks, d, 2 * c + z % 2) for d in range(LOCAL)], z)
            for s in range(2):
                real = (m - 1.0) * WEIGHTS[c] * prim[s]
                field_ref[c * 8 + z, s * 8 : s * 8 + 8] = real
                field_ref[24 + c * 8 + z, s * 8 : s * 8 + 8] = 0.5 * real

    def body(j, carry):
        columns = pl.ds(pl.multiple_of(j * 128, 128), 128)
        for pair in range(VECS // 2):
            d, kl = pair // 2, 2 * (pair % 2)
            both = [vector_row(blocks, d, kl + i, j) for i in range(2)]
            rows_ref[16 * pair : 16 * pair + 16, columns] = jnp.concatenate(both).astype(BF16)
        rest = field_ref[j]
        for piece in range(3):
            part = rest.astype(BF16)
            rest = rest - part.astype(F32)
            first = 8 * VECS + 16 * piece
            rows_ref[first : first + 16, columns] = part
        return carry

    lax.fori_loop(0, ROWS, body, 0)
    full = nt_dot(rows_ref[0:128], rows_ref[...])
    row, lane = iota((128, 128), 0), iota((128, 128), 1)
    gram = jnp.where(row % 8 == lane % 8, full[:, 0:128], 0.0).reshape(VECS, 8, 128)
    gram = jnp.sum(gram, axis=1)
    gram = full_dot(gram, jnp.where(row // 8 == lane % 16, 1.0, 0.0).astype(F32))
    gram = jnp.where(iota((VECS, 128), 1) // 16 == iota((VECS, 128), 0) % 8, gram, 0.0)
    gram = jnp.sum(gram.reshape(2, 8, 128), axis=1)
    inner = full[:, 128:144] + full[:, 144:160] + full[:, 160:176]
    inner = jnp.where(iota((128, 16), 0) % 8 == iota((128, 16), 1) % 8, inner, 0.0)
    inner = jnp.sum(inner.reshape(VECS, 8, 16), axis=1)
    lines = []
    for s in range(2):
        chosen = jnp.where(iota((8, 16), 1) // 8 == s, 1.0, 0.0).astype(F32)
        lines.append(nt_dot(chosen, inner, HIGH)[0:1])
    line = jnp.concatenate(lines + [jnp.zeros((1, 96), F32)], axis=1)
    rows = jnp.concatenate([gram, line, jnp.zeros((1, 128), F32)], axis=0)
    out_ref[...] = jnp.broadcast_to(rows[None], out_ref.shape)


def invert(rows):
    lane, row = iota((VECS, 128), 1), iota((VECS, 128), 0)
    wide = jnp.where(row < 8, rows[0:1], rows[1:2])
    wide = jnp.where(lane // 16 == row % 8, wide, 0.0)
    fold = jnp.where(iota((128, 128), 0) % 16 == iota((128, 128), 1), 1.0, 0.0).astype(F32)
    work = full_dot(wide, fold) + jnp.where(lane == row + VECS, 1.0, 0.0)
    for j in range(VECS):
        pivot = work[j : j + 1] / work[j : j + 1, j : j + 1]
        work = jnp.where(row == j, pivot, work - work[:, j : j + 1] * pivot)
    return pltpu.roll(work, 128 - VECS, 1)


def prepare_kernel(size_x, size_y, src_ref, *refs):
    blocks, halos, refs = refs[:BLOCKS], refs[BLOCKS : BLOCKS + 4], refs[BLOCKS + 4 :]
    m_ref, rhs_ref, fields = refs[0], refs[1], refs[2:]
    unpack_once(blocks, halos, *fields)
    x_pos, y_pos, mask = grid_mask(size_x, size_y)
    top = iota((8, 128), 0) < 4
    pick = pick_matrix(F32)
    sides = []
    for d in range(LOCAL):
        near, far = side_tile(blocks, d, 12).astype(F32), halo_side(halos, d, 12)
        near = full_dot(jnp.transpose(near), pick)[:48].reshape(6, 8, 128)
        far = full_dot(jnp.transpose(far), pick)[:48].reshape(6, 8, 128)
        sides.append((near, far))
    for c in range(3):
        for z in range(8):
            at = 2 * c + z % 2
            quarters = []
            for d in range(LOCAL):
                inner_m = induction_row(blocks, d, at)
                after, before = halo_row(halos, d, CUT + at % 3)
                if at < 3:
                    edge = jnp.where(top, after, before)
                else:
                    edge = pltpu.roll(jnp.where(top, before, after), 4, 0)
                left = jnp.concatenate([inner_m, edge], axis=0)
                right = jnp.concatenate([sides[d][0][at], sides[d][1][at]], axis=0)
                quarters.append(jnp.concatenate([left, right], axis=1))
            m_ref[c * 8 + z] = pick_layer(quarters, z)
    for s in range(2):

        def body(z, carry, s=s):
            prim = primary_field(src_ref[s], z, x_pos, y_pos, size_x, size_y)
            for c in range(3):
                at = c * 8 + z
                real = (m_ref[at] - 1.0) * WEIGHTS[c] * prim
                rhs_ref[s * 24 + at] = jnp.where(mask, real, 0.0)
            return carry

        lax.fori_loop(0, 8, body, 0)


def begin_kernel(size_x, size_y, got_ref, *refs):
    fields, m_ref, rhs_ref = refs[:4], refs[4], refs[5]
    r_ref, q_ref, inv_ref, state_ref, out_ref, side_ref, sums_ref = refs[6:]
    total = jnp.sum(got_ref[...], axis=0)
    inverse = invert(total[0:2])
    inv_ref[...] = inverse
    inner = total[2:3]
    _, _, mask = grid_mask(size_x, size_y)
    start = [solve(inverse, inner, s * VECS) for s in range(2)]
    lane = iota((VECS, 128), 1)
    state_ref[...] = jnp.where(lane == 2, start[0], jnp.where(lane == 3, start[1], 0.0))
    coeffs = [[spread(-start[s][k : k + 1]) for k in range(VECS)] for s in range(2)]

    def rhs(s, j, rows, columns):
        value = rhs_ref[s * 24 + lax.rem(j, 24), rows, columns]
        return jnp.where(j < 24, value, 0.5 * value)

    def put(rows, columns):
        def store(s, j, value):
            r_ref[s * ROWS + j, rows, columns] = value + rhs(s, j, rows, columns)

        return store

    combine_ext(
        coeffs, fields,
        put(slice(0, 8), slice(0, 128)), put(slice(8, 16), slice(0, 128)), side_ref,
    )
    for s in range(2):

        def body(step, carry, s=s):
            for i in range(AT_ONCE):
                j = step * AT_ONCE + i
                at = s * ROWS + j
                r_ref[at, :, 128:256] = side_ref[at] + rhs(s, j, slice(0, 16), slice(128, 256))
            return carry

        lax.fori_loop(0, ROWS // AT_ONCE, body, 0)
    apply_operator(r_ref, m_ref, q_ref, mask)
    finish_first(fields[0], r_ref, q_ref, sums_ref, out_ref)


def finish_first(c_ref, r_ref, q_ref, sums_ref, out_ref):
    sums_ref[...] = jnp.zeros_like(sums_ref)
    r, q = brick(r_ref), brick(q_ref)
    inner_all(c_ref, q, sums_ref)
    inner_pairs([(r, r), (r, q)], sums_ref, 32)
    out_ref[...] = jnp.broadcast_to(row_of_sums(sums_ref), out_ref.shape)


def first_kernel(size_x, size_y, got_ref, *refs):
    fields, refs = refs[:4], refs[4:]
    r_ref, q_ref, m_ref, inv_ref, old_ref = refs[:5]
    u_ref, a_ref, state_ref, out_ref, side_ref, sums_ref = refs[5:]
    row = jnp.sum(got_ref[...], axis=0, keepdims=True)
    _, _, mask = grid_mask(size_x, size_y)
    lane = iota((VECS, 128), 1)
    state = old_ref[...]
    coeffs, q_scale, r_scale = [], [], []
    for s in range(2):
        rr, rq = entry(row, 32 + 2 * s), entry(row, 33 + 2 * s)
        beta = jnp.sqrt(rr + EPS)
        g_zero = solve(inv_ref[...], row, s * VECS) / beta
        h_00 = rq / (beta * beta)
        coeffs.append([spread(-g_zero[k : k + 1]) for k in range(VECS)])
        q_scale.append(spread(1.0 / beta))
        r_scale.append(spread(-h_00 / beta))
        state = jnp.where(lane == s, g_zero, state)
        state = jnp.where(lane == 8 + s, beta, state)
        state = jnp.where(lane == 10 + s, h_00, state)
        state = jnp.where(lane == 12 + s, rr, state)
    state_ref[...] = state

    def put(rows, columns):
        def store(s, j, value):
            at = s * ROWS + j
            value = value + q_scale[s] * q_ref[at, rows, columns]
            u_ref[at, rows, columns] = value + r_scale[s] * r_ref[at, rows, columns]

        return store

    combine_ext(
        coeffs, fields,
        put(slice(0, 8), slice(0, 128)), put(slice(8, 16), slice(0, 128)), side_ref,
    )
    for s in range(2):

        def body(step, carry, s=s):
            for i in range(AT_ONCE):
                at = s * ROWS + step * AT_ONCE + i
                for half in range(2):
                    rows = slice(half * 8, half * 8 + 8)
                    new = side_ref[at, rows] + q_scale[s] * q_ref[at, rows, 128:256]
                    u_ref[at, rows, 128:256] = new + r_scale[s] * r_ref[at, rows, 128:256]
            return carry

        lax.fori_loop(0, ROWS // AT_ONCE, body, 0)
    apply_operator(u_ref, m_ref, a_ref, mask)
    sums_ref[...] = jnp.zeros_like(sums_ref)
    r, u, a = brick(r_ref), brick(u_ref), brick(a_ref)
    inner_all(fields[0], a, sums_ref)
    inner_pairs([(u, u), (r, u), (r, a), (u, a), (a, a)], sums_ref, 32)
    out_ref[...] = jnp.broadcast_to(row_of_sums(sums_ref), out_ref.shape)


def close_cycle(row, inverse, state, s):
    uu, ru, ra, ua, aa = [entry(row, 32 + 5 * s + i) for i in range(5)]
    g_zero = state[:, s : s + 1]
    beta, h_00, rr = [state[0:1, first + s : first + s + 1] for first in (8, 10, 12)]
    h_10 = jnp.sqrt(uu + EPS)
    inner = column_of(row, s * VECS) / h_10
    g_one = solve(inverse, row, s * VECS) / h_10
    h_01 = ra / (beta * h_10)
    h_11 = ua / (h_10 * h_10)
    left = aa / (h_10 * h_10) - jnp.sum(g_one * inner, axis=0, keepdims=True)
    left = left - 2.0 * (h_01 * h_01 + h_11 * h_11)
    left = left + h_01 * h_01 * (rr / (beta * beta)) + h_11 * h_11 * (uu / (h_10 * h_10))
    left = left + 2.0 * h_01 * h_11 * (ru / (beta * h_10))
    h_21_square = jnp.maximum(left, 0.0) + EPS
    n_00 = h_00 * h_00 + h_10 * h_10
    n_01 = h_00 * h_01 + h_10 * h_11
    n_11 = h_01 * h_01 + h_11 * h_11 + h_21_square
    l_00 = jnp.sqrt(n_00)
    l_10 = n_01 / l_00
    l_11 = jnp.sqrt(n_11 - l_10 * l_10)
    z_0 = beta * h_00 / l_00
    z_1 = (beta * h_01 - l_10 * z_0) / l_11
    y_1 = z_1 / l_11
    y_0 = (z_0 - l_10 * y_1) / l_00
    t_0 = beta - h_00 * y_0 - h_01 * y_1
    t_1 = -h_10 * y_0 - h_11 * y_1
    return {
        "r": (t_0 + y_1 * h_01) / beta,
        "u": (t_1 + y_1 * h_11) / h_10,
        "a": -y_1 / h_10,
        "c": y_1 * g_one,
        "sol_r": y_0 / beta,
        "sol_u": y_1 / h_10,
        "basis": state[:, 2 + s : 3 + s] - g_zero * y_0 - g_one * y_1,
    }


def next_kernel(size_x, size_y, got_ref, *refs):
    fields, refs = refs[:4], refs[4:]
    r_ref, u_ref, a_ref, m_ref, inv_ref, old_ref = refs[:6]
    new_ref, q_ref, sol_ref, state_ref, out_ref, side_ref, sums_ref = refs[6:]
    row = jnp.sum(got_ref[...], axis=0, keepdims=True)
    _, _, mask = grid_mask(size_x, size_y)
    state = old_ref[...]
    small = [close_cycle(row, inv_ref[...], state, s) for s in range(2)]
    lane = iota((VECS, 128), 1)
    state_ref[...] = jnp.where(
        lane == 2, small[0]["basis"], jnp.where(lane == 3, small[1]["basis"], 0.0)
    )
    coeffs = [[spread(small[s]["c"][k : k + 1]) for k in range(VECS)] for s in range(2)]
    scale = [{name: spread(small[s][name]) for name in ("r", "u", "a", "sol_r", "sol_u")} for s in range(2)]

    def total(s, at, rows, columns, value):
        value = value + scale[s]["r"] * r_ref[at, rows, columns]
        value = value + scale[s]["u"] * u_ref[at, rows, columns]
        return value + scale[s]["a"] * a_ref[at, rows, columns]

    def put(rows, columns):
        def store(s, j, value):
            at = s * ROWS + j
            new_ref[at, rows, columns] = total(s, at, rows, columns, value)

        return store

    combine_ext(
        coeffs, fields,
        put(slice(0, 8), slice(0, 128)), put(slice(8, 16), slice(0, 128)), side_ref,
    )
    for s in range(2):

        def body(step, carry, s=s):
            for i in range(AT_ONCE):
                at = s * ROWS + step * AT_ONCE + i
                for half in range(2):
                    rows = slice(half * 8, half * 8 + 8)
                    value = side_ref[at, rows]
                    new_ref[at, rows, 128:256] = total(s, at, rows, slice(128, 256), value)
                sol_ref[at] = (
                    scale[s]["sol_r"] * r_ref[at, 0:8, 0:128]
                    + scale[s]["sol_u"] * u_ref[at, 0:8, 0:128]
                )
            return carry

        lax.fori_loop(0, ROWS // AT_ONCE, body, 0)
    apply_operator(new_ref, m_ref, q_ref, mask)
    finish_first(fields[0], new_ref, q_ref, sums_ref, out_ref)


def basis_row(basis, d, kl, j):
    row = kl * ROWS + j
    if d == 0:
        return basis[0][row].astype(F32)
    first = {1: 1, 3: 3, 2: 5}[d]
    return basis[first][row].astype(F32) if kl < 2 else basis[first + 1][row - CUT].astype(F32)


def last_kernel(got_ref, c_ref, *refs):
    basis, refs = refs[:7], refs[7:]
    r_ref, u_ref, a_ref, inv_ref, old_ref, sol_ref = refs[:6]
    solution_ref, residual_ref = refs[6:]
    row = jnp.sum(got_ref[...], axis=0, keepdims=True)
    state = old_ref[...]
    small = [close_cycle(row, inv_ref[...], state, s) for s in range(2)]
    coeffs = [[spread(one["c"][k : k + 1]) for k in range(VECS)] for one in small]
    basis_coeffs = [[spread(one["basis"][k : k + 1]) for k in range(VECS)] for one in small]
    names = ("r", "u", "a", "sol_r", "sol_u")
    scale = [{name: spread(one[name]) for name in names} for one in small]

    def residual_body(step, carry):
        rows = [step * AT_ONCE + i for i in range(AT_ONCE)]
        values = [[], []]
        for s in range(2):
            for j in rows:
                r, u, a = brick(r_ref)(s, j), brick(u_ref)(s, j), brick(a_ref)(s, j)
                values[s].append(scale[s]["r"] * r + scale[s]["u"] * u + scale[s]["a"] * a)
        for k in range(VECS):
            for i, j in enumerate(rows):
                vec = c_ref[k * ROWS + j]
                for s in range(2):
                    values[s][i] = values[s][i] + coeffs[s][k] * vec
        for s in range(2):
            for i, j in enumerate(rows):
                residual_ref[s * ROWS + j] = values[s][i]
        return carry

    def solution_body(step, carry):
        rows = [step * AT_ONCE + i for i in range(AT_ONCE)]
        values = [[], []]
        for s in range(2):
            for j in rows:
                r, u = brick(r_ref)(s, j), brick(u_ref)(s, j)
                old = sol_ref[s * ROWS + j]
                values[s].append(old + scale[s]["sol_r"] * r + scale[s]["sol_u"] * u)
        for d in range(LOCAL):
            for kl in range(LOCAL):
                for i, j in enumerate(rows):
                    vec = basis_row(basis, d, kl, j)
                    for s in range(2):
                        values[s][i] = values[s][i] + basis_coeffs[s][d * LOCAL + kl] * vec
        for s in range(2):
            for i, j in enumerate(rows):
                solution_ref[s * ROWS + j] = values[s][i]
        return carry

    lax.fori_loop(0, ROWS // AT_ONCE, residual_body, 0)
    lax.fori_loop(0, ROWS // AT_ONCE, solution_body, 0)


def call(kernel, outs, args, scratch=(), smem=0):
    vmem = pl.BlockSpec(memory_space=pltpu.VMEM)
    return pl.pallas_call(
        kernel,
        out_shape=outs,
        in_specs=[pl.BlockSpec(memory_space=pltpu.SMEM)] * smem + [vmem] * (len(args) - smem),
        out_specs=jax.tree.map(lambda _: vmem, outs),
        scratch_shapes=list(scratch),
        compiler_params=pltpu.CompilerParams(vmem_limit_bytes=20 * 1024 * 1024),
    )(*args)


def shape(*dims, dtype=F32):
    return jax.ShapeDtypeStruct(dims, dtype)


def exchange(value):
    return lax.all_to_all(value, ("gx", "gy"), 0, 0)


def steps(axis, wrap=False):
    size = lax.axis_size(axis)
    up = [(i, (i + 1) % size) for i in range(size if wrap else size - 1)]
    return up, [(j, i) for i, j in up]


def tied(first, *rest):
    return lax.optimization_barrier((first, *rest))


def on_device(src_cell, basis, images, induction):
    size_x, size_y = 8 * lax.axis_size("gx"), 128 * lax.axis_size("gy")
    peers = lax.axis_size("gx") * lax.axis_size("gy")
    right, left = steps("tx", wrap=True)
    block = jnp.concatenate(
        [images.reshape(LOCAL * ROWS, 8, 128), induction.reshape(6, 8, 128)], axis=0
    )
    own = call(pack_y_kernel, shape(PACKED, 8, 128, dtype=BF16), (block,))
    one = lax.ppermute(block, "tx", right)
    three = lax.ppermute(block, "tx", left)
    up, down = steps("gy")
    after, before = lax.ppermute(own, "gy", down), lax.ppermute(own, "gy", up)
    side = jnp.where(lax.broadcasted_iota(jnp.int32, own.shape, 1) < 4, after, before)
    far_side = lax.ppermute(side, "tx", [(i, (i + 2) % LOCAL) for i in range(LOCAL)])
    far_side, one, three = tied(far_side, one, three)
    far_low = lax.ppermute(jnp.concatenate([one[:CUT], side]), "tx", right)
    far_high = lax.ppermute(jnp.concatenate([three[CUT:], side]), "tx", left)
    up, down = steps("gx")

    def exchange_x(group, sides, sources):
        count = len(group) * HALF + len(sides) * PACKED
        half = shape(count, 8, 128, dtype=BF16)
        low, high = call(functools.partial(pack_x_kernel, group, sides), (half, half), sources)
        return lax.ppermute(low, "gx", down), lax.ppermute(high, "gx", up)

    early = exchange_x(EARLY, EARLY_SIDES, (block, one, three, side, side, side))
    blocks = (block, one, three, far_low, far_high, side, far_side)

    late = exchange_x(LATE, LATE_SIDES, blocks)

    sums = pltpu.VMEM((128, 128), F32)
    side_scratch = pltpu.VMEM((2 * ROWS, 16, 128), F32)
    sent = call(
        functools.partial(gram_kernel, size_x, size_y),
        shape(peers, 4, 128),
        (src_cell, *blocks),
        (pltpu.VMEM((ROWS, 16, 128), F32), pltpu.VMEM((8 * VECS + 48, ROWS * 128), BF16)),
        smem=1,
    )
    got = exchange(sent)
    whole, tiles = shape(VECS * ROWS, 8, 128), shape(3 * VECS, 8, 128)
    m, rhs, *fields = call(
        functools.partial(prepare_kernel, size_x, size_y),
        (shape(24, 16, 256), shape(ROWS, 16, 256), whole, whole, tiles, tiles),
        (src_cell, *blocks, *early, *late),
        smem=1,
    )
    wide = shape(2 * ROWS, 16, 256)
    line = shape(peers, 128)
    small = shape(VECS, 128)
    own_basis = basis.reshape(LOCAL * ROWS, 8, 128)

    def total(value):
        return exchange(value.reshape(peers, 1, 128)).reshape(peers, 128)

    got, piece = tied(got, own_basis[:CUT])
    one_low, three_low = lax.ppermute(piece, "tx", right), lax.ppermute(piece, "tx", left)
    r, q, inverse, state, sent = call(
        functools.partial(begin_kernel, size_x, size_y),
        (wide, wide, small, small, line),
        (got, *fields, m, rhs),
        (side_scratch, sums),
    )

    def first(r, q, state, got):
        return call(
            functools.partial(first_kernel, size_x, size_y),
            (wide, wide, small, line),
            (got, *fields, r, q, m, inverse, state),
            (side_scratch, sums),
        )

    sent, one_low, three_low = tied(sent, one_low, three_low)
    got, piece = tied(total(sent), own_basis[CUT:])
    one_high, three_high = lax.ppermute(piece, "tx", right), lax.ppermute(piece, "tx", left)
    u, a, state, sent = first(r, q, state, got)
    sent, one_high, three_high = tied(sent, one_high, three_high)
    got, one_low, three_high = tied(total(sent), one_low, three_high)
    two_low, two_high = lax.ppermute(one_low, "tx", right), lax.ppermute(three_high, "tx", left)
    r, q, field, state, sent = call(
        functools.partial(next_kernel, size_x, size_y),
        (wide, wide, shape(2 * ROWS, 8, 128), small, line),
        (got, *fields, r, u, a, m, inverse, state),
        (side_scratch, sums),
    )
    sent, two_low, two_high = tied(sent, two_low, two_high)
    u, a, state, sent = first(r, q, state, total(sent))
    bases = (own_basis, one_low, one_high, three_low, three_high, two_low, two_high)
    narrow = shape(2 * ROWS, 8, 128)
    field, residual = call(
        last_kernel,
        (narrow, narrow),
        (total(sent), fields[0], *bases, r, u, a, inverse, state, field),
    )
    full = (2, 2, 3, 8, 8, 128)
    return field.reshape(full), residual.reshape(full)


def solution(mesh):
    in_specs = (
        P("tx"),
        P("tx", None, None, None, "gx", "gy"),
        P("tx", None, None, None, "gx", "gy"),
        P(None, "tx", "gx", "gy"),
    )
    out_specs = (P("tx", None, None, None, "gx", "gy"), P("tx", None, None, None, "gx", "gy"))
    return jax.shard_map(
        on_device, mesh=mesh, in_specs=in_specs, out_specs=out_specs, check_vma=False
    )
```

```python
import functools

import jax
import jax.numpy as jnp
from jax import lax
from jax.experimental import pallas as pl
from jax.experimental.pallas import tpu as pltpu
from jax.sharding import PartitionSpec as P

EPS = 1e-06
VECS = 16
LOCAL = 4
ROWS = 48
BLOCK = 198
HALF = 99
PACKED = 13
WEIGHTS = (1.0, 0.5, 0.25)
AT_ONCE = 4
HIGH = lax.Precision.HIGHEST
F32 = jnp.float32
BF16 = jnp.bfloat16


def iota(shape, axis):
    return lax.broadcasted_iota(jnp.int32, shape, axis)


def pick_matrix(dtype):
    col = iota((8, 128), 0)
    lane = iota((8, 128), 1)
    return jnp.where(lane == jnp.where(col < 4, col, col + 120), 1.0, 0.0).astype(dtype)


def nt_dot(left, right, precision=None):
    return lax.dot_general(
        left, right, (((1,), (1,)), ((), ())), precision=precision, preferred_element_type=F32
    )


def full_dot(left, right):
    return lax.dot_general(
        left, right, (((1,), (0,)), ((), ())), precision=HIGH, preferred_element_type=F32
    )


BLOCKS = 7
CUT = 2 * ROWS


def vector_row(blocks, d, kl, j):
    row = kl * ROWS + j
    if d != 2:
        return blocks[(0, 1, None, 2)[d]][row].astype(F32)
    return blocks[3][row].astype(F32) if kl < 2 else blocks[4][row - CUT].astype(F32)


def induction_row(blocks, d, at):
    if d != 2:
        return blocks[(0, 1, None, 2)[d]][LOCAL * ROWS + at].astype(F32)
    return blocks[4][LOCAL * ROWS - CUT + at].astype(F32)


def side_tile(blocks, d, tile):
    ref, first = ((5, 0), (3, CUT), (6, 0), (4, BLOCK - CUT))[d]
    return blocks[ref][first + tile]


def pack_y_kernel(block_ref, out_ref):
    pick = pick_matrix(BF16)
    for tile in range(PACKED):
        first = tile * 16
        count = min(16, BLOCK - first)
        rows = block_ref[first : first + count].astype(F32).reshape(count * 8, 128).astype(BF16)
        picked = nt_dot(pick, rows)
        if count < 16:
            picked = jnp.concatenate([picked, jnp.zeros((8, 128 - count * 8), F32)], axis=1)
        out_ref[tile] = picked.astype(BF16)


GROUP = (0, 1, 2, 3)


def halo_row(halos, d, row):
    at = d * HALF + row
    return halos[0][at].astype(F32), halos[1][at].astype(F32)


def halo_side(halos, d, tile):
    at = LOCAL * HALF + d * PACKED + tile
    after, before = halos[0][at].astype(F32), halos[1][at].astype(F32)
    return jnp.where(iota((8, 128), 1) % 8 < 4, after, before)


def pack_x_kernel(group, sides, *refs):
    blocks, (lo_ref, hi_ref) = refs[:-2], refs[-2:]
    top = iota((8, 128), 0) < 4

    def pair(one, two, at):
        two = pltpu.roll(two, 4, 0)
        lo_ref[at] = jnp.where(top, one, two).astype(BF16)
        hi_ref[at] = jnp.where(top, two, one).astype(BF16)

    def body(j, carry):
        for place, d in enumerate(group):
            for kl in range(2):
                pair(
                    vector_row(blocks, d, kl, j),
                    vector_row(blocks, d, kl + 2, j),
                    place * HALF + kl * ROWS + j,
                )
        return carry

    lax.fori_loop(0, ROWS, body, 0)
    for place, d in enumerate(group):
        for i in range(3):
            pair(
                induction_row(blocks, d, i),
                induction_row(blocks, d, i + 3),
                place * HALF + CUT + i,
            )
    for place, d in enumerate(sides):
        for tile in range(PACKED):
            piece = side_tile(blocks, d, tile)
            lo_ref[len(group) * HALF + place * PACKED + tile] = piece
            hi_ref[len(group) * HALF + place * PACKED + tile] = piece


def inner_all(c_ref, field, sums_ref):
    def body(step, accs):
        accs = list(accs)
        for j in (2 * step, 2 * step + 1):
            one, two = field(0, j), field(1, j)
            for k in range(VECS):
                vec = c_ref[k * ROWS + j]
                accs[2 * k] = accs[2 * k] + vec * one
                accs[2 * k + 1] = accs[2 * k + 1] + vec * two
        return tuple(accs)

    zero = jnp.zeros((8, 128), F32)
    accs = lax.fori_loop(0, ROWS // 2, body, (zero,) * (2 * VECS))
    for k in range(VECS):
        for s in range(2):
            sums_ref[s * VECS + k : s * VECS + k + 1] = jnp.sum(
                accs[2 * k + s], axis=0, keepdims=True
            )


def inner_pairs(pairs, sums_ref, first):
    count = len(pairs)

    def body(step, accs):
        new = []
        for s in range(2):
            for i, (one, two) in enumerate(pairs):
                acc = accs[s * count + i]
                for row in range(AT_ONCE):
                    j = step * AT_ONCE + row
                    acc = acc + one(s, j) * two(s, j)
                new.append(acc)
        return tuple(new)

    accs = lax.fori_loop(0, ROWS // AT_ONCE, body, (jnp.zeros((8, 128), F32),) * (2 * count))
    for i, acc in enumerate(accs):
        sums_ref[first + i : first + i + 1] = jnp.sum(acc, axis=0, keepdims=True)


def row_of_sums(sums_ref):
    return nt_dot(jnp.ones((8, 128), F32), sums_ref[...], HIGH)[0:1]


def entry(row, lane):
    return row[:, lane : lane + 1]


def column_of(row, first):
    part = row[:, first : first + VECS]
    eye = iota((VECS, VECS), 0) == iota((VECS, VECS), 1)
    return jnp.sum(jnp.where(eye, part, 0.0), axis=1, keepdims=True)


def solve(inverse, row, first):
    return jnp.sum(inverse[:, :VECS] * row[:, first : first + VECS], axis=1, keepdims=True)


def spread(value):
    return jnp.broadcast_to(value, (8, 128))


def grid_mask(size_x, size_y):
    row, lane = iota((16, 256), 0), iota((16, 256), 1)
    x_pos = lax.axis_index("gx") * 8 + jnp.where(row < 12, row, row - 16)
    y_pos = lax.axis_index("gy") * 128 + jnp.where(lane < 132, lane, lane - 256)
    inside = (x_pos >= 0) & (x_pos < size_x) & (y_pos >= 0) & (y_pos < size_y)
    inside = inside & ((lane < 132) | (lane >= 252))
    return x_pos, y_pos, inside


def primary_field(cell, z, x_pos, y_pos, size_x, size_y):
    plane = size_x * size_y
    src_z = cell // plane
    rest = cell % plane
    d_z = (z - src_z).astype(F32)
    d_x = (x_pos - rest // size_y).astype(F32)
    d_y = (y_pos - rest % size_y).astype(F32)
    dist = jnp.sqrt(d_z * d_z + d_x * d_x + d_y * d_y)
    return jnp.exp(-dist / ((size_x + size_y) / 8.0))


def unpack_once(blocks, halos, c_ref, x_ref, near_ref, far_ref):
    top = iota((8, 128), 0) < 4

    def body(j, carry):
        for d in range(LOCAL):
            for kl in range(LOCAL):
                k = d * LOCAL + kl
                c_ref[k * ROWS + j] = vector_row(blocks, d, kl, j)
                after, before = halo_row(halos, d, (kl % 2) * ROWS + j)
                if kl < 2:
                    x_ref[k * ROWS + j] = jnp.where(top, after, before)
                else:
                    x_ref[k * ROWS + j] = pltpu.roll(jnp.where(top, before, after), 4, 0)
        return carry

    lax.fori_loop(0, ROWS, body, 0, unroll=2)
    for d in range(LOCAL):
        for t in range(PACKED - 1):
            near_ref[d * 12 + t] = side_tile(blocks, d, t).astype(F32)
            far_ref[d * 12 + t] = halo_side(halos, d, t)


def plus(total, term):
    return term if total is None else total + term


def combine_ext(coeffs, fields, interior, halo_x, unpacked_ref):
    c_ref, x_ref, near_ref, far_ref = fields

    def body(step, carry):
        rows = [step * AT_ONCE + i for i in range(AT_ONCE)]
        inner = [[None] * AT_ONCE, [None] * AT_ONCE]
        outer = [[None] * AT_ONCE, [None] * AT_ONCE]
        for k in range(VECS):
            for i, j in enumerate(rows):
                vec, edge = c_ref[k * ROWS + j], x_ref[k * ROWS + j]
                for s in range(2):
                    inner[s][i] = plus(inner[s][i], coeffs[s][k] * vec)
                    outer[s][i] = plus(outer[s][i], coeffs[s][k] * edge)
        for i, j in enumerate(rows):
            for s in range(2):
                interior(s, j, inner[s][i])
                halo_x(s, j, outer[s][i])
        return carry

    lax.fori_loop(0, ROWS // AT_ONCE, body, 0)
    pick = pick_matrix(F32)
    for s in range(2):
        for tile in range(3):
            near = jnp.zeros((8, 128), F32)
            far = jnp.zeros((8, 128), F32)
            for k in range(VECS):
                near = near + coeffs[s][k] * near_ref[k * 3 + tile]
                far = far + coeffs[s][k] * far_ref[k * 3 + tile]
            place = s * ROWS + tile * 16
            near = full_dot(jnp.transpose(near), pick).reshape(16, 8, 128)
            far = full_dot(jnp.transpose(far), pick).reshape(16, 8, 128)
            unpacked_ref[place : place + 16, 0:8] = near
            unpacked_ref[place : place + 16, 8:16] = far


def apply_operator(e_ref, m_ref, out_ref, mask):
    def ahead(f, axis):
        return pltpu.roll(f, f.shape[axis] - 1, axis)

    def behind(f, axis):
        return pltpu.roll(f, 1, axis)

    def body(index, carry):
        base = index * 24
        other = jnp.where(index % 2 == 0, base + 24, base - 24)
        sign = jnp.where(index % 2 == 0, -1.0, 1.0).astype(F32)
        zero = jnp.zeros((16, 256), F32)
        b_x_old = -e_ref[base + 8]
        b_y_old = e_ref[base]
        for z in range(8):
            e_x, e_y, e_z = e_ref[base + z], e_ref[base + 8 + z], e_ref[base + 16 + z]
            up_x = e_ref[base + z + 1] if z < 7 else zero
            up_y = e_ref[base + 8 + z + 1] if z < 7 else zero
            b_x = (ahead(e_z, 1) - e_z) - (up_y - e_y)
            b_y = (up_x - e_x) - (ahead(e_z, 0) - e_z)
            b_z = (ahead(e_y, 0) - e_y) - (ahead(e_x, 1) - e_x)
            c_x = (b_z - behind(b_z, 1)) - (b_y - b_y_old)
            c_y = (b_x - b_x_old) - (b_z - behind(b_z, 0))
            c_z = (b_y - behind(b_y, 0)) - (b_x - behind(b_x, 1))
            for c, value in enumerate((c_x, c_y, c_z)):
                at = c * 8 + z
                value = value + sign * (m_ref[at] * e_ref[other + at])
                out_ref[base + at] = jnp.where(mask, value, 0.0)
            b_x_old, b_y_old = b_x, b_y
        return carry

    lax.fori_loop(0, 4, body, 0)


def brick(ref):
    return lambda s, j: ref[s * ROWS + j, 0:8, 0:128]


def pick_layer(values, z):
    want = lax.rem(lax.axis_index("tx") - z // 2 + LOCAL, LOCAL)
    result = values[0]
    for d in range(1, LOCAL):
        result = jnp.where(want == d, values[d], result)
    return result


def gram_kernel(size_x, size_y, src_ref, *refs):
    blocks, out_ref, field_ref, rows_ref = refs[:BLOCKS], *refs[BLOCKS:]
    x_pos = lax.axis_index("gx") * 8 + iota((8, 128), 0)
    y_pos = lax.axis_index("gy") * 128 + iota((8, 128), 1)
    for z in range(8):
        prim = [
            primary_field(src_ref[s], z, x_pos, y_pos, size_x, size_y) for s in range(2)
        ]
        for c in range(3):
            m = pick_layer([induction_row(blocks, d, 2 * c + z % 2) for d in range(LOCAL)], z)
            for s in range(2):
                real = (m - 1.0) * WEIGHTS[c] * prim[s]
                field_ref[c * 8 + z, s * 8 : s * 8 + 8] = real
                field_ref[24 + c * 8 + z, s * 8 : s * 8 + 8] = 0.5 * real

    def body(j, carry):
        columns = pl.ds(pl.multiple_of(j * 128, 128), 128)
        for pair in range(VECS // 2):
            d, kl = pair // 2, 2 * (pair % 2)
            both = [vector_row(blocks, d, kl + i, j) for i in range(2)]
            rows_ref[16 * pair : 16 * pair + 16, columns] = jnp.concatenate(both).astype(BF16)
        rest = field_ref[j]
        for piece in range(3):
            part = rest.astype(BF16)
            rest = rest - part.astype(F32)
            first = 8 * VECS + 16 * piece
            rows_ref[first : first + 16, columns] = part
        return carry

    lax.fori_loop(0, ROWS, body, 0)
    full = nt_dot(rows_ref[0:128], rows_ref[...])
    row, lane = iota((128, 128), 0), iota((128, 128), 1)
    gram = jnp.where(row % 8 == lane % 8, full[:, 0:128], 0.0).reshape(VECS, 8, 128)
    gram = jnp.sum(gram, axis=1)
    gram = full_dot(gram, jnp.where(row // 8 == lane % 16, 1.0, 0.0).astype(F32))
    gram = jnp.where(iota((VECS, 128), 1) // 16 == iota((VECS, 128), 0) % 8, gram, 0.0)
    gram = jnp.sum(gram.reshape(2, 8, 128), axis=1)
    inner = full[:, 128:144] + full[:, 144:160] + full[:, 160:176]
    inner = jnp.where(iota((128, 16), 0) % 8 == iota((128, 16), 1) % 8, inner, 0.0)
    inner = jnp.sum(inner.reshape(VECS, 8, 16), axis=1)
    lines = []
    for s in range(2):
        chosen = jnp.where(iota((8, 16), 1) // 8 == s, 1.0, 0.0).astype(F32)
        lines.append(nt_dot(chosen, inner, HIGH)[0:1])
    line = jnp.concatenate(lines + [jnp.zeros((1, 96), F32)], axis=1)
    rows = jnp.concatenate([gram, line, jnp.zeros((1, 128), F32)], axis=0)
    out_ref[...] = jnp.broadcast_to(rows[None], out_ref.shape)


def invert(rows):
    lane, row = iota((VECS, 128), 1), iota((VECS, 128), 0)
    wide = jnp.where(row < 8, rows[0:1], rows[1:2])
    wide = jnp.where(lane // 16 == row % 8, wide, 0.0)
    fold = jnp.where(iota((128, 128), 0) % 16 == iota((128, 128), 1), 1.0, 0.0).astype(F32)
    work = full_dot(wide, fold) + jnp.where(lane == row + VECS, 1.0, 0.0)
    for j in range(VECS):
        pivot = work[j : j + 1] / work[j : j + 1, j : j + 1]
        work = jnp.where(row == j, pivot, work - work[:, j : j + 1] * pivot)
    return pltpu.roll(work, 128 - VECS, 1)


def prepare_kernel(size_x, size_y, src_ref, *refs):
    blocks, halos, refs = refs[:BLOCKS], refs[BLOCKS : BLOCKS + 2], refs[BLOCKS + 2 :]
    m_ref, rhs_ref, fields = refs[0], refs[1], refs[2:]
    unpack_once(blocks, halos, *fields)
    x_pos, y_pos, mask = grid_mask(size_x, size_y)
    top = iota((8, 128), 0) < 4
    pick = pick_matrix(F32)
    sides = []
    for d in range(LOCAL):
        near, far = side_tile(blocks, d, 12).astype(F32), halo_side(halos, d, 12)
        near = full_dot(jnp.transpose(near), pick)[:48].reshape(6, 8, 128)
        far = full_dot(jnp.transpose(far), pick)[:48].reshape(6, 8, 128)
        sides.append((near, far))
    for c in range(3):
        for z in range(8):
            at = 2 * c + z % 2
            quarters = []
            for d in range(LOCAL):
                inner_m = induction_row(blocks, d, at)
                after, before = halo_row(halos, d, CUT + at % 3)
                if at < 3:
                    edge = jnp.where(top, after, before)
                else:
                    edge = pltpu.roll(jnp.where(top, before, after), 4, 0)
                left = jnp.concatenate([inner_m, edge], axis=0)
                right = jnp.concatenate([sides[d][0][at], sides[d][1][at]], axis=0)
                quarters.append(jnp.concatenate([left, right], axis=1))
            m_ref[c * 8 + z] = pick_layer(quarters, z)
    for s in range(2):

        def body(z, carry, s=s):
            prim = primary_field(src_ref[s], z, x_pos, y_pos, size_x, size_y)
            for c in range(3):
                at = c * 8 + z
                real = (m_ref[at] - 1.0) * WEIGHTS[c] * prim
                rhs_ref[s * 24 + at] = jnp.where(mask, real, 0.0)
            return carry

        lax.fori_loop(0, 8, body, 0)


def begin_kernel(size_x, size_y, got_ref, *refs):
    fields, m_ref, rhs_ref = refs[:4], refs[4], refs[5]
    r_ref, q_ref, inv_ref, state_ref, out_ref, side_ref, sums_ref = refs[6:]
    total = jnp.sum(got_ref[...], axis=0)
    inverse = invert(total[0:2])
    inv_ref[...] = inverse
    inner = total[2:3]
    _, _, mask = grid_mask(size_x, size_y)
    start = [solve(inverse, inner, s * VECS) for s in range(2)]
    lane = iota((VECS, 128), 1)
    state_ref[...] = jnp.where(lane == 2, start[0], jnp.where(lane == 3, start[1], 0.0))
    coeffs = [[spread(-start[s][k : k + 1]) for k in range(VECS)] for s in range(2)]

    def rhs(s, j, rows, columns):
        value = rhs_ref[s * 24 + lax.rem(j, 24), rows, columns]
        return jnp.where(j < 24, value, 0.5 * value)

    def put(rows, columns):
        def store(s, j, value):
            r_ref[s * ROWS + j, rows, columns] = value + rhs(s, j, rows, columns)

        return store

    combine_ext(
        coeffs, fields,
        put(slice(0, 8), slice(0, 128)), put(slice(8, 16), slice(0, 128)), side_ref,
    )
    for s in range(2):

        def body(step, carry, s=s):
            for i in range(AT_ONCE):
                j = step * AT_ONCE + i
                at = s * ROWS + j
                r_ref[at, :, 128:256] = side_ref[at] + rhs(s, j, slice(0, 16), slice(128, 256))
            return carry

        lax.fori_loop(0, ROWS // AT_ONCE, body, 0)
    apply_operator(r_ref, m_ref, q_ref, mask)
    finish_first(fields[0], r_ref, q_ref, sums_ref, out_ref)


def finish_first(c_ref, r_ref, q_ref, sums_ref, out_ref):
    sums_ref[...] = jnp.zeros_like(sums_ref)
    r, q = brick(r_ref), brick(q_ref)
    inner_all(c_ref, q, sums_ref)
    inner_pairs([(r, r), (r, q)], sums_ref, 32)
    out_ref[...] = jnp.broadcast_to(row_of_sums(sums_ref), out_ref.shape)


def first_kernel(size_x, size_y, got_ref, *refs):
    fields, refs = refs[:4], refs[4:]
    r_ref, q_ref, m_ref, inv_ref, old_ref = refs[:5]
    u_ref, a_ref, state_ref, out_ref, side_ref, sums_ref = refs[5:]
    row = jnp.sum(got_ref[...], axis=0, keepdims=True)
    _, _, mask = grid_mask(size_x, size_y)
    lane = iota((VECS, 128), 1)
    state = old_ref[...]
    coeffs, q_scale, r_scale = [], [], []
    for s in range(2):
        rr, rq = entry(row, 32 + 2 * s), entry(row, 33 + 2 * s)
        beta = jnp.sqrt(rr + EPS)
        g_zero = solve(inv_ref[...], row, s * VECS) / beta
        h_00 = rq / (beta * beta)
        coeffs.append([spread(-g_zero[k : k + 1]) for k in range(VECS)])
        q_scale.append(spread(1.0 / beta))
        r_scale.append(spread(-h_00 / beta))
        state = jnp.where(lane == s, g_zero, state)
        state = jnp.where(lane == 8 + s, beta, state)
        state = jnp.where(lane == 10 + s, h_00, state)
        state = jnp.where(lane == 12 + s, rr, state)
    state_ref[...] = state

    def put(rows, columns):
        def store(s, j, value):
            at = s * ROWS + j
            value = value + q_scale[s] * q_ref[at, rows, columns]
            u_ref[at, rows, columns] = value + r_scale[s] * r_ref[at, rows, columns]

        return store

    combine_ext(
        coeffs, fields,
        put(slice(0, 8), slice(0, 128)), put(slice(8, 16), slice(0, 128)), side_ref,
    )
    for s in range(2):

        def body(step, carry, s=s):
            for i in range(AT_ONCE):
                at = s * ROWS + step * AT_ONCE + i
                for half in range(2):
                    rows = slice(half * 8, half * 8 + 8)
                    new = side_ref[at, rows] + q_scale[s] * q_ref[at, rows, 128:256]
                    u_ref[at, rows, 128:256] = new + r_scale[s] * r_ref[at, rows, 128:256]
            return carry

        lax.fori_loop(0, ROWS // AT_ONCE, body, 0)
    apply_operator(u_ref, m_ref, a_ref, mask)
    sums_ref[...] = jnp.zeros_like(sums_ref)
    r, u, a = brick(r_ref), brick(u_ref), brick(a_ref)
    inner_all(fields[0], a, sums_ref)
    inner_pairs([(u, u), (r, u), (r, a), (u, a), (a, a)], sums_ref, 32)
    out_ref[...] = jnp.broadcast_to(row_of_sums(sums_ref), out_ref.shape)


def close_cycle(row, inverse, state, s):
    uu, ru, ra, ua, aa = [entry(row, 32 + 5 * s + i) for i in range(5)]
    g_zero = state[:, s : s + 1]
    beta, h_00, rr = [state[0:1, first + s : first + s + 1] for first in (8, 10, 12)]
    h_10 = jnp.sqrt(uu + EPS)
    inner = column_of(row, s * VECS) / h_10
    g_one = solve(inverse, row, s * VECS) / h_10
    h_01 = ra / (beta * h_10)
    h_11 = ua / (h_10 * h_10)
    left = aa / (h_10 * h_10) - jnp.sum(g_one * inner, axis=0, keepdims=True)
    left = left - 2.0 * (h_01 * h_01 + h_11 * h_11)
    left = left + h_01 * h_01 * (rr / (beta * beta)) + h_11 * h_11 * (uu / (h_10 * h_10))
    left = left + 2.0 * h_01 * h_11 * (ru / (beta * h_10))
    h_21_square = jnp.maximum(left, 0.0) + EPS
    n_00 = h_00 * h_00 + h_10 * h_10
    n_01 = h_00 * h_01 + h_10 * h_11
    n_11 = h_01 * h_01 + h_11 * h_11 + h_21_square
    l_00 = jnp.sqrt(n_00)
    l_10 = n_01 / l_00
    l_11 = jnp.sqrt(n_11 - l_10 * l_10)
    z_0 = beta * h_00 / l_00
    z_1 = (beta * h_01 - l_10 * z_0) / l_11
    y_1 = z_1 / l_11
    y_0 = (z_0 - l_10 * y_1) / l_00
    t_0 = beta - h_00 * y_0 - h_01 * y_1
    t_1 = -h_10 * y_0 - h_11 * y_1
    return {
        "r": (t_0 + y_1 * h_01) / beta,
        "u": (t_1 + y_1 * h_11) / h_10,
        "a": -y_1 / h_10,
        "c": y_1 * g_one,
        "sol_r": y_0 / beta,
        "sol_u": y_1 / h_10,
        "basis": state[:, 2 + s : 3 + s] - g_zero * y_0 - g_one * y_1,
    }


def next_kernel(size_x, size_y, got_ref, *refs):
    fields, refs = refs[:4], refs[4:]
    r_ref, u_ref, a_ref, m_ref, inv_ref, old_ref = refs[:6]
    new_ref, q_ref, sol_ref, state_ref, out_ref, side_ref, sums_ref = refs[6:]
    row = jnp.sum(got_ref[...], axis=0, keepdims=True)
    _, _, mask = grid_mask(size_x, size_y)
    state = old_ref[...]
    small = [close_cycle(row, inv_ref[...], state, s) for s in range(2)]
    lane = iota((VECS, 128), 1)
    state_ref[...] = jnp.where(
        lane == 2, small[0]["basis"], jnp.where(lane == 3, small[1]["basis"], 0.0)
    )
    coeffs = [[spread(small[s]["c"][k : k + 1]) for k in range(VECS)] for s in range(2)]
    scale = [{name: spread(small[s][name]) for name in ("r", "u", "a", "sol_r", "sol_u")} for s in range(2)]

    def total(s, at, rows, columns, value):
        value = value + scale[s]["r"] * r_ref[at, rows, columns]
        value = value + scale[s]["u"] * u_ref[at, rows, columns]
        return value + scale[s]["a"] * a_ref[at, rows, columns]

    def put(rows, columns):
        def store(s, j, value):
            at = s * ROWS + j
            new_ref[at, rows, columns] = total(s, at, rows, columns, value)

        return store

    combine_ext(
        coeffs, fields,
        put(slice(0, 8), slice(0, 128)), put(slice(8, 16), slice(0, 128)), side_ref,
    )
    for s in range(2):

        def body(step, carry, s=s):
            for i in range(AT_ONCE):
                at = s * ROWS + step * AT_ONCE + i
                for half in range(2):
                    rows = slice(half * 8, half * 8 + 8)
                    value = side_ref[at, rows]
                    new_ref[at, rows, 128:256] = total(s, at, rows, slice(128, 256), value)
                sol_ref[at] = (
                    scale[s]["sol_r"] * r_ref[at, 0:8, 0:128]
                    + scale[s]["sol_u"] * u_ref[at, 0:8, 0:128]
                )
            return carry

        lax.fori_loop(0, ROWS // AT_ONCE, body, 0)
    apply_operator(new_ref, m_ref, q_ref, mask)
    finish_first(fields[0], new_ref, q_ref, sums_ref, out_ref)


def basis_row(basis, d, kl, j):
    row = kl * ROWS + j
    first = (0, 2, 6, 4)[d]
    return basis[first][row].astype(F32) if kl < 2 else basis[first + 1][row - CUT].astype(F32)


def last_kernel(got_ref, c_ref, *refs):
    basis, refs = refs[:8], refs[8:]
    r_ref, u_ref, a_ref, inv_ref, old_ref, sol_ref = refs[:6]
    solution_ref, residual_ref = refs[6:]
    row = jnp.sum(got_ref[...], axis=0, keepdims=True)
    state = old_ref[...]
    small = [close_cycle(row, inv_ref[...], state, s) for s in range(2)]
    coeffs = [[spread(one["c"][k : k + 1]) for k in range(VECS)] for one in small]
    basis_coeffs = [[spread(one["basis"][k : k + 1]) for k in range(VECS)] for one in small]
    names = ("r", "u", "a", "sol_r", "sol_u")
    scale = [{name: spread(one[name]) for name in names} for one in small]

    def residual_body(step, carry):
        rows = [step * AT_ONCE + i for i in range(AT_ONCE)]
        values = [[], []]
        for s in range(2):
            for j in rows:
                r, u, a = brick(r_ref)(s, j), brick(u_ref)(s, j), brick(a_ref)(s, j)
                values[s].append(scale[s]["r"] * r + scale[s]["u"] * u + scale[s]["a"] * a)
        for k in range(VECS):
            for i, j in enumerate(rows):
                vec = c_ref[k * ROWS + j]
                for s in range(2):
                    values[s][i] = values[s][i] + coeffs[s][k] * vec
        for s in range(2):
            for i, j in enumerate(rows):
                residual_ref[s * ROWS + j] = values[s][i]
        return carry

    def solution_body(step, carry):
        rows = [step * AT_ONCE + i for i in range(AT_ONCE)]
        values = [[], []]
        for s in range(2):
            for j in rows:
                r, u = brick(r_ref)(s, j), brick(u_ref)(s, j)
                old = sol_ref[s * ROWS + j]
                values[s].append(old + scale[s]["sol_r"] * r + scale[s]["sol_u"] * u)
        for d in range(LOCAL):
            for kl in range(LOCAL):
                for i, j in enumerate(rows):
                    vec = basis_row(basis, d, kl, j)
                    for s in range(2):
                        values[s][i] = values[s][i] + basis_coeffs[s][d * LOCAL + kl] * vec
        for s in range(2):
            for i, j in enumerate(rows):
                solution_ref[s * ROWS + j] = values[s][i]
        return carry

    lax.fori_loop(0, ROWS // AT_ONCE, residual_body, 0)
    lax.fori_loop(0, ROWS // AT_ONCE, solution_body, 0)


def call(kernel, outs, args, scratch=(), smem=0):
    vmem = pl.BlockSpec(memory_space=pltpu.VMEM)
    return pl.pallas_call(
        kernel,
        out_shape=outs,
        in_specs=[pl.BlockSpec(memory_space=pltpu.SMEM)] * smem + [vmem] * (len(args) - smem),
        out_specs=jax.tree.map(lambda _: vmem, outs),
        scratch_shapes=list(scratch),
        compiler_params=pltpu.CompilerParams(vmem_limit_bytes=20 * 1024 * 1024),
    )(*args)


def shape(*dims, dtype=F32):
    return jax.ShapeDtypeStruct(dims, dtype)


def exchange(value):
    return lax.all_to_all(value, ("gx", "gy"), 0, 0)


def steps(axis, wrap=False):
    size = lax.axis_size(axis)
    up = [(i, (i + 1) % size) for i in range(size if wrap else size - 1)]
    return up, [(j, i) for i, j in up]


def tied(first, *rest):
    return lax.optimization_barrier((first, *rest))


def on_device(src_cell, basis, images, induction):
    size_x, size_y = 8 * lax.axis_size("gx"), 128 * lax.axis_size("gy")
    peers = lax.axis_size("gx") * lax.axis_size("gy")
    right, left = steps("tx", wrap=True)
    block = jnp.concatenate(
        [images.reshape(LOCAL * ROWS, 8, 128), induction.reshape(6, 8, 128)], axis=0
    )
    own = call(pack_y_kernel, shape(PACKED, 8, 128, dtype=BF16), (block,))
    one = lax.ppermute(block, "tx", right)
    three = lax.ppermute(block, "tx", left)
    up, down = steps("gy")
    after, before = lax.ppermute(own, "gy", down), lax.ppermute(own, "gy", up)
    side = jnp.where(lax.broadcasted_iota(jnp.int32, own.shape, 1) < 4, after, before)
    far_side = lax.ppermute(side, "tx", [(i, (i + 2) % LOCAL) for i in range(LOCAL)])
    own_basis = basis.reshape(LOCAL * ROWS, 8, 128)
    far_side, one, three, basis_low, basis_high = tied(
        far_side, one, three, own_basis[:CUT], own_basis[CUT:]
    )
    far_low = lax.ppermute(jnp.concatenate([one[:CUT], side]), "tx", right)
    far_high = lax.ppermute(jnp.concatenate([three[CUT:], side]), "tx", left)
    up, down = steps("gx")

    def exchange_x(group, sides, sources):
        count = len(group) * HALF + len(sides) * PACKED
        half = shape(count, 8, 128, dtype=BF16)
        low, high = call(functools.partial(pack_x_kernel, group, sides), (half, half), sources)
        return lax.ppermute(low, "gx", down), lax.ppermute(high, "gx", up)

    blocks = (block, one, three, far_low, far_high, side, far_side)

    halos = exchange_x(GROUP, GROUP, blocks)

    sums = pltpu.VMEM((128, 128), F32)
    side_scratch = pltpu.VMEM((2 * ROWS, 16, 128), F32)
    sent = call(
        functools.partial(gram_kernel, size_x, size_y),
        shape(peers, 4, 128),
        (src_cell, *blocks),
        (pltpu.VMEM((ROWS, 16, 128), F32), pltpu.VMEM((8 * VECS + 48, ROWS * 128), BF16)),
        smem=1,
    )
    got = exchange(sent)
    whole, tiles = shape(VECS * ROWS, 8, 128), shape(3 * VECS, 8, 128)
    m, rhs, *fields = call(
        functools.partial(prepare_kernel, size_x, size_y),
        (shape(24, 16, 256), shape(ROWS, 16, 256), whole, whole, tiles, tiles),
        (src_cell, *blocks, *halos),
        smem=1,
    )
    wide = shape(2 * ROWS, 16, 256)
    line = shape(peers, 128)
    small = shape(VECS, 128)

    def total(value):
        return exchange(value.reshape(peers, 1, 128)).reshape(peers, 128)

    got, piece = tied(got, basis_low)
    one_low, three_low = lax.ppermute(piece, "tx", right), lax.ppermute(piece, "tx", left)
    r, q, inverse, state, sent = call(
        functools.partial(begin_kernel, size_x, size_y),
        (wide, wide, small, small, line),
        (got, *fields, m, rhs),
        (side_scratch, sums),
    )

    def first(r, q, state, got):
        return call(
            functools.partial(first_kernel, size_x, size_y),
            (wide, wide, small, line),
            (got, *fields, r, q, m, inverse, state),
            (side_scratch, sums),
        )

    sent, one_low, three_low = tied(sent, one_low, three_low)
    got, piece = tied(total(sent), basis_high)
    one_high, three_high = lax.ppermute(piece, "tx", right), lax.ppermute(piece, "tx", left)
    u, a, state, sent = first(r, q, state, got)
    sent, one_high, three_high = tied(sent, one_high, three_high)
    got, one_low, three_high = tied(total(sent), one_low, three_high)
    two_low, two_high = lax.ppermute(one_low, "tx", right), lax.ppermute(three_high, "tx", left)
    r, q, field, state, sent = call(
        functools.partial(next_kernel, size_x, size_y),
        (wide, wide, shape(2 * ROWS, 8, 128), small, line),
        (got, *fields, r, u, a, m, inverse, state),
        (side_scratch, sums),
    )
    sent, two_low, two_high = tied(sent, two_low, two_high)
    u, a, state, sent = first(r, q, state, total(sent))
    bases = (basis_low, basis_high, one_low, one_high, three_low, three_high, two_low, two_high)
    narrow = shape(2 * ROWS, 8, 128)
    field, residual = call(
        last_kernel,
        (narrow, narrow),
        (total(sent), fields[0], *bases, r, u, a, inverse, state, field),
    )
    full = (2, 2, 3, 8, 8, 128)
    return field.reshape(full), residual.reshape(full)


def solution(mesh):
    in_specs = (
        P("tx"),
        P("tx", None, None, None, "gx", "gy"),
        P("tx", None, None, None, "gx", "gy"),
        P(None, "tx", "gx", "gy"),
    )
    out_specs = (P("tx", None, None, None, "gx", "gy"), P("tx", None, None, None, "gx", "gy"))
    return jax.shard_map(
        on_device, mesh=mesh, in_specs=in_specs, out_specs=out_specs, check_vma=False
    )
```

```python
import functools

import jax
import jax.numpy as jnp
from jax import lax
from jax.experimental import pallas as pl
from jax.experimental.pallas import tpu as pltpu
from jax.sharding import PartitionSpec as P

EPS = 1e-06
VECS = 16
LOCAL = 4
ROWS = 48
BLOCK = 198
HALF = 99
PACKED = 13
WEIGHTS = (1.0, 0.5, 0.25)
AT_ONCE = 8
HIGH = lax.Precision.HIGHEST
F32 = jnp.float32
BF16 = jnp.bfloat16


def iota(shape, axis):
    return lax.broadcasted_iota(jnp.int32, shape, axis)


def pick_matrix(dtype):
    col = iota((8, 128), 0)
    lane = iota((8, 128), 1)
    return jnp.where(lane == jnp.where(col < 4, col, col + 120), 1.0, 0.0).astype(dtype)


def nt_dot(left, right, precision=None):
    return lax.dot_general(
        left, right, (((1,), (1,)), ((), ())), precision=precision, preferred_element_type=F32
    )


def full_dot(left, right):
    return lax.dot_general(
        left, right, (((1,), (0,)), ((), ())), precision=HIGH, preferred_element_type=F32
    )


BLOCKS = 7
CUT = 2 * ROWS


def vector_row(blocks, d, kl, j):
    row = kl * ROWS + j
    if d != 2:
        return blocks[(0, 1, None, 2)[d]][row].astype(F32)
    return blocks[3][row].astype(F32) if kl < 2 else blocks[4][row - CUT].astype(F32)


def induction_row(blocks, d, at):
    if d != 2:
        return blocks[(0, 1, None, 2)[d]][LOCAL * ROWS + at].astype(F32)
    return blocks[4][LOCAL * ROWS - CUT + at].astype(F32)


def side_tile(blocks, d, tile):
    ref, first = ((5, 0), (3, CUT), (6, 0), (4, BLOCK - CUT))[d]
    return blocks[ref][first + tile]


def pack_y_kernel(block_ref, out_ref):
    pick = pick_matrix(BF16)
    for tile in range(PACKED):
        first = tile * 16
        count = min(16, BLOCK - first)
        rows = block_ref[first : first + count].astype(F32).reshape(count * 8, 128).astype(BF16)
        picked = nt_dot(pick, rows)
        if count < 16:
            picked = jnp.concatenate([picked, jnp.zeros((8, 128 - count * 8), F32)], axis=1)
        out_ref[tile] = picked.astype(BF16)


EARLY, LATE = (0, 1, 3), (2,)
EARLY_SIDES, LATE_SIDES = (0,), (1, 2, 3)


def halo_row(halos, d, row):
    ref = 2 if d == 2 else 0
    at = (0 if d == 2 else EARLY.index(d)) * HALF + row
    return halos[ref][at].astype(F32), halos[ref + 1][at].astype(F32)


def halo_side(halos, d, tile):
    ref = 0 if d == 0 else 2
    at = (len(EARLY) * HALF if d == 0 else HALF + LATE_SIDES.index(d) * PACKED) + tile
    after, before = halos[ref][at].astype(F32), halos[ref + 1][at].astype(F32)
    return jnp.where(iota((8, 128), 1) % 8 < 4, after, before)


def pack_x_kernel(group, sides, *refs):
    blocks, (lo_ref, hi_ref) = refs[:-2], refs[-2:]
    top = iota((8, 128), 0) < 4

    def pair(one, two, at):
        two = pltpu.roll(two, 4, 0)
        lo_ref[at] = jnp.where(top, one, two).astype(BF16)
        hi_ref[at] = jnp.where(top, two, one).astype(BF16)

    def body(j, carry):
        for place, d in enumerate(group):
            for kl in range(2):
                pair(
                    vector_row(blocks, d, kl, j),
                    vector_row(blocks, d, kl + 2, j),
                    place * HALF + kl * ROWS + j,
                )
        return carry

    lax.fori_loop(0, ROWS, body, 0)
    for place, d in enumerate(group):
        for i in range(3):
            pair(
                induction_row(blocks, d, i),
                induction_row(blocks, d, i + 3),
                place * HALF + CUT + i,
            )
    for place, d in enumerate(sides):
        for tile in range(PACKED):
            piece = side_tile(blocks, d, tile)
            lo_ref[len(group) * HALF + place * PACKED + tile] = piece
            hi_ref[len(group) * HALF + place * PACKED + tile] = piece


def inner_all(c_ref, field, sums_ref):
    def body(step, accs):
        accs = list(accs)
        for j in [AT_ONCE * step + i for i in range(AT_ONCE)]:
            one, two = field(0, j), field(1, j)
            for k in range(VECS):
                vec = c_ref[k * ROWS + j]
                accs[2 * k] = accs[2 * k] + vec * one
                accs[2 * k + 1] = accs[2 * k + 1] + vec * two
        return tuple(accs)

    zero = jnp.zeros((8, 128), F32)
    accs = lax.fori_loop(0, ROWS // AT_ONCE, body, (zero,) * (2 * VECS))
    for k in range(VECS):
        for s in range(2):
            sums_ref[s * VECS + k : s * VECS + k + 1] = jnp.sum(
                accs[2 * k + s], axis=0, keepdims=True
            )


def inner_pairs(pairs, sums_ref, first):
    count = len(pairs)

    def body(step, accs):
        new = []
        for s in range(2):
            for i, (one, two) in enumerate(pairs):
                acc = accs[s * count + i]
                for row in range(AT_ONCE):
                    j = step * AT_ONCE + row
                    acc = acc + one(s, j) * two(s, j)
                new.append(acc)
        return tuple(new)

    accs = lax.fori_loop(0, ROWS // AT_ONCE, body, (jnp.zeros((8, 128), F32),) * (2 * count))
    for i, acc in enumerate(accs):
        sums_ref[first + i : first + i + 1] = jnp.sum(acc, axis=0, keepdims=True)


def row_of_sums(sums_ref):
    return nt_dot(jnp.ones((8, 128), F32), sums_ref[...], HIGH)[0:1]


def entry(row, lane):
    return row[:, lane : lane + 1]


def column_of(row, first):
    part = row[:, first : first + VECS]
    eye = iota((VECS, VECS), 0) == iota((VECS, VECS), 1)
    return jnp.sum(jnp.where(eye, part, 0.0), axis=1, keepdims=True)


def solve(inverse, row, first):
    return jnp.sum(inverse[:, :VECS] * row[:, first : first + VECS], axis=1, keepdims=True)


def spread(value):
    return jnp.broadcast_to(value, (8, 128))


def grid_mask(size_x, size_y):
    row, lane = iota((16, 256), 0), iota((16, 256), 1)
    x_pos = lax.axis_index("gx") * 8 + jnp.where(row < 12, row, row - 16)
    y_pos = lax.axis_index("gy") * 128 + jnp.where(lane < 132, lane, lane - 256)
    inside = (x_pos >= 0) & (x_pos < size_x) & (y_pos >= 0) & (y_pos < size_y)
    inside = inside & ((lane < 132) | (lane >= 252))
    return x_pos, y_pos, inside


def primary_field(cell, z, x_pos, y_pos, size_x, size_y):
    plane = size_x * size_y
    src_z = cell // plane
    rest = cell % plane
    d_z = (z - src_z).astype(F32)
    d_x = (x_pos - rest // size_y).astype(F32)
    d_y = (y_pos - rest % size_y).astype(F32)
    dist = jnp.sqrt(d_z * d_z + d_x * d_x + d_y * d_y)
    return jnp.exp(-dist / ((size_x + size_y) / 8.0))


def unpack_once(blocks, halos, c_ref, x_ref, near_ref, far_ref):
    top = iota((8, 128), 0) < 4

    def body(j, carry):
        for d in range(LOCAL):
            for kl in range(LOCAL):
                k = d * LOCAL + kl
                c_ref[k * ROWS + j] = vector_row(blocks, d, kl, j)
                after, before = halo_row(halos, d, (kl % 2) * ROWS + j)
                if kl < 2:
                    x_ref[k * ROWS + j] = jnp.where(top, after, before)
                else:
                    x_ref[k * ROWS + j] = pltpu.roll(jnp.where(top, before, after), 4, 0)
        return carry

    lax.fori_loop(0, ROWS, body, 0, unroll=2)
    for d in range(LOCAL):
        for t in range(PACKED - 1):
            near_ref[d * 12 + t] = side_tile(blocks, d, t).astype(F32)
            far_ref[d * 12 + t] = halo_side(halos, d, t)


def plus(total, term):
    return term if total is None else total + term


def combine_ext(coeffs, fields, interior, halo_x, unpacked_ref):
    c_ref, x_ref, near_ref, far_ref = fields

    def body(step, carry):
        rows = [step * AT_ONCE + i for i in range(AT_ONCE)]
        inner = [[None] * AT_ONCE, [None] * AT_ONCE]
        outer = [[None] * AT_ONCE, [None] * AT_ONCE]
        for k in range(VECS):
            for i, j in enumerate(rows):
                vec, edge = c_ref[k * ROWS + j], x_ref[k * ROWS + j]
                for s in range(2):
                    inner[s][i] = plus(inner[s][i], coeffs[s][k] * vec)
                    outer[s][i] = plus(outer[s][i], coeffs[s][k] * edge)
        for i, j in enumerate(rows):
            for s in range(2):
                interior(s, j, inner[s][i])
                halo_x(s, j, outer[s][i])
        return carry

    lax.fori_loop(0, ROWS // AT_ONCE, body, 0)
    pick = pick_matrix(F32)
    for s in range(2):
        for tile in range(3):
            near = jnp.zeros((8, 128), F32)
            far = jnp.zeros((8, 128), F32)
            for k in range(VECS):
                near = near + coeffs[s][k] * near_ref[k * 3 + tile]
                far = far + coeffs[s][k] * far_ref[k * 3 + tile]
            place = s * ROWS + tile * 16
            near = full_dot(jnp.transpose(near), pick).reshape(16, 8, 128)
            far = full_dot(jnp.transpose(far), pick).reshape(16, 8, 128)
            unpacked_ref[place : place + 16, 0:8] = near
            unpacked_ref[place : place + 16, 8:16] = far


def apply_operator(e_ref, m_ref, out_ref, mask):
    def ahead(f, axis):
        return pltpu.roll(f, f.shape[axis] - 1, axis)

    def behind(f, axis):
        return pltpu.roll(f, 1, axis)

    def body(index, carry):
        base = index * 24
        other = jnp.where(index % 2 == 0, base + 24, base - 24)
        sign = jnp.where(index % 2 == 0, -1.0, 1.0).astype(F32)
        zero = jnp.zeros((16, 256), F32)
        b_x_old = -e_ref[base + 8]
        b_y_old = e_ref[base]
        for z in range(8):
            e_x, e_y, e_z = e_ref[base + z], e_ref[base + 8 + z], e_ref[base + 16 + z]
            up_x = e_ref[base + z + 1] if z < 7 else zero
            up_y = e_ref[base + 8 + z + 1] if z < 7 else zero
            b_x = (ahead(e_z, 1) - e_z) - (up_y - e_y)
            b_y = (up_x - e_x) - (ahead(e_z, 0) - e_z)
            b_z = (ahead(e_y, 0) - e_y) - (ahead(e_x, 1) - e_x)
            c_x = (b_z - behind(b_z, 1)) - (b_y - b_y_old)
            c_y = (b_x - b_x_old) - (b_z - behind(b_z, 0))
            c_z = (b_y - behind(b_y, 0)) - (b_x - behind(b_x, 1))
            for c, value in enumerate((c_x, c_y, c_z)):
                at = c * 8 + z
                value = value + sign * (m_ref[at] * e_ref[other + at])
                out_ref[base + at] = jnp.where(mask, value, 0.0)
            b_x_old, b_y_old = b_x, b_y
        return carry

    lax.fori_loop(0, 4, body, 0)


def brick(ref):
    return lambda s, j: ref[s * ROWS + j, 0:8, 0:128]


def pick_layer(values, z):
    want = lax.rem(lax.axis_index("tx") - z // 2 + LOCAL, LOCAL)
    result = values[0]
    for d in range(1, LOCAL):
        result = jnp.where(want == d, values[d], result)
    return result


def gram_kernel(size_x, size_y, src_ref, *refs):
    blocks, out_ref, field_ref, rows_ref = refs[:BLOCKS], *refs[BLOCKS:]
    x_pos = lax.axis_index("gx") * 8 + iota((8, 128), 0)
    y_pos = lax.axis_index("gy") * 128 + iota((8, 128), 1)
    for z in range(8):
        prim = [
            primary_field(src_ref[s], z, x_pos, y_pos, size_x, size_y) for s in range(2)
        ]
        for c in range(3):
            m = pick_layer([induction_row(blocks, d, 2 * c + z % 2) for d in range(LOCAL)], z)
            for s in range(2):
                real = (m - 1.0) * WEIGHTS[c] * prim[s]
                field_ref[c * 8 + z, s * 8 : s * 8 + 8] = real
                field_ref[24 + c * 8 + z, s * 8 : s * 8 + 8] = 0.5 * real

    def body(j, carry):
        columns = pl.ds(pl.multiple_of(j * 128, 128), 128)
        for pair in range(VECS // 2):
            d, kl = pair // 2, 2 * (pair % 2)
            both = [vector_row(blocks, d, kl + i, j) for i in range(2)]
            rows_ref[16 * pair : 16 * pair + 16, columns] = jnp.concatenate(both).astype(BF16)
        rest = field_ref[j]
        for piece in range(3):
            part = rest.astype(BF16)
            rest = rest - part.astype(F32)
            first = 8 * VECS + 16 * piece
            rows_ref[first : first + 16, columns] = part
        return carry

    lax.fori_loop(0, ROWS, body, 0)
    full = nt_dot(rows_ref[0:128], rows_ref[...])
    row, lane = iota((128, 128), 0), iota((128, 128), 1)
    gram = jnp.where(row % 8 == lane % 8, full[:, 0:128], 0.0).reshape(VECS, 8, 128)
    gram = jnp.sum(gram, axis=1)
    gram = full_dot(gram, jnp.where(row // 8 == lane % 16, 1.0, 0.0).astype(F32))
    gram = jnp.where(iota((VECS, 128), 1) // 16 == iota((VECS, 128), 0) % 8, gram, 0.0)
    gram = jnp.sum(gram.reshape(2, 8, 128), axis=1)
    inner = full[:, 128:144] + full[:, 144:160] + full[:, 160:176]
    inner = jnp.where(iota((128, 16), 0) % 8 == iota((128, 16), 1) % 8, inner, 0.0)
    inner = jnp.sum(inner.reshape(VECS, 8, 16), axis=1)
    lines = []
    for s in range(2):
        chosen = jnp.where(iota((8, 16), 1) // 8 == s, 1.0, 0.0).astype(F32)
        lines.append(nt_dot(chosen, inner, HIGH)[0:1])
    line = jnp.concatenate(lines + [jnp.zeros((1, 96), F32)], axis=1)
    rows = jnp.concatenate([gram, line], axis=0)
    out_ref[...] = jnp.broadcast_to(rows[None], out_ref.shape)


def invert(rows):
    lane, row = iota((VECS, 128), 1), iota((VECS, 128), 0)
    wide = jnp.where(row < 8, rows[0:1], rows[1:2])
    wide = jnp.where(lane // 16 == row % 8, wide, 0.0)
    fold = jnp.where(iota((128, 128), 0) % 16 == iota((128, 128), 1), 1.0, 0.0).astype(F32)
    work = full_dot(wide, fold) + jnp.where(lane == row + VECS, 1.0, 0.0)
    for j in range(VECS):
        pivot = work[j : j + 1] / work[j : j + 1, j : j + 1]
        work = jnp.where(row == j, pivot, work - work[:, j : j + 1] * pivot)
    return pltpu.roll(work, 128 - VECS, 1)


def prepare_kernel(size_x, size_y, src_ref, *refs):
    blocks, halos, refs = refs[:BLOCKS], refs[BLOCKS : BLOCKS + 4], refs[BLOCKS + 4 :]
    m_ref, rhs_ref, fields = refs[0], refs[1], refs[2:]
    unpack_once(blocks, halos, *fields)
    x_pos, y_pos, mask = grid_mask(size_x, size_y)
    top = iota((8, 128), 0) < 4
    pick = pick_matrix(F32)
    sides = []
    for d in range(LOCAL):
        near, far = side_tile(blocks, d, 12).astype(F32), halo_side(halos, d, 12)
        near = full_dot(jnp.transpose(near), pick)[:48].reshape(6, 8, 128)
        far = full_dot(jnp.transpose(far), pick)[:48].reshape(6, 8, 128)
        sides.append((near, far))
    for c in range(3):
        for z in range(8):
            at = 2 * c + z % 2
            quarters = []
            for d in range(LOCAL):
                inner_m = induction_row(blocks, d, at)
                after, before = halo_row(halos, d, CUT + at % 3)
                if at < 3:
                    edge = jnp.where(top, after, before)
                else:
                    edge = pltpu.roll(jnp.where(top, before, after), 4, 0)
                left = jnp.concatenate([inner_m, edge], axis=0)
                right = jnp.concatenate([sides[d][0][at], sides[d][1][at]], axis=0)
                quarters.append(jnp.concatenate([left, right], axis=1))
            m_ref[c * 8 + z] = pick_layer(quarters, z)
    for s in range(2):

        def body(z, carry, s=s):
            prim = primary_field(src_ref[s], z, x_pos, y_pos, size_x, size_y)
            for c in range(3):
                at = c * 8 + z
                real = (m_ref[at] - 1.0) * WEIGHTS[c] * prim
                rhs_ref[s * 24 + at] = jnp.where(mask, real, 0.0)
            return carry

        lax.fori_loop(0, 8, body, 0)


def begin_kernel(size_x, size_y, got_ref, *refs):
    fields, m_ref, rhs_ref = refs[:4], refs[4], refs[5]
    r_ref, q_ref, inv_ref, state_ref, out_ref, side_ref, sums_ref = refs[6:]
    total = jnp.sum(got_ref[...], axis=0)
    inverse = invert(total[0:2])
    inv_ref[...] = inverse
    inner = total[2:3]
    _, _, mask = grid_mask(size_x, size_y)
    start = [solve(inverse, inner, s * VECS) for s in range(2)]
    lane = iota((VECS, 128), 1)
    state_ref[...] = jnp.where(lane == 2, start[0], jnp.where(lane == 3, start[1], 0.0))
    coeffs = [[spread(-start[s][k : k + 1]) for k in range(VECS)] for s in range(2)]

    def rhs(s, j, rows, columns):
        value = rhs_ref[s * 24 + lax.rem(j, 24), rows, columns]
        return jnp.where(j < 24, value, 0.5 * value)

    def put(rows, columns):
        def store(s, j, value):
            r_ref[s * ROWS + j, rows, columns] = value + rhs(s, j, rows, columns)

        return store

    combine_ext(
        coeffs, fields,
        put(slice(0, 8), slice(0, 128)), put(slice(8, 16), slice(0, 128)), side_ref,
    )
    for s in range(2):

        def body(step, carry, s=s):
            for i in range(AT_ONCE):
                j = step * AT_ONCE + i
                at = s * ROWS + j
                r_ref[at, :, 128:256] = side_ref[at] + rhs(s, j, slice(0, 16), slice(128, 256))
            return carry

        lax.fori_loop(0, ROWS // AT_ONCE, body, 0)
    apply_operator(r_ref, m_ref, q_ref, mask)
    finish_first(fields[0], r_ref, q_ref, sums_ref, out_ref)


def finish_first(c_ref, r_ref, q_ref, sums_ref, out_ref):
    sums_ref[...] = jnp.zeros_like(sums_ref)
    r, q = brick(r_ref), brick(q_ref)
    inner_all(c_ref, q, sums_ref)
    inner_pairs([(r, r), (r, q)], sums_ref, 32)
    out_ref[...] = jnp.broadcast_to(row_of_sums(sums_ref), out_ref.shape)


def first_kernel(size_x, size_y, got_ref, *refs):
    fields, refs = refs[:4], refs[4:]
    r_ref, q_ref, m_ref, inv_ref, old_ref = refs[:5]
    u_ref, a_ref, state_ref, out_ref, side_ref, sums_ref = refs[5:]
    row = jnp.sum(got_ref[...], axis=0, keepdims=True)
    _, _, mask = grid_mask(size_x, size_y)
    lane = iota((VECS, 128), 1)
    state = old_ref[...]
    coeffs, q_scale, r_scale = [], [], []
    for s in range(2):
        rr, rq = entry(row, 32 + 2 * s), entry(row, 33 + 2 * s)
        beta = jnp.sqrt(rr + EPS)
        g_zero = solve(inv_ref[...], row, s * VECS) / beta
        h_00 = rq / (beta * beta)
        coeffs.append([spread(-g_zero[k : k + 1]) for k in range(VECS)])
        q_scale.append(spread(1.0 / beta))
        r_scale.append(spread(-h_00 / beta))
        state = jnp.where(lane == s, g_zero, state)
        state = jnp.where(lane == 8 + s, beta, state)
        state = jnp.where(lane == 10 + s, h_00, state)
        state = jnp.where(lane == 12 + s, rr, state)
    state_ref[...] = state

    def put(rows, columns):
        def store(s, j, value):
            at = s * ROWS + j
            value = value + q_scale[s] * q_ref[at, rows, columns]
            u_ref[at, rows, columns] = value + r_scale[s] * r_ref[at, rows, columns]

        return store

    combine_ext(
        coeffs, fields,
        put(slice(0, 8), slice(0, 128)), put(slice(8, 16), slice(0, 128)), side_ref,
    )
    for s in range(2):

        def body(step, carry, s=s):
            for i in range(AT_ONCE):
                at = s * ROWS + step * AT_ONCE + i
                for half in range(2):
                    rows = slice(half * 8, half * 8 + 8)
                    new = side_ref[at, rows] + q_scale[s] * q_ref[at, rows, 128:256]
                    u_ref[at, rows, 128:256] = new + r_scale[s] * r_ref[at, rows, 128:256]
            return carry

        lax.fori_loop(0, ROWS // AT_ONCE, body, 0)
    apply_operator(u_ref, m_ref, a_ref, mask)
    sums_ref[...] = jnp.zeros_like(sums_ref)
    r, u, a = brick(r_ref), brick(u_ref), brick(a_ref)
    inner_all(fields[0], a, sums_ref)
    inner_pairs([(u, u), (r, u), (r, a), (u, a), (a, a)], sums_ref, 32)
    out_ref[...] = jnp.broadcast_to(row_of_sums(sums_ref), out_ref.shape)


def close_cycle(row, inverse, state, s):
    uu, ru, ra, ua, aa = [entry(row, 32 + 5 * s + i) for i in range(5)]
    g_zero = state[:, s : s + 1]
    beta, h_00, rr = [state[0:1, first + s : first + s + 1] for first in (8, 10, 12)]
    h_10 = jnp.sqrt(uu + EPS)
    inner = column_of(row, s * VECS) / h_10
    g_one = solve(inverse, row, s * VECS) / h_10
    h_01 = ra / (beta * h_10)
    h_11 = ua / (h_10 * h_10)
    left = aa / (h_10 * h_10) - jnp.sum(g_one * inner, axis=0, keepdims=True)
    left = left - 2.0 * (h_01 * h_01 + h_11 * h_11)
    left = left + h_01 * h_01 * (rr / (beta * beta)) + h_11 * h_11 * (uu / (h_10 * h_10))
    left = left + 2.0 * h_01 * h_11 * (ru / (beta * h_10))
    h_21_square = jnp.maximum(left, 0.0) + EPS
    n_00 = h_00 * h_00 + h_10 * h_10
    n_01 = h_00 * h_01 + h_10 * h_11
    n_11 = h_01 * h_01 + h_11 * h_11 + h_21_square
    l_00 = jnp.sqrt(n_00)
    l_10 = n_01 / l_00
    l_11 = jnp.sqrt(n_11 - l_10 * l_10)
    z_0 = beta * h_00 / l_00
    z_1 = (beta * h_01 - l_10 * z_0) / l_11
    y_1 = z_1 / l_11
    y_0 = (z_0 - l_10 * y_1) / l_00
    t_0 = beta - h_00 * y_0 - h_01 * y_1
    t_1 = -h_10 * y_0 - h_11 * y_1
    return {
        "r": (t_0 + y_1 * h_01) / beta,
        "u": (t_1 + y_1 * h_11) / h_10,
        "a": -y_1 / h_10,
        "c": y_1 * g_one,
        "sol_r": y_0 / beta,
        "sol_u": y_1 / h_10,
        "basis": state[:, 2 + s : 3 + s] - g_zero * y_0 - g_one * y_1,
    }


def next_kernel(size_x, size_y, got_ref, *refs):
    fields, refs = refs[:4], refs[4:]
    r_ref, u_ref, a_ref, m_ref, inv_ref, old_ref = refs[:6]
    new_ref, q_ref, sol_ref, state_ref, out_ref, side_ref, sums_ref = refs[6:]
    row = jnp.sum(got_ref[...], axis=0, keepdims=True)
    _, _, mask = grid_mask(size_x, size_y)
    state = old_ref[...]
    small = [close_cycle(row, inv_ref[...], state, s) for s in range(2)]
    lane = iota((VECS, 128), 1)
    state_ref[...] = jnp.where(
        lane == 2, small[0]["basis"], jnp.where(lane == 3, small[1]["basis"], 0.0)
    )
    coeffs = [[spread(small[s]["c"][k : k + 1]) for k in range(VECS)] for s in range(2)]
    scale = [{name: spread(small[s][name]) for name in ("r", "u", "a", "sol_r", "sol_u")} for s in range(2)]

    def total(s, at, rows, columns, value):
        value = value + scale[s]["r"] * r_ref[at, rows, columns]
        value = value + scale[s]["u"] * u_ref[at, rows, columns]
        return value + scale[s]["a"] * a_ref[at, rows, columns]

    def put(rows, columns):
        def store(s, j, value):
            at = s * ROWS + j
            new_ref[at, rows, columns] = total(s, at, rows, columns, value)

        return store

    combine_ext(
        coeffs, fields,
        put(slice(0, 8), slice(0, 128)), put(slice(8, 16), slice(0, 128)), side_ref,
    )
    for s in range(2):

        def body(step, carry, s=s):
            for i in range(AT_ONCE):
                at = s * ROWS + step * AT_ONCE + i
                for half in range(2):
                    rows = slice(half * 8, half * 8 + 8)
                    value = side_ref[at, rows]
                    new_ref[at, rows, 128:256] = total(s, at, rows, slice(128, 256), value)
                sol_ref[at] = (
                    scale[s]["sol_r"] * r_ref[at, 0:8, 0:128]
                    + scale[s]["sol_u"] * u_ref[at, 0:8, 0:128]
                )
            return carry

        lax.fori_loop(0, ROWS // AT_ONCE, body, 0)
    apply_operator(new_ref, m_ref, q_ref, mask)
    finish_first(fields[0], new_ref, q_ref, sums_ref, out_ref)


def basis_row(basis, d, kl, j):
    row = kl * ROWS + j
    if d == 0:
        return basis[0][row].astype(F32)
    first = {1: 1, 3: 3, 2: 5}[d]
    return basis[first][row].astype(F32) if kl < 2 else basis[first + 1][row - CUT].astype(F32)


def last_kernel(got_ref, c_ref, *refs):
    basis, refs = refs[:7], refs[7:]
    r_ref, u_ref, a_ref, inv_ref, old_ref, sol_ref = refs[:6]
    solution_ref, residual_ref = refs[6:]
    row = jnp.sum(got_ref[...], axis=0, keepdims=True)
    state = old_ref[...]
    small = [close_cycle(row, inv_ref[...], state, s) for s in range(2)]
    coeffs = [[spread(one["c"][k : k + 1]) for k in range(VECS)] for one in small]
    basis_coeffs = [[spread(one["basis"][k : k + 1]) for k in range(VECS)] for one in small]
    names = ("r", "u", "a", "sol_r", "sol_u")
    scale = [{name: spread(one[name]) for name in names} for one in small]

    def residual_body(step, carry):
        rows = [step * AT_ONCE + i for i in range(AT_ONCE)]
        values = [[], []]
        for s in range(2):
            for j in rows:
                r, u, a = brick(r_ref)(s, j), brick(u_ref)(s, j), brick(a_ref)(s, j)
                values[s].append(scale[s]["r"] * r + scale[s]["u"] * u + scale[s]["a"] * a)
        for k in range(VECS):
            for i, j in enumerate(rows):
                vec = c_ref[k * ROWS + j]
                for s in range(2):
                    values[s][i] = values[s][i] + coeffs[s][k] * vec
        for s in range(2):
            for i, j in enumerate(rows):
                residual_ref[s * ROWS + j] = values[s][i]
        return carry

    def solution_body(step, carry):
        rows = [step * AT_ONCE + i for i in range(AT_ONCE)]
        values = [[], []]
        for s in range(2):
            for j in rows:
                r, u = brick(r_ref)(s, j), brick(u_ref)(s, j)
                old = sol_ref[s * ROWS + j]
                values[s].append(old + scale[s]["sol_r"] * r + scale[s]["sol_u"] * u)
        for d in range(LOCAL):
            for kl in range(LOCAL):
                for i, j in enumerate(rows):
                    vec = basis_row(basis, d, kl, j)
                    for s in range(2):
                        values[s][i] = values[s][i] + basis_coeffs[s][d * LOCAL + kl] * vec
        for s in range(2):
            for i, j in enumerate(rows):
                solution_ref[s * ROWS + j] = values[s][i]
        return carry

    lax.fori_loop(0, ROWS // AT_ONCE, residual_body, 0)
    lax.fori_loop(0, ROWS // AT_ONCE, solution_body, 0)


def call(kernel, outs, args, scratch=(), smem=0):
    vmem = pl.BlockSpec(memory_space=pltpu.VMEM)
    return pl.pallas_call(
        kernel,
        out_shape=outs,
        in_specs=[pl.BlockSpec(memory_space=pltpu.SMEM)] * smem + [vmem] * (len(args) - smem),
        out_specs=jax.tree.map(lambda _: vmem, outs),
        scratch_shapes=list(scratch),
        compiler_params=pltpu.CompilerParams(vmem_limit_bytes=20 * 1024 * 1024),
    )(*args)


def shape(*dims, dtype=F32):
    return jax.ShapeDtypeStruct(dims, dtype)


def exchange(value):
    return lax.all_to_all(value, ("gx", "gy"), 0, 0)


def steps(axis, wrap=False):
    size = lax.axis_size(axis)
    up = [(i, (i + 1) % size) for i in range(size if wrap else size - 1)]
    return up, [(j, i) for i, j in up]


def tied(first, *rest):
    return lax.optimization_barrier((first, *rest))


def on_device(src_cell, basis, images, induction):
    size_x, size_y = 8 * lax.axis_size("gx"), 128 * lax.axis_size("gy")
    peers = lax.axis_size("gx") * lax.axis_size("gy")
    right, left = steps("tx", wrap=True)
    block = jnp.concatenate(
        [images.reshape(LOCAL * ROWS, 8, 128), induction.reshape(6, 8, 128)], axis=0
    )
    own = call(pack_y_kernel, shape(PACKED, 8, 128, dtype=BF16), (block,))
    one = lax.ppermute(block, "tx", right)
    three = lax.ppermute(block, "tx", left)
    up, down = steps("gy")
    after, before = lax.ppermute(own, "gy", down), lax.ppermute(own, "gy", up)
    side = jnp.where(lax.broadcasted_iota(jnp.int32, own.shape, 1) < 4, after, before)
    far_side = lax.ppermute(side, "tx", [(i, (i + 2) % LOCAL) for i in range(LOCAL)])
    far_side, one, three = tied(far_side, one, three)
    far_low = lax.ppermute(jnp.concatenate([one[:CUT], side]), "tx", right)
    far_high = lax.ppermute(jnp.concatenate([three[CUT:], side]), "tx", left)
    up, down = steps("gx")

    def exchange_x(group, sides, sources):
        count = len(group) * HALF + len(sides) * PACKED
        half = shape(count, 8, 128, dtype=BF16)
        low, high = call(functools.partial(pack_x_kernel, group, sides), (half, half), sources)
        return lax.ppermute(low, "gx", down), lax.ppermute(high, "gx", up)

    early = exchange_x(EARLY, EARLY_SIDES, (block, one, three, side, side, side))
    blocks = (block, one, three, far_low, far_high, side, far_side)

    late = exchange_x(LATE, LATE_SIDES, blocks)

    sums = pltpu.VMEM((128, 128), F32)
    side_scratch = pltpu.VMEM((2 * ROWS, 16, 128), F32)
    sent = call(
        functools.partial(gram_kernel, size_x, size_y),
        shape(peers, 3, 128),
        (src_cell, *blocks),
        (pltpu.VMEM((ROWS, 16, 128), F32), pltpu.VMEM((8 * VECS + 48, ROWS * 128), BF16)),
        smem=1,
    )
    got = exchange(sent)
    whole, tiles = shape(VECS * ROWS, 8, 128), shape(3 * VECS, 8, 128)
    m, rhs, *fields = call(
        functools.partial(prepare_kernel, size_x, size_y),
        (shape(24, 16, 256), shape(ROWS, 16, 256), whole, whole, tiles, tiles),
        (src_cell, *blocks, *early, *late),
        smem=1,
    )
    wide = shape(2 * ROWS, 16, 256)
    line = shape(peers, 128)
    small = shape(VECS, 128)
    own_basis = basis.reshape(LOCAL * ROWS, 8, 128)

    def total(value):
        return exchange(value.reshape(peers, 1, 128)).reshape(peers, 128)

    got, piece = tied(got, own_basis[:CUT])
    one_low, three_low = lax.ppermute(piece, "tx", right), lax.ppermute(piece, "tx", left)
    r, q, inverse, state, sent = call(
        functools.partial(begin_kernel, size_x, size_y),
        (wide, wide, small, small, line),
        (got, *fields, m, rhs),
        (side_scratch, sums),
    )

    def first(r, q, state, got):
        return call(
            functools.partial(first_kernel, size_x, size_y),
            (wide, wide, small, line),
            (got, *fields, r, q, m, inverse, state),
            (side_scratch, sums),
        )

    sent, one_low, three_low = tied(sent, one_low, three_low)
    got, piece = tied(total(sent), own_basis[CUT:])
    one_high, three_high = lax.ppermute(piece, "tx", right), lax.ppermute(piece, "tx", left)
    u, a, state, sent = first(r, q, state, got)
    sent, one_high, three_high = tied(sent, one_high, three_high)
    got, one_low, three_high = tied(total(sent), one_low, three_high)
    two_low, two_high = lax.ppermute(one_low, "tx", right), lax.ppermute(three_high, "tx", left)
    r, q, field, state, sent = call(
        functools.partial(next_kernel, size_x, size_y),
        (wide, wide, shape(2 * ROWS, 8, 128), small, line),
        (got, *fields, r, u, a, m, inverse, state),
        (side_scratch, sums),
    )
    sent, two_low, two_high = tied(sent, two_low, two_high)
    u, a, state, sent = first(r, q, state, total(sent))
    bases = (own_basis, one_low, one_high, three_low, three_high, two_low, two_high)
    narrow = shape(2 * ROWS, 8, 128)
    field, residual = call(
        last_kernel,
        (narrow, narrow),
        (total(sent), fields[0], *bases, r, u, a, inverse, state, field),
    )
    full = (2, 2, 3, 8, 8, 128)
    return field.reshape(full), residual.reshape(full)


def solution(mesh):
    in_specs = (
        P("tx"),
        P("tx", None, None, None, "gx", "gy"),
        P("tx", None, None, None, "gx", "gy"),
        P(None, "tx", "gx", "gy"),
    )
    out_specs = (P("tx", None, None, None, "gx", "gy"), P("tx", None, None, None, "gx", "gy"))
    return jax.shard_map(
        on_device, mesh=mesh, in_specs=in_specs, out_specs=out_specs, check_vma=False
    )
```

```python
import functools

import jax
import jax.numpy as jnp
from jax import lax
from jax.experimental import pallas as pl
from jax.experimental.pallas import tpu as pltpu
from jax.sharding import PartitionSpec as P

EPS = 1e-06
VECS = 16
LOCAL = 4
ROWS = 48
BLOCK = 198
HALF = 99
PACKED = 13
WEIGHTS = (1.0, 0.5, 0.25)
AT_ONCE = 12
HIGH = lax.Precision.HIGHEST
F32 = jnp.float32
BF16 = jnp.bfloat16


def iota(shape, axis):
    return lax.broadcasted_iota(jnp.int32, shape, axis)


def pick_matrix(dtype):
    col = iota((8, 128), 0)
    lane = iota((8, 128), 1)
    return jnp.where(lane == jnp.where(col < 4, col, col + 120), 1.0, 0.0).astype(dtype)


def nt_dot(left, right, precision=None):
    return lax.dot_general(
        left, right, (((1,), (1,)), ((), ())), precision=precision, preferred_element_type=F32
    )


def full_dot(left, right):
    return lax.dot_general(
        left, right, (((1,), (0,)), ((), ())), precision=HIGH, preferred_element_type=F32
    )


BLOCKS = 7
CUT = 2 * ROWS


def vector_row(blocks, d, kl, j):
    row = kl * ROWS + j
    if d != 2:
        return blocks[(0, 1, None, 2)[d]][row].astype(F32)
    return blocks[3][row].astype(F32) if kl < 2 else blocks[4][row - CUT].astype(F32)


def induction_row(blocks, d, at):
    if d != 2:
        return blocks[(0, 1, None, 2)[d]][LOCAL * ROWS + at].astype(F32)
    return blocks[4][LOCAL * ROWS - CUT + at].astype(F32)


def side_tile(blocks, d, tile):
    ref, first = ((5, 0), (3, CUT), (6, 0), (4, BLOCK - CUT))[d]
    return blocks[ref][first + tile]


def pack_y_kernel(block_ref, out_ref):
    pick = pick_matrix(BF16)
    for tile in range(PACKED):
        first = tile * 16
        count = min(16, BLOCK - first)
        rows = block_ref[first : first + count].astype(F32).reshape(count * 8, 128).astype(BF16)
        picked = nt_dot(pick, rows)
        if count < 16:
            picked = jnp.concatenate([picked, jnp.zeros((8, 128 - count * 8), F32)], axis=1)
        out_ref[tile] = picked.astype(BF16)


EARLY, LATE = (0, 1, 3), (2,)
EARLY_SIDES, LATE_SIDES = (0,), (1, 2, 3)


def halo_row(halos, d, row):
    ref = 2 if d == 2 else 0
    at = (0 if d == 2 else EARLY.index(d)) * HALF + row
    return halos[ref][at].astype(F32), halos[ref + 1][at].astype(F32)


def halo_side(halos, d, tile):
    ref = 0 if d == 0 else 2
    at = (len(EARLY) * HALF if d == 0 else HALF + LATE_SIDES.index(d) * PACKED) + tile
    after, before = halos[ref][at].astype(F32), halos[ref + 1][at].astype(F32)
    return jnp.where(iota((8, 128), 1) % 8 < 4, after, before)


def pack_x_kernel(group, sides, *refs):
    blocks, (lo_ref, hi_ref) = refs[:-2], refs[-2:]
    top = iota((8, 128), 0) < 4

    def pair(one, two, at):
        two = pltpu.roll(two, 4, 0)
        lo_ref[at] = jnp.where(top, one, two).astype(BF16)
        hi_ref[at] = jnp.where(top, two, one).astype(BF16)

    def body(j, carry):
        for place, d in enumerate(group):
            for kl in range(2):
                pair(
                    vector_row(blocks, d, kl, j),
                    vector_row(blocks, d, kl + 2, j),
                    place * HALF + kl * ROWS + j,
                )
        return carry

    lax.fori_loop(0, ROWS, body, 0)
    for place, d in enumerate(group):
        for i in range(3):
            pair(
                induction_row(blocks, d, i),
                induction_row(blocks, d, i + 3),
                place * HALF + CUT + i,
            )
    for place, d in enumerate(sides):
        for tile in range(PACKED):
            piece = side_tile(blocks, d, tile)
            lo_ref[len(group) * HALF + place * PACKED + tile] = piece
            hi_ref[len(group) * HALF + place * PACKED + tile] = piece


def inner_all(c_ref, field, sums_ref):
    def body(step, accs):
        accs = list(accs)
        for j in [AT_ONCE * step + i for i in range(AT_ONCE)]:
            one, two = field(0, j), field(1, j)
            for k in range(VECS):
                vec = c_ref[k * ROWS + j]
                accs[2 * k] = accs[2 * k] + vec * one
                accs[2 * k + 1] = accs[2 * k + 1] + vec * two
        return tuple(accs)

    zero = jnp.zeros((8, 128), F32)
    accs = lax.fori_loop(0, ROWS // AT_ONCE, body, (zero,) * (2 * VECS))
    for k in range(VECS):
        for s in range(2):
            sums_ref[s * VECS + k : s * VECS + k + 1] = jnp.sum(
                accs[2 * k + s], axis=0, keepdims=True
            )


def inner_pairs(pairs, sums_ref, first):
    count = len(pairs)

    def body(step, accs):
        new = []
        for s in range(2):
            for i, (one, two) in enumerate(pairs):
                acc = accs[s * count + i]
                for row in range(AT_ONCE):
                    j = step * AT_ONCE + row
                    acc = acc + one(s, j) * two(s, j)
                new.append(acc)
        return tuple(new)

    accs = lax.fori_loop(0, ROWS // AT_ONCE, body, (jnp.zeros((8, 128), F32),) * (2 * count))
    for i, acc in enumerate(accs):
        sums_ref[first + i : first + i + 1] = jnp.sum(acc, axis=0, keepdims=True)


def row_of_sums(sums_ref):
    return nt_dot(jnp.ones((8, 128), F32), sums_ref[...], HIGH)[0:1]


def entry(row, lane):
    return row[:, lane : lane + 1]


def column_of(row, first):
    part = row[:, first : first + VECS]
    eye = iota((VECS, VECS), 0) == iota((VECS, VECS), 1)
    return jnp.sum(jnp.where(eye, part, 0.0), axis=1, keepdims=True)


def solve(inverse, row, first):
    return jnp.sum(inverse[:, :VECS] * row[:, first : first + VECS], axis=1, keepdims=True)


def spread(value):
    return jnp.broadcast_to(value, (8, 128))


def grid_mask(size_x, size_y):
    row, lane = iota((16, 256), 0), iota((16, 256), 1)
    x_pos = lax.axis_index("gx") * 8 + jnp.where(row < 12, row, row - 16)
    y_pos = lax.axis_index("gy") * 128 + jnp.where(lane < 132, lane, lane - 256)
    inside = (x_pos >= 0) & (x_pos < size_x) & (y_pos >= 0) & (y_pos < size_y)
    inside = inside & ((lane < 132) | (lane >= 252))
    return x_pos, y_pos, inside


def primary_field(cell, z, x_pos, y_pos, size_x, size_y):
    plane = size_x * size_y
    src_z = cell // plane
    rest = cell % plane
    d_z = (z - src_z).astype(F32)
    d_x = (x_pos - rest // size_y).astype(F32)
    d_y = (y_pos - rest % size_y).astype(F32)
    dist = jnp.sqrt(d_z * d_z + d_x * d_x + d_y * d_y)
    return jnp.exp(-dist / ((size_x + size_y) / 8.0))


def unpack_once(blocks, halos, c_ref, x_ref, near_ref, far_ref):
    top = iota((8, 128), 0) < 4

    def body(j, carry):
        for d in range(LOCAL):
            for kl in range(LOCAL):
                k = d * LOCAL + kl
                c_ref[k * ROWS + j] = vector_row(blocks, d, kl, j)
                after, before = halo_row(halos, d, (kl % 2) * ROWS + j)
                if kl < 2:
                    x_ref[k * ROWS + j] = jnp.where(top, after, before)
                else:
                    x_ref[k * ROWS + j] = pltpu.roll(jnp.where(top, before, after), 4, 0)
        return carry

    lax.fori_loop(0, ROWS, body, 0, unroll=2)
    for d in range(LOCAL):
        for t in range(PACKED - 1):
            near_ref[d * 12 + t] = side_tile(blocks, d, t).astype(F32)
            far_ref[d * 12 + t] = halo_side(halos, d, t)


def plus(total, term):
    return term if total is None else total + term


def combine_ext(coeffs, fields, interior, halo_x, unpacked_ref):
    c_ref, x_ref, near_ref, far_ref = fields

    def body(step, carry):
        rows = [step * AT_ONCE + i for i in range(AT_ONCE)]
        inner = [[None] * AT_ONCE, [None] * AT_ONCE]
        outer = [[None] * AT_ONCE, [None] * AT_ONCE]
        for k in range(VECS):
            for i, j in enumerate(rows):
                vec, edge = c_ref[k * ROWS + j], x_ref[k * ROWS + j]
                for s in range(2):
                    inner[s][i] = plus(inner[s][i], coeffs[s][k] * vec)
                    outer[s][i] = plus(outer[s][i], coeffs[s][k] * edge)
        for i, j in enumerate(rows):
            for s in range(2):
                interior(s, j, inner[s][i])
                halo_x(s, j, outer[s][i])
        return carry

    lax.fori_loop(0, ROWS // AT_ONCE, body, 0)
    pick = pick_matrix(F32)
    for s in range(2):
        for tile in range(3):
            near = jnp.zeros((8, 128), F32)
            far = jnp.zeros((8, 128), F32)
            for k in range(VECS):
                near = near + coeffs[s][k] * near_ref[k * 3 + tile]
                far = far + coeffs[s][k] * far_ref[k * 3 + tile]
            place = s * ROWS + tile * 16
            near = full_dot(jnp.transpose(near), pick).reshape(16, 8, 128)
            far = full_dot(jnp.transpose(far), pick).reshape(16, 8, 128)
            unpacked_ref[place : place + 16, 0:8] = near
            unpacked_ref[place : place + 16, 8:16] = far


def apply_operator(e_ref, m_ref, out_ref, mask):
    def ahead(f, axis):
        return pltpu.roll(f, f.shape[axis] - 1, axis)

    def behind(f, axis):
        return pltpu.roll(f, 1, axis)

    def body(index, carry):
        base = index * 24
        other = jnp.where(index % 2 == 0, base + 24, base - 24)
        sign = jnp.where(index % 2 == 0, -1.0, 1.0).astype(F32)
        zero = jnp.zeros((16, 256), F32)
        b_x_old = -e_ref[base + 8]
        b_y_old = e_ref[base]
        for z in range(8):
            e_x, e_y, e_z = e_ref[base + z], e_ref[base + 8 + z], e_ref[base + 16 + z]
            up_x = e_ref[base + z + 1] if z < 7 else zero
            up_y = e_ref[base + 8 + z + 1] if z < 7 else zero
            b_x = (ahead(e_z, 1) - e_z) - (up_y - e_y)
            b_y = (up_x - e_x) - (ahead(e_z, 0) - e_z)
            b_z = (ahead(e_y, 0) - e_y) - (ahead(e_x, 1) - e_x)
            c_x = (b_z - behind(b_z, 1)) - (b_y - b_y_old)
            c_y = (b_x - b_x_old) - (b_z - behind(b_z, 0))
            c_z = (b_y - behind(b_y, 0)) - (b_x - behind(b_x, 1))
            for c, value in enumerate((c_x, c_y, c_z)):
                at = c * 8 + z
                value = value + sign * (m_ref[at] * e_ref[other + at])
                out_ref[base + at] = jnp.where(mask, value, 0.0)
            b_x_old, b_y_old = b_x, b_y
        return carry

    lax.fori_loop(0, 4, body, 0)


def brick(ref):
    return lambda s, j: ref[s * ROWS + j, 0:8, 0:128]


def pick_layer(values, z):
    want = lax.rem(lax.axis_index("tx") - z // 2 + LOCAL, LOCAL)
    result = values[0]
    for d in range(1, LOCAL):
        result = jnp.where(want == d, values[d], result)
    return result


def gram_kernel(size_x, size_y, src_ref, *refs):
    blocks, out_ref, field_ref, rows_ref = refs[:BLOCKS], *refs[BLOCKS:]
    x_pos = lax.axis_index("gx") * 8 + iota((8, 128), 0)
    y_pos = lax.axis_index("gy") * 128 + iota((8, 128), 1)
    for z in range(8):
        prim = [
            primary_field(src_ref[s], z, x_pos, y_pos, size_x, size_y) for s in range(2)
        ]
        for c in range(3):
            m = pick_layer([induction_row(blocks, d, 2 * c + z % 2) for d in range(LOCAL)], z)
            for s in range(2):
                real = (m - 1.0) * WEIGHTS[c] * prim[s]
                field_ref[c * 8 + z, s * 8 : s * 8 + 8] = real
                field_ref[24 + c * 8 + z, s * 8 : s * 8 + 8] = 0.5 * real

    def body(j, carry):
        columns = pl.ds(pl.multiple_of(j * 128, 128), 128)
        for pair in range(VECS // 2):
            d, kl = pair // 2, 2 * (pair % 2)
            both = [vector_row(blocks, d, kl + i, j) for i in range(2)]
            rows_ref[16 * pair : 16 * pair + 16, columns] = jnp.concatenate(both).astype(BF16)
        rest = field_ref[j]
        for piece in range(3):
            part = rest.astype(BF16)
            rest = rest - part.astype(F32)
            first = 8 * VECS + 16 * piece
            rows_ref[first : first + 16, columns] = part
        return carry

    lax.fori_loop(0, ROWS, body, 0)
    full = nt_dot(rows_ref[0:128], rows_ref[...])
    row, lane = iota((128, 128), 0), iota((128, 128), 1)
    gram = jnp.where(row % 8 == lane % 8, full[:, 0:128], 0.0).reshape(VECS, 8, 128)
    gram = jnp.sum(gram, axis=1)
    gram = full_dot(gram, jnp.where(row // 8 == lane % 16, 1.0, 0.0).astype(F32))
    gram = jnp.where(iota((VECS, 128), 1) // 16 == iota((VECS, 128), 0) % 8, gram, 0.0)
    gram = jnp.sum(gram.reshape(2, 8, 128), axis=1)
    inner = full[:, 128:144] + full[:, 144:160] + full[:, 160:176]
    inner = jnp.where(iota((128, 16), 0) % 8 == iota((128, 16), 1) % 8, inner, 0.0)
    inner = jnp.sum(inner.reshape(VECS, 8, 16), axis=1)
    lines = []
    for s in range(2):
        chosen = jnp.where(iota((8, 16), 1) // 8 == s, 1.0, 0.0).astype(F32)
        lines.append(nt_dot(chosen, inner, HIGH)[0:1])
    line = jnp.concatenate(lines + [jnp.zeros((1, 96), F32)], axis=1)
    rows = jnp.concatenate([gram, line], axis=0)
    out_ref[...] = jnp.broadcast_to(rows[None], out_ref.shape)


def invert(rows):
    lane, row = iota((VECS, 128), 1), iota((VECS, 128), 0)
    wide = jnp.where(row < 8, rows[0:1], rows[1:2])
    wide = jnp.where(lane // 16 == row % 8, wide, 0.0)
    fold = jnp.where(iota((128, 128), 0) % 16 == iota((128, 128), 1), 1.0, 0.0).astype(F32)
    work = full_dot(wide, fold) + jnp.where(lane == row + VECS, 1.0, 0.0)
    for j in range(VECS):
        pivot = work[j : j + 1] / work[j : j + 1, j : j + 1]
        work = jnp.where(row == j, pivot, work - work[:, j : j + 1] * pivot)
    return pltpu.roll(work, 128 - VECS, 1)


def prepare_kernel(size_x, size_y, src_ref, *refs):
    blocks, halos, refs = refs[:BLOCKS], refs[BLOCKS : BLOCKS + 4], refs[BLOCKS + 4 :]
    m_ref, rhs_ref, fields = refs[0], refs[1], refs[2:]
    unpack_once(blocks, halos, *fields)
    x_pos, y_pos, mask = grid_mask(size_x, size_y)
    top = iota((8, 128), 0) < 4
    pick = pick_matrix(F32)
    sides = []
    for d in range(LOCAL):
        near, far = side_tile(blocks, d, 12).astype(F32), halo_side(halos, d, 12)
        near = full_dot(jnp.transpose(near), pick)[:48].reshape(6, 8, 128)
        far = full_dot(jnp.transpose(far), pick)[:48].reshape(6, 8, 128)
        sides.append((near, far))
    for c in range(3):
        for z in range(8):
            at = 2 * c + z % 2
            quarters = []
            for d in range(LOCAL):
                inner_m = induction_row(blocks, d, at)
                after, before = halo_row(halos, d, CUT + at % 3)
                if at < 3:
                    edge = jnp.where(top, after, before)
                else:
                    edge = pltpu.roll(jnp.where(top, before, after), 4, 0)
                left = jnp.concatenate([inner_m, edge], axis=0)
                right = jnp.concatenate([sides[d][0][at], sides[d][1][at]], axis=0)
                quarters.append(jnp.concatenate([left, right], axis=1))
            m_ref[c * 8 + z] = pick_layer(quarters, z)
    for s in range(2):

        def body(z, carry, s=s):
            prim = primary_field(src_ref[s], z, x_pos, y_pos, size_x, size_y)
            for c in range(3):
                at = c * 8 + z
                real = (m_ref[at] - 1.0) * WEIGHTS[c] * prim
                rhs_ref[s * 24 + at] = jnp.where(mask, real, 0.0)
            return carry

        lax.fori_loop(0, 8, body, 0)


def begin_kernel(size_x, size_y, got_ref, *refs):
    fields, m_ref, rhs_ref = refs[:4], refs[4], refs[5]
    r_ref, q_ref, inv_ref, state_ref, out_ref, side_ref, sums_ref = refs[6:]
    total = jnp.sum(got_ref[...], axis=0)
    inverse = invert(total[0:2])
    inv_ref[...] = inverse
    inner = total[2:3]
    _, _, mask = grid_mask(size_x, size_y)
    start = [solve(inverse, inner, s * VECS) for s in range(2)]
    lane = iota((VECS, 128), 1)
    state_ref[...] = jnp.where(lane == 2, start[0], jnp.where(lane == 3, start[1], 0.0))
    coeffs = [[spread(-start[s][k : k + 1]) for k in range(VECS)] for s in range(2)]

    def rhs(s, j, rows, columns):
        value = rhs_ref[s * 24 + lax.rem(j, 24), rows, columns]
        return jnp.where(j < 24, value, 0.5 * value)

    def put(rows, columns):
        def store(s, j, value):
            r_ref[s * ROWS + j, rows, columns] = value + rhs(s, j, rows, columns)

        return store

    combine_ext(
        coeffs, fields,
        put(slice(0, 8), slice(0, 128)), put(slice(8, 16), slice(0, 128)), side_ref,
    )
    for s in range(2):

        def body(step, carry, s=s):
            for i in range(AT_ONCE):
                j = step * AT_ONCE + i
                at = s * ROWS + j
                r_ref[at, :, 128:256] = side_ref[at] + rhs(s, j, slice(0, 16), slice(128, 256))
            return carry

        lax.fori_loop(0, ROWS // AT_ONCE, body, 0)
    apply_operator(r_ref, m_ref, q_ref, mask)
    finish_first(fields[0], r_ref, q_ref, sums_ref, out_ref)


def finish_first(c_ref, r_ref, q_ref, sums_ref, out_ref):
    sums_ref[...] = jnp.zeros_like(sums_ref)
    r, q = brick(r_ref), brick(q_ref)
    inner_all(c_ref, q, sums_ref)
    inner_pairs([(r, r), (r, q)], sums_ref, 32)
    out_ref[...] = jnp.broadcast_to(row_of_sums(sums_ref), out_ref.shape)


def first_kernel(size_x, size_y, got_ref, *refs):
    fields, refs = refs[:4], refs[4:]
    r_ref, q_ref, m_ref, inv_ref, old_ref = refs[:5]
    u_ref, a_ref, state_ref, out_ref, side_ref, sums_ref = refs[5:]
    row = jnp.sum(got_ref[...], axis=0, keepdims=True)
    _, _, mask = grid_mask(size_x, size_y)
    lane = iota((VECS, 128), 1)
    state = old_ref[...]
    coeffs, q_scale, r_scale = [], [], []
    for s in range(2):
        rr, rq = entry(row, 32 + 2 * s), entry(row, 33 + 2 * s)
        beta = jnp.sqrt(rr + EPS)
        g_zero = solve(inv_ref[...], row, s * VECS) / beta
        h_00 = rq / (beta * beta)
        coeffs.append([spread(-g_zero[k : k + 1]) for k in range(VECS)])
        q_scale.append(spread(1.0 / beta))
        r_scale.append(spread(-h_00 / beta))
        state = jnp.where(lane == s, g_zero, state)
        state = jnp.where(lane == 8 + s, beta, state)
        state = jnp.where(lane == 10 + s, h_00, state)
        state = jnp.where(lane == 12 + s, rr, state)
    state_ref[...] = state

    def put(rows, columns):
        def store(s, j, value):
            at = s * ROWS + j
            value = value + q_scale[s] * q_ref[at, rows, columns]
            u_ref[at, rows, columns] = value + r_scale[s] * r_ref[at, rows, columns]

        return store

    combine_ext(
        coeffs, fields,
        put(slice(0, 8), slice(0, 128)), put(slice(8, 16), slice(0, 128)), side_ref,
    )
    for s in range(2):

        def body(step, carry, s=s):
            for i in range(AT_ONCE):
                at = s * ROWS + step * AT_ONCE + i
                for half in range(2):
                    rows = slice(half * 8, half * 8 + 8)
                    new = side_ref[at, rows] + q_scale[s] * q_ref[at, rows, 128:256]
                    u_ref[at, rows, 128:256] = new + r_scale[s] * r_ref[at, rows, 128:256]
            return carry

        lax.fori_loop(0, ROWS // AT_ONCE, body, 0)
    apply_operator(u_ref, m_ref, a_ref, mask)
    sums_ref[...] = jnp.zeros_like(sums_ref)
    r, u, a = brick(r_ref), brick(u_ref), brick(a_ref)
    inner_all(fields[0], a, sums_ref)
    inner_pairs([(u, u), (r, u), (r, a), (u, a), (a, a)], sums_ref, 32)
    out_ref[...] = jnp.broadcast_to(row_of_sums(sums_ref), out_ref.shape)


def close_cycle(row, inverse, state, s):
    uu, ru, ra, ua, aa = [entry(row, 32 + 5 * s + i) for i in range(5)]
    g_zero = state[:, s : s + 1]
    beta, h_00, rr = [state[0:1, first + s : first + s + 1] for first in (8, 10, 12)]
    h_10 = jnp.sqrt(uu + EPS)
    inner = column_of(row, s * VECS) / h_10
    g_one = solve(inverse, row, s * VECS) / h_10
    h_01 = ra / (beta * h_10)
    h_11 = ua / (h_10 * h_10)
    left = aa / (h_10 * h_10) - jnp.sum(g_one * inner, axis=0, keepdims=True)
    left = left - 2.0 * (h_01 * h_01 + h_11 * h_11)
    left = left + h_01 * h_01 * (rr / (beta * beta)) + h_11 * h_11 * (uu / (h_10 * h_10))
    left = left + 2.0 * h_01 * h_11 * (ru / (beta * h_10))
    h_21_square = jnp.maximum(left, 0.0) + EPS
    n_00 = h_00 * h_00 + h_10 * h_10
    n_01 = h_00 * h_01 + h_10 * h_11
    n_11 = h_01 * h_01 + h_11 * h_11 + h_21_square
    l_00 = jnp.sqrt(n_00)
    l_10 = n_01 / l_00
    l_11 = jnp.sqrt(n_11 - l_10 * l_10)
    z_0 = beta * h_00 / l_00
    z_1 = (beta * h_01 - l_10 * z_0) / l_11
    y_1 = z_1 / l_11
    y_0 = (z_0 - l_10 * y_1) / l_00
    t_0 = beta - h_00 * y_0 - h_01 * y_1
    t_1 = -h_10 * y_0 - h_11 * y_1
    return {
        "r": (t_0 + y_1 * h_01) / beta,
        "u": (t_1 + y_1 * h_11) / h_10,
        "a": -y_1 / h_10,
        "c": y_1 * g_one,
        "sol_r": y_0 / beta,
        "sol_u": y_1 / h_10,
        "basis": state[:, 2 + s : 3 + s] - g_zero * y_0 - g_one * y_1,
    }


def next_kernel(size_x, size_y, got_ref, *refs):
    fields, refs = refs[:4], refs[4:]
    r_ref, u_ref, a_ref, m_ref, inv_ref, old_ref = refs[:6]
    new_ref, q_ref, sol_ref, state_ref, out_ref, side_ref, sums_ref = refs[6:]
    row = jnp.sum(got_ref[...], axis=0, keepdims=True)
    _, _, mask = grid_mask(size_x, size_y)
    state = old_ref[...]
    small = [close_cycle(row, inv_ref[...], state, s) for s in range(2)]
    lane = iota((VECS, 128), 1)
    state_ref[...] = jnp.where(
        lane == 2, small[0]["basis"], jnp.where(lane == 3, small[1]["basis"], 0.0)
    )
    coeffs = [[spread(small[s]["c"][k : k + 1]) for k in range(VECS)] for s in range(2)]
    scale = [{name: spread(small[s][name]) for name in ("r", "u", "a", "sol_r", "sol_u")} for s in range(2)]

    def total(s, at, rows, columns, value):
        value = value + scale[s]["r"] * r_ref[at, rows, columns]
        value = value + scale[s]["u"] * u_ref[at, rows, columns]
        return value + scale[s]["a"] * a_ref[at, rows, columns]

    def put(rows, columns):
        def store(s, j, value):
            at = s * ROWS + j
            new_ref[at, rows, columns] = total(s, at, rows, columns, value)

        return store

    combine_ext(
        coeffs, fields,
        put(slice(0, 8), slice(0, 128)), put(slice(8, 16), slice(0, 128)), side_ref,
    )
    for s in range(2):

        def body(step, carry, s=s):
            for i in range(AT_ONCE):
                at = s * ROWS + step * AT_ONCE + i
                for half in range(2):
                    rows = slice(half * 8, half * 8 + 8)
                    value = side_ref[at, rows]
                    new_ref[at, rows, 128:256] = total(s, at, rows, slice(128, 256), value)
                sol_ref[at] = (
                    scale[s]["sol_r"] * r_ref[at, 0:8, 0:128]
                    + scale[s]["sol_u"] * u_ref[at, 0:8, 0:128]
                )
            return carry

        lax.fori_loop(0, ROWS // AT_ONCE, body, 0)
    apply_operator(new_ref, m_ref, q_ref, mask)
    finish_first(fields[0], new_ref, q_ref, sums_ref, out_ref)


def basis_row(basis, d, kl, j):
    row = kl * ROWS + j
    if d == 0:
        return basis[0][row].astype(F32)
    first = {1: 1, 3: 3, 2: 5}[d]
    return basis[first][row].astype(F32) if kl < 2 else basis[first + 1][row - CUT].astype(F32)


def last_kernel(got_ref, c_ref, *refs):
    basis, refs = refs[:7], refs[7:]
    r_ref, u_ref, a_ref, inv_ref, old_ref, sol_ref = refs[:6]
    solution_ref, residual_ref = refs[6:]
    row = jnp.sum(got_ref[...], axis=0, keepdims=True)
    state = old_ref[...]
    small = [close_cycle(row, inv_ref[...], state, s) for s in range(2)]
    coeffs = [[spread(one["c"][k : k + 1]) for k in range(VECS)] for one in small]
    basis_coeffs = [[spread(one["basis"][k : k + 1]) for k in range(VECS)] for one in small]
    names = ("r", "u", "a", "sol_r", "sol_u")
    scale = [{name: spread(one[name]) for name in names} for one in small]

    def residual_body(step, carry):
        rows = [step * AT_ONCE + i for i in range(AT_ONCE)]
        values = [[], []]
        for s in range(2):
            for j in rows:
                r, u, a = brick(r_ref)(s, j), brick(u_ref)(s, j), brick(a_ref)(s, j)
                values[s].append(scale[s]["r"] * r + scale[s]["u"] * u + scale[s]["a"] * a)
        for k in range(VECS):
            for i, j in enumerate(rows):
                vec = c_ref[k * ROWS + j]
                for s in range(2):
                    values[s][i] = values[s][i] + coeffs[s][k] * vec
        for s in range(2):
            for i, j in enumerate(rows):
                residual_ref[s * ROWS + j] = values[s][i]
        return carry

    def solution_body(step, carry):
        rows = [step * AT_ONCE + i for i in range(AT_ONCE)]
        values = [[], []]
        for s in range(2):
            for j in rows:
                r, u = brick(r_ref)(s, j), brick(u_ref)(s, j)
                old = sol_ref[s * ROWS + j]
                values[s].append(old + scale[s]["sol_r"] * r + scale[s]["sol_u"] * u)
        for d in range(LOCAL):
            for kl in range(LOCAL):
                for i, j in enumerate(rows):
                    vec = basis_row(basis, d, kl, j)
                    for s in range(2):
                        values[s][i] = values[s][i] + basis_coeffs[s][d * LOCAL + kl] * vec
        for s in range(2):
            for i, j in enumerate(rows):
                solution_ref[s * ROWS + j] = values[s][i]
        return carry

    lax.fori_loop(0, ROWS // AT_ONCE, residual_body, 0)
    lax.fori_loop(0, ROWS // AT_ONCE, solution_body, 0)


def call(kernel, outs, args, scratch=(), smem=0):
    vmem = pl.BlockSpec(memory_space=pltpu.VMEM)
    return pl.pallas_call(
        kernel,
        out_shape=outs,
        in_specs=[pl.BlockSpec(memory_space=pltpu.SMEM)] * smem + [vmem] * (len(args) - smem),
        out_specs=jax.tree.map(lambda _: vmem, outs),
        scratch_shapes=list(scratch),
        compiler_params=pltpu.CompilerParams(vmem_limit_bytes=20 * 1024 * 1024),
    )(*args)


def shape(*dims, dtype=F32):
    return jax.ShapeDtypeStruct(dims, dtype)


def exchange(value):
    return lax.all_to_all(value, ("gx", "gy"), 0, 0)


def steps(axis, wrap=False):
    size = lax.axis_size(axis)
    up = [(i, (i + 1) % size) for i in range(size if wrap else size - 1)]
    return up, [(j, i) for i, j in up]


def tied(first, *rest):
    return lax.optimization_barrier((first, *rest))


def on_device(src_cell, basis, images, induction):
    size_x, size_y = 8 * lax.axis_size("gx"), 128 * lax.axis_size("gy")
    peers = lax.axis_size("gx") * lax.axis_size("gy")
    right, left = steps("tx", wrap=True)
    block = jnp.concatenate(
        [images.reshape(LOCAL * ROWS, 8, 128), induction.reshape(6, 8, 128)], axis=0
    )
    own = call(pack_y_kernel, shape(PACKED, 8, 128, dtype=BF16), (block,))
    one = lax.ppermute(block, "tx", right)
    three = lax.ppermute(block, "tx", left)
    up, down = steps("gy")
    after, before = lax.ppermute(own, "gy", down), lax.ppermute(own, "gy", up)
    side = jnp.where(lax.broadcasted_iota(jnp.int32, own.shape, 1) < 4, after, before)
    far_side = lax.ppermute(side, "tx", [(i, (i + 2) % LOCAL) for i in range(LOCAL)])
    far_side, one, three = tied(far_side, one, three)
    far_low = lax.ppermute(jnp.concatenate([one[:CUT], side]), "tx", right)
    far_high = lax.ppermute(jnp.concatenate([three[CUT:], side]), "tx", left)
    up, down = steps("gx")

    def exchange_x(group, sides, sources):
        count = len(group) * HALF + len(sides) * PACKED
        half = shape(count, 8, 128, dtype=BF16)
        low, high = call(functools.partial(pack_x_kernel, group, sides), (half, half), sources)
        return lax.ppermute(low, "gx", down), lax.ppermute(high, "gx", up)

    early = exchange_x(EARLY, EARLY_SIDES, (block, one, three, side, side, side))
    blocks = (block, one, three, far_low, far_high, side, far_side)

    late = exchange_x(LATE, LATE_SIDES, blocks)

    sums = pltpu.VMEM((128, 128), F32)
    side_scratch = pltpu.VMEM((2 * ROWS, 16, 128), F32)
    sent = call(
        functools.partial(gram_kernel, size_x, size_y),
        shape(peers, 3, 128),
        (src_cell, *blocks),
        (pltpu.VMEM((ROWS, 16, 128), F32), pltpu.VMEM((8 * VECS + 48, ROWS * 128), BF16)),
        smem=1,
    )
    got = exchange(sent)
    whole, tiles = shape(VECS * ROWS, 8, 128), shape(3 * VECS, 8, 128)
    m, rhs, *fields = call(
        functools.partial(prepare_kernel, size_x, size_y),
        (shape(24, 16, 256), shape(ROWS, 16, 256), whole, whole, tiles, tiles),
        (src_cell, *blocks, *early, *late),
        smem=1,
    )
    wide = shape(2 * ROWS, 16, 256)
    line = shape(peers, 128)
    small = shape(VECS, 128)
    own_basis = basis.reshape(LOCAL * ROWS, 8, 128)

    def total(value):
        return exchange(value.reshape(peers, 1, 128)).reshape(peers, 128)

    got, piece = tied(got, own_basis[:CUT])
    one_low, three_low = lax.ppermute(piece, "tx", right), lax.ppermute(piece, "tx", left)
    r, q, inverse, state, sent = call(
        functools.partial(begin_kernel, size_x, size_y),
        (wide, wide, small, small, line),
        (got, *fields, m, rhs),
        (side_scratch, sums),
    )

    def first(r, q, state, got):
        return call(
            functools.partial(first_kernel, size_x, size_y),
            (wide, wide, small, line),
            (got, *fields, r, q, m, inverse, state),
            (side_scratch, sums),
        )

    sent, one_low, three_low = tied(sent, one_low, three_low)
    got, piece = tied(total(sent), own_basis[CUT:])
    one_high, three_high = lax.ppermute(piece, "tx", right), lax.ppermute(piece, "tx", left)
    u, a, state, sent = first(r, q, state, got)
    sent, one_high, three_high = tied(sent, one_high, three_high)
    got, one_low, three_high = tied(total(sent), one_low, three_high)
    two_low, two_high = lax.ppermute(one_low, "tx", right), lax.ppermute(three_high, "tx", left)
    r, q, field, state, sent = call(
        functools.partial(next_kernel, size_x, size_y),
        (wide, wide, shape(2 * ROWS, 8, 128), small, line),
        (got, *fields, r, u, a, m, inverse, state),
        (side_scratch, sums),
    )
    sent, two_low, two_high = tied(sent, two_low, two_high)
    u, a, state, sent = first(r, q, state, total(sent))
    bases = (own_basis, one_low, one_high, three_low, three_high, two_low, two_high)
    narrow = shape(2 * ROWS, 8, 128)
    field, residual = call(
        last_kernel,
        (narrow, narrow),
        (total(sent), fields[0], *bases, r, u, a, inverse, state, field),
    )
    full = (2, 2, 3, 8, 8, 128)
    return field.reshape(full), residual.reshape(full)


def solution(mesh):
    in_specs = (
        P("tx"),
        P("tx", None, None, None, "gx", "gy"),
        P("tx", None, None, None, "gx", "gy"),
        P(None, "tx", "gx", "gy"),
    )
    out_specs = (P("tx", None, None, None, "gx", "gy"), P("tx", None, None, None, "gx", "gy"))
    return jax.shard_map(
        on_device, mesh=mesh, in_specs=in_specs, out_specs=out_specs, check_vma=False
    )
```
